32 devices in a mesh: member: 4 (over y, core), space: 8 (over z, x).
Axes of the slice: x: 2, y: 2, z: 4, core: 2. Of those that a mesh axis runs over, the one named last changes fastest.
Arguments:
- prior_sample: float32 [256, 65536], P('member', 'space'), may hold values from -6 to 6
- measured_point_location: int32 [32, 128], P('space'), may hold values from 0 to 8191
- measured_data: float32 [32, 128], P('space'), may hold values from -12 to 12
- measurement_noise_sigma: float32 [32, 128], P('space'), may hold values from 2 to 64
- measured_slots_used: int32 [8], P('space'), may hold values from 128 to 512, as said below
Outputs:
- analysis: float32 [256, 65536], P('member', 'space')
The draws below stay inside these ranges and needn't reach their ends.
Inputs may be any that keep to these rules, and one draw needn't show every extreme that they name: measured_slots_used gives for each space block how many of its first slots are in use; some block uses all 512 slots. `measured_point_location`: each index is a state point of the observation's own space block.
All inputs are finite; a program needn't handle non-finite values.
Results may differ from the reference program's by a relative error of at most 0.000088.
Values sent between devices are 32-bit elements; how exact they have to be, the bound alone decides.
A program may use at most 64 MiB of HBM per device.

```python
import math
import jax
import jax.numpy as jnp
from jax import lax

SAMPLE_TOTAL = 256
ROW = 128
POINTS_IN_REGION = 8192
REGION_TOTAL = 8
GRID_POINTS = 65536
OBS_BLK = 512
OBS_ROWS = 32


def draw_measured_slots_used(key, part):
    counts = jax.random.randint(key, (REGION_TOTAL,), OBS_BLK // 4, OBS_BLK + 1)
    chosen = jax.random.randint(jax.random.fold_in(key, 7), (), 0, REGION_TOTAL)
    full_block = jnp.arange(REGION_TOTAL) == chosen
    return jnp.where(full_block, OBS_BLK, counts).astype(jnp.int32)


def touch_ends(array, own_key, low, top_value):
    shape = array.shape
    index_at = [jax.random.randint(jax.random.fold_in(own_key, axis), (), 0, shape[axis]) for axis in range(len(shape))]
    array = array.at[tuple(index_at)].set(low)
    longest = shape.index(max(shape))
    index_at[longest] = (index_at[longest] + 1) % shape[longest]
    return array.at[tuple(index_at)].set(top_value)


def block_levels(key, shape, split, least, high):
    def one(position, blocks):
        draws = jax.random.uniform(jax.random.fold_in(jax.random.fold_in(key, 6), position), (blocks,), jnp.float32, least / len(split), high / len(split))
        return jnp.repeat(jnp.exp(draws), shape[position] // blocks).reshape((-1,) + (1,) * (len(shape) - position - 1))

    factor_of = one(*split[0])
    for cut in split[1:]:
        factor_of = factor_of * one(*cut)
    return factor_of


def bell_draw(rng, shape, width, limit, shards=(), kind=jnp.bfloat16):
    entries = jax.random.normal(rng, shape, jnp.float32) * width
    if len(shards) > 0:
        entries = block_levels(rng, shape, shards, -0.22, 0.18) * entries
    return jnp.clip(entries, min=-limit, max=limit).astype(kind)


def setup_inputs(seed: int = 0) -> dict:
    key_list = jax.random.split(jax.random.key(seed), 6)
    prior_sample = bell_draw(key_list[0], (SAMPLE_TOTAL, GRID_POINTS), 1.0, 6.0, ((0, 4), (1, 8)), jnp.float32)
    measured_point_location = touch_ends(jax.random.randint(key_list[1], (OBS_ROWS, ROW), 0, POINTS_IN_REGION), jax.random.fold_in(key_list[1], 1), 0, POINTS_IN_REGION - 1).astype(jnp.int32)
    measured_data = bell_draw(key_list[2], (OBS_ROWS, ROW), 3.0, 12.0, ((0, 8),), jnp.float32)
    measurement_noise_sigma = jnp.clip(jnp.exp(math.log(64.0) - 3.465736 * jax.random.uniform(key_list[3], (OBS_ROWS, ROW), jnp.float32) ** block_levels(key_list[3], (OBS_ROWS, ROW), ((0, 8),), -0.2, 0.2)), 2.0, 64.0)
    measured_slots_used = draw_measured_slots_used(jax.random.fold_in(key_list[5], 71), 0)
    return {"prior_sample": prior_sample, "measured_point_location": measured_point_location, "measured_data": measured_data, "measurement_noise_sigma": measurement_noise_sigma, "measured_slots_used": measured_slots_used}


def lower_inverse(lower_factor):
    size_k = lower_factor.shape[0]
    ident = jnp.eye(size_k, dtype=lower_factor.dtype)
    return lax.linalg.triangular_solve(lower_factor, ident, left_side=True, lower=True)

def reference(prior_sample, measured_point_location, measured_data, measurement_noise_sigma, measured_slots_used):
    exact_arithmetic = lax.Precision.HIGHEST
    sample_total = prior_sample.shape[0]
    region_total = prior_sample.reshape(sample_total, REGION_TOTAL, POINTS_IN_REGION)
    index_blocks = measured_point_location.reshape(REGION_TOTAL, OBS_BLK)
    propagated_grid = jax.vmap(lambda block, places: jnp.take(block, places, axis=1), in_axes=(1, 0), out_axes=1)(region_total, index_blocks)
    propagated_grid = propagated_grid.reshape(sample_total, REGION_TOTAL * OBS_BLK)
    slots = jnp.arange(OBS_BLK, dtype=jnp.int32)
    valid = (slots[None, :] < measured_slots_used[:, None]).reshape(-1)
    weight = jnp.where(valid, 1.0 / measurement_noise_sigma.reshape(-1), jnp.zeros_like(measurement_noise_sigma.reshape(-1)))
    sim_mean = lax.optimization_barrier(jnp.mean(propagated_grid, axis=0))
    perturbed = (propagated_grid - sim_mean[None, :]) * weight[None, :]
    innovation = (measured_data.reshape(-1) - sim_mean) * weight
    gram_all = jnp.dot(perturbed, perturbed.T, precision=exact_arithmetic)
    cross = jnp.dot(perturbed, innovation, precision=exact_arithmetic)
    cov_matrix = gram_all + (sample_total - 1) * jnp.eye(sample_total, dtype=gram_all.dtype)
    lower_factor = jnp.linalg.cholesky(cov_matrix)
    inverse = lower_inverse(lower_factor)
    projected = jnp.dot(inverse, cross, precision=exact_arithmetic)
    mean_weight = jnp.dot(inverse.T, projected, precision=exact_arithmetic)
    weight_matrix_update = math.sqrt(sample_total - 1) * inverse + mean_weight[None, :]
    prior_average = lax.optimization_barrier(jnp.mean(prior_sample, axis=0))
    return prior_average[None, :] + jnp.dot(weight_matrix_update, prior_sample - prior_average[None, :], precision=exact_arithmetic)
```

```python
import functools
import math

import jax
import jax.numpy as jnp
from jax import lax
from jax.experimental import pallas as pl
from jax.experimental.pallas import tpu as pltpu
from jax.sharding import PartitionSpec as P


def solve_lower(lower_factor, target):
    return lax.linalg.triangular_solve(lower_factor, target, left_side=True, lower=True)


def general_body(
    prior_sample,
    measured_point_location,
    measured_data,
    measurement_noise_sigma,
    measured_slots_used,
):
    exact_arithmetic = lax.Precision.HIGHEST
    anomaly_matrix, points_in_region = prior_sample.shape
    region_batches = lax.axis_size("member")
    sample_total = anomaly_matrix * region_batches
    pointwise_spread = points_in_region // region_batches
    linear_position = measured_point_location.reshape(-1)
    obs_blk = linear_position.shape[0]
    observation_deviation = obs_blk // region_batches
    propagated_grid = jnp.take(prior_sample, linear_position, axis=1).reshape(
        anomaly_matrix, region_batches, observation_deviation
    )
    prior_regions = prior_sample.reshape(anomaly_matrix, region_batches, pointwise_spread)
    prior_sample_full, integrate_dynamics = (
        lax.all_to_all(prior_regions, "member", split_axis=1, concat_axis=0, tiled=True),
        lax.all_to_all(propagated_grid, "member", split_axis=1, concat_axis=0, tiled=True),
    )
    integrate_dynamics = integrate_dynamics.reshape(sample_total, observation_deviation)
    rank = lax.axis_index("member")
    start = rank * observation_deviation
    my_value = lax.dynamic_slice_in_dim(measured_data.reshape(-1), start, observation_deviation)
    my_sigma = lax.dynamic_slice_in_dim(
        measurement_noise_sigma.reshape(-1), start, observation_deviation
    )
    slots = start + jnp.arange(observation_deviation, dtype=jnp.int32)
    valid = slots < measured_slots_used[0]
    weight = jnp.where(valid, 1.0 / my_sigma, jnp.zeros_like(my_sigma))
    sim_mean = jnp.mean(integrate_dynamics, axis=0)
    perturbed = (integrate_dynamics - sim_mean[None, :]) * weight[None, :]
    innovation = (my_value - sim_mean) * weight
    gram_loc = jnp.dot(perturbed, perturbed.T, precision=exact_arithmetic)
    cross_loc = jnp.dot(perturbed, innovation, precision=exact_arithmetic)
    gram_block, cross_block = lax.psum((gram_loc, cross_loc), "member")
    gram_all, cross = lax.psum((gram_block, cross_block), "space")
    cov_matrix = gram_all + (sample_total - 1) * jnp.eye(sample_total, dtype=jnp.float32)
    lower_factor = jnp.linalg.cholesky(cov_matrix)
    inverse = solve_lower(lower_factor, jnp.eye(sample_total, dtype=jnp.float32))
    projected = jnp.dot(inverse, cross, precision=exact_arithmetic)
    mean_weight = jnp.dot(inverse.T, projected, precision=exact_arithmetic)
    weight_matrix_update = math.sqrt(sample_total - 1) * inverse + mean_weight[None, :]
    sample_vectors = prior_sample_full.reshape(sample_total, -1)
    prior_average = jnp.mean(sample_vectors, axis=0)
    updated_sample = prior_average[None, :] + jnp.dot(
        weight_matrix_update, sample_vectors - prior_average[None, :], precision=exact_arithmetic
    )
    returned = lax.all_to_all(
        updated_sample.reshape(prior_sample_full.shape),
        "member",
        split_axis=0,
        concat_axis=1,
        tiled=True,
    )
    return returned.reshape(anomaly_matrix, points_in_region)


MESH = pl.DeviceIdType.MESH
VMEM_SPEC = pl.BlockSpec(memory_space=pltpu.VMEM)
LANES = 128
MIB = 1 << 20
SUBLANES = 8


def split2(x):
    high = x.astype(jnp.bfloat16)
    low = (x - high.astype(jnp.float32)).astype(jnp.bfloat16)
    return high, low


def dot3(a, b, dims=((1,), (0,))):
    ah, al = split2(a)
    bh, bl = split2(b)
    d = functools.partial(
        lax.dot_general, dimension_numbers=(dims, ((), ())), preferred_element_type=jnp.float32
    )
    return (d(ah, bl) + d(al, bh)) + d(ah, bh)


def flat_row(ref):
    return jnp.concatenate([ref[i : i + 1, :] for i in range(ref.shape[0])], axis=1)


def gather_kernel(starts, x_ref, idx_ref, out_ref, *chunk_refs):
    step = pl.program_id(0)
    members, points = x_ref.shape
    shape = (SUBLANES, LANES)
    for (first, count), chunk_ref in zip(starts, chunk_refs):

        @pl.when((step >= first) & (step < first + count))
        def _(chunk_ref=chunk_ref):
            chunk_ref[...] = x_ref[...]

    for c in range(idx_ref.shape[0]):
        index = jnp.broadcast_to(idx_ref[c : c + 1, :], shape)
        lane = jnp.bitwise_and(index, LANES - 1)
        block = jnp.right_shift(index, LANES.bit_length() - 1) - step * (points // LANES)
        hits = [block == j for j in range(points // LANES)]
        columns = slice(c * LANES, (c + 1) * LANES)
        for g in range(0, members, SUBLANES):
            old = out_ref[g : g + SUBLANES, columns]
            got = jnp.where(step == 0, jnp.zeros(shape, jnp.float32), old)
            for j in range(points // LANES):
                x = x_ref[g : g + SUBLANES, j * LANES : (j + 1) * LANES]
                got = jnp.where(hits[j], jnp.take_along_axis(x, lane, axis=1), got)
            out_ref[g : g + SUBLANES, columns] = got


def gather_observed(prior, index, starts, tile):
    members, points = prior.shape
    slots = index.size
    f32 = jnp.float32
    return pl.pallas_call(
        functools.partial(gather_kernel, starts),
        grid=(points // tile,),
        out_shape=[jax.ShapeDtypeStruct((members, slots), f32)]
        + [jax.ShapeDtypeStruct((members, count * tile), f32) for _, count in starts],
        in_specs=[
            pl.BlockSpec((members, tile), lambda i: (0, i)),
            pl.BlockSpec(index.shape, lambda i: (0, 0)),
        ],
        out_specs=[pl.BlockSpec((members, slots), lambda i: (0, 0))]
        + [
            pl.BlockSpec(
                (members, tile),
                lambda i, first=first, count=count: (0, jnp.clip(i - first, 0, count - 1)),
            )
            for first, count in starts
        ],
        compiler_params=pltpu.CompilerParams(vmem_limit_bytes=12 * MIB),
        cost_estimate=pl.CostEstimate(
            flops=2 * members * slots * 256, bytes_accessed=16_000_000, transcendentals=0
        ),
    )(prior, index)


def send(src, dst, ssem, rsem, member, space):
    copy = pltpu.make_async_remote_copy(
        src_ref=src,
        dst_ref=dst,
        send_sem=ssem,
        recv_sem=rsem,
        device_id={"member": member, "space": space},
        device_id_type=MESH,
    )
    copy.start()
    return copy


def meet(devices):
    barrier = pltpu.get_barrier_semaphore()
    for member, space in devices:
        pl.semaphore_signal(
            barrier, inc=1, device_id={"member": member, "space": space}, device_id_type=MESH
        )
    pl.semaphore_wait(barrier, len(devices))


def neighbours():
    rank = lax.axis_index("member")
    return rank, rank + 1 - 2 * lax.rem(rank, 2), lax.rem(rank + 2, 4)


def exchange_kernel(ev_ref, out_ref, pair, ssem, rsem):
    rank, _, across = neighbours()
    place = lax.axis_index("space")
    rows = ev_ref.shape[0]
    meet([(across, place)])
    mine = pl.ds(pl.multiple_of((rank // 2) * rows, SUBLANES), rows)
    copy = send(ev_ref, pair.at[mine], ssem, rsem, across, place)
    pair[mine, :] = ev_ref[...]
    copy.wait()
    out_ref[...] = pair[...]


def exchange_observed(ev):
    rows, slots = ev.shape
    dma = pltpu.SemaphoreType.DMA
    pair = (rows * 2, slots)
    return pl.pallas_call(
        exchange_kernel,
        out_shape=jax.ShapeDtypeStruct(pair, jnp.float32),
        in_specs=[VMEM_SPEC],
        out_specs=VMEM_SPEC,
        scratch_shapes=[pltpu.VMEM(pair, jnp.float32), dma(()), dma(())],
        compiler_params=pltpu.CompilerParams(
            collective_id=0, has_side_effects=True, vmem_limit_bytes=4 * MIB
        ),
        cost_estimate=pl.CostEstimate(
            flops=1_000_000, bytes_accessed=20_000_000, transcendentals=0
        ),
    )(ev)


def gram_kernel(
    spaces,
    ev_ref,
    data_ref,
    sigma_ref,
    used_ref,
    out_ref,
    full,
    gram,
    parts,
    total,
    inv_ref,
    rs_send,
    rs_recv,
    ag_send,
    ag_recv,
    fin_send,
    fin_recv,
    ex_send,
    ex_recv,
):
    rank, side, _ = neighbours()
    place = lax.axis_index("space")
    half = lax.rem(rank, 2)
    samples, slots = full.shape
    rows = samples // 2
    group = samples // 4
    chunk = rows // spaces
    meet([(side, place)] + [(rank, lax.rem(place + d, spaces)) for d in range(1, spaces)])

    shared = []
    for i in range(2):
        source = ev_ref.at[pl.ds(i * group, group)]
        target = full.at[pl.ds(pl.multiple_of((half + 2 * i) * group, SUBLANES), group)]
        shared.append(send(source, target, ex_send.at[i], ex_recv.at[i], side, place))
    for i in range(2):
        own = pl.ds(pl.multiple_of((half + 2 * i) * group, SUBLANES), group)
        full[own, :] = ev_ref[i * group : (i + 1) * group, :]
    slot = lax.broadcasted_iota(jnp.int32, (1, slots), 1)
    weight = jnp.where(slot < used_ref[0], 1.0 / flat_row(sigma_ref), 0.0)
    for copy in shared:
        copy.wait_recv()
    ev = full[...]
    mean = jnp.sum(ev, axis=0, keepdims=True) * (1.0 / samples)
    anomalies = (ev - mean) * weight
    innovation = (flat_row(data_ref) - mean) * weight
    first = lax.broadcasted_iota(jnp.int32, (LANES, slots), 0) == 0
    extra = jnp.where(first, jnp.broadcast_to(innovation, (LANES, slots)), 0.0)
    mine = (full[pl.ds(pl.multiple_of(half * rows, SUBLANES), rows), :] - mean) * weight
    right = jnp.concatenate([anomalies, extra], axis=0)
    gram[...] = dot3(mine, right, ((1,), (1,)))

    copies = []
    for d in range(1, spaces):
        other = lax.rem(place + d, spaces)
        copies.append(
            send(
                gram.at[pl.ds(pl.multiple_of(other * chunk, SUBLANES), chunk)],
                parts.at[d - 1],
                rs_send.at[d - 1],
                rs_recv.at[d - 1],
                rank,
                other,
            )
        )
    acc = gram[pl.ds(pl.multiple_of(place * chunk, SUBLANES), chunk), :]
    for d in range(1, spaces):
        copies[d - 1].wait_recv()
        acc = acc + parts[d - 1]
    piece = pl.ds(pl.multiple_of(half * rows + place * chunk, SUBLANES), chunk)
    total[piece, :] = acc
    spread = []
    for d in range(1, spaces):
        other = lax.rem(place + d, spaces)
        spread.append(
            send(
                total.at[piece], total.at[piece], ag_send.at[d - 1], ag_recv.at[d - 1], rank, other
            )
        )
    for copy in spread:
        copy.wait_recv()
    mine_rows = total.at[pl.ds(pl.multiple_of(half * rows, SUBLANES), rows)]
    last = send(mine_rows, mine_rows, fin_send, fin_recv, side, place)
    last.wait_recv()
    for copy in (*shared, *copies, *spread, last):
        copy.wait_send()
    transform_kernel(total, out_ref, inv_ref)


def summed_gram(ev, data, sigma, used, spaces):
    rows, slots = ev.shape
    samples = rows * 2
    width = samples + LANES
    dma = pltpu.SemaphoreType.DMA
    return pl.pallas_call(
        functools.partial(gram_kernel, spaces),
        out_shape=jax.ShapeDtypeStruct((samples, samples), jnp.float32),
        in_specs=[VMEM_SPEC] * 3 + [pl.BlockSpec(memory_space=pltpu.SMEM)],
        out_specs=VMEM_SPEC,
        scratch_shapes=[
            pltpu.VMEM((samples, slots), jnp.float32),
            pltpu.VMEM((rows, width), jnp.float32),
            pltpu.VMEM((spaces - 1, rows // spaces, width), jnp.float32),
            pltpu.VMEM((samples, width), jnp.float32),
            pltpu.VMEM((samples, samples), jnp.float32),
            dma((spaces - 1,)),
            dma((spaces - 1,)),
            dma((spaces - 1,)),
            dma((spaces - 1,)),
            dma(()),
            dma(()),
            dma((2,)),
            dma((2,)),
        ],
        compiler_params=pltpu.CompilerParams(collective_id=1, has_side_effects=True, vmem_limit_bytes=16 * MIB),
        cost_estimate=pl.CostEstimate(
            flops=4_000_000, bytes_accessed=6_000_000, transcendentals=0
        ),
    )(ev, data, sigma, used)


PIVOTS = 4


def inverse_factor(a):
    size = a.shape[0]
    count = size // SUBLANES
    shape = (SUBLANES, size)
    m = [a[SUBLANES * i : SUBLANES * (i + 1), :] for i in range(count)]
    diag = [None] * count
    lane = lax.broadcasted_iota(jnp.int32, shape, 1)
    sub = lax.broadcasted_iota(jnp.int32, shape, 0)

    def column(x, k):
        return jnp.broadcast_to(x[:, k : k + 1], shape)

    def row(x, r):
        return jnp.broadcast_to(x[r : r + 1, :], shape)

    for k in range(0, size, PIVOTS):
        t, r = divmod(k, SUBLANES)
        inside = (lane >= k) & (lane < k + PIVOTS)
        cols = [column(m[t], k + q) for q in range(PIVOTS)]
        pivot = {(q, p): row(cols[p], r + q) for p in range(PIVOTS) for q in range(p, PIVOTS)}
        base = [
            jnp.where(inside, jnp.where(lane == k + q, 1.0, 0.0), row(m[t], r + q))
            for q in range(PIVOTS)
        ]
        inverse = []
        for p in range(PIVOTS):
            inverse.append(1.0 / pivot[p, p])
            for q in range(p + 1, PIVOTS):
                factor = pivot[q, p] * inverse[p]
                base[q] = base[q] - factor * base[p]
                for s in range(q, PIVOTS):
                    pivot[s, q] = pivot[s, q] - factor * pivot[s, p]
        for p in range(PIVOTS):
            old = diag[t]
            diag[t] = pivot[p, p] if old is None else jnp.where(sub >= r + p, pivot[p, p], old)
        for i in range(t, count):
            cols_i = cols if i == t else [column(m[i], k + q) for q in range(PIVOTS)]
            cols_i = list(cols_i)
            if i == t:
                unit = jnp.where(lane - k == sub - r, 1.0, 0.0)
                x = jnp.where(inside & (sub >= r), unit, m[i])
            else:
                x = jnp.where(inside, 0.0, m[i])
            for p in range(PIVOTS):
                mult = cols_i[p] * inverse[p]
                if i == t:
                    mult = jnp.where(sub > r + p, mult, 0.0)
                for q in range(p + 1, PIVOTS):
                    cols_i[q] = cols_i[q] - mult * pivot[q, p]
                x = x - mult * base[p]
            m[i] = x
    out = []
    for i in range(count):
        keep = lane <= sub + SUBLANES * i
        out.append(jnp.where(keep, m[i] * lax.rsqrt(diag[i]), 0.0))
    return jnp.concatenate(out, axis=0)


def eye_mask(rows, cols):
    shape = (rows, cols)
    return lax.broadcasted_iota(jnp.int32, shape, 0) == lax.broadcasted_iota(jnp.int32, shape, 1)


def transform_kernel(g_ref, out_ref, inv_ref):
    samples = g_ref.shape[0]
    b = LANES
    ridge = float(samples - 1)
    n = samples // b
    work = {}
    for i in range(n):
        for j in range(i + 1):
            block = g_ref[i * b : (i + 1) * b, j * b : (j + 1) * b]
            work[i, j] = block + jnp.where(eye_mask(b, b), ridge, 0.0) if i == j else block
    inv = {}
    low = {}
    for k in range(n):
        inv[k, k] = inverse_factor(work[k, k])
        for i in range(k + 1, n):
            low[i, k] = dot3(work[i, k], inv[k, k], ((1,), (1,)))
        for i in range(k + 1, n):
            for j in range(k + 1, i + 1):
                work[i, j] = work[i, j] - dot3(low[i, k], low[j, k], ((1,), (1,)))
        for j in range(k):
            acc = dot3(low[k, j], inv[j, j])
            for s in range(j + 1, k):
                acc = acc + dot3(low[k, s], inv[s, j])
            inv[k, j] = -dot3(inv[k, k], acc)
    zero = jnp.zeros((b, b), jnp.float32)
    full = jnp.concatenate(
        [
            jnp.concatenate([inv[i, j] if j <= i else zero for j in range(n)], axis=1)
            for i in range(n)
        ],
        axis=0,
    )
    inv_ref[...] = full
    cross = g_ref[:, samples : samples + b]
    projected = dot3(full, cross)
    mean_weight = jnp.sum(full * projected[:, 0:1], axis=0, keepdims=True)
    out_ref[...] = math.sqrt(samples - 1) * full + mean_weight


def analysis_kernel(t_ref, own_ref, side_ref, across_ref, both_ref, out_ref, x_ref):
    rank = lax.axis_index("member")
    rows = own_ref.shape[0]
    samples = x_ref.shape[0]
    side = rank + 1 - 2 * lax.rem(rank, 2)
    across = lax.rem(rank + 2, 4)
    both = lax.rem(side + 2, 4)
    pieces = ((rank, own_ref), (side, side_ref), (across, across_ref), (both, both_ref))
    total = None
    for member, ref in pieces:
        part = jnp.sum(ref[...], axis=0, keepdims=True)
        total = part if total is None else total + part
    mean = total * (1.0 / samples)
    for member, ref in pieces:
        x_ref[pl.ds(pl.multiple_of(member * rows, SUBLANES), rows), :] = ref[...] - mean
    mine = t_ref[pl.ds(pl.multiple_of(rank * rows, SUBLANES), rows), :]
    th, tl = split2(mine)
    xh, xl = split2(x_ref[...])
    dot = functools.partial(jnp.dot, preferred_element_type=jnp.float32)
    both_parts = dot(jnp.concatenate([th, tl], axis=0), xh)
    out_ref[...] = mean + ((both_parts[rows:] + dot(th, xl)) + both_parts[:rows])


def analysis_chunk(transform, own, pieces, first, out, tile=1024):
    rows, points = own.shape
    samples = transform.shape[0]
    whole = pl.BlockSpec((samples, samples), lambda i: (0, 0))
    placed = pl.BlockSpec((rows, tile), lambda i: (0, i + first))
    block = pl.BlockSpec((rows, tile), lambda i: (0, i))
    kernel, extra, specs, alias = analysis_kernel, (), [], {}
    if out is not None:
        kernel = lambda t, o, s, a, b, _, *rest: analysis_kernel(t, o, s, a, b, *rest)
        extra, specs, alias = (out,), [pl.BlockSpec(memory_space=pl.ANY)], {5: 0}
    return pl.pallas_call(
        kernel,
        grid=(pieces[1].shape[1] // tile,),
        out_shape=jax.ShapeDtypeStruct((rows, points), jnp.float32),
        in_specs=[whole, placed, placed] + [block] * 2 + specs,
        out_specs=placed,
        scratch_shapes=[pltpu.VMEM((samples, tile), jnp.float32)],
        input_output_aliases=alias,
        compiler_params=pltpu.CompilerParams(vmem_limit_bytes=12 * MIB),
    )(transform, own, *pieces, *extra)


TILE = 1024
EIGHTHS = (1, 3, 3, 1)


def body(*arrays):
    prior_sample = arrays[0]
    rows, points = prior_sample.shape
    members, spaces = lax.axis_size("member"), lax.axis_size("space")
    if (
        members != 4
        or rows * members % (2 * SUBLANES * spaces)
        or rows * members % LANES
        or rows % SUBLANES
        or points % (8 * TILE)
    ):
        return general_body(*arrays)
    return fast_body(members, spaces, *arrays)


def fast_body(members, spaces, prior_sample, location, data, sigma, used):
    points = prior_sample.shape[1]
    near = [(i, i ^ 1) for i in range(members)]
    far = [(i, i ^ 2) for i in range(members)]
    counts = [e * points // (8 * TILE) for e in EIGHTHS]
    starts = [(sum(counts[:i]), n) for i, n in enumerate(counts)]
    across = [lax.ppermute(prior_sample[:, : counts[0] * TILE], "member", far)]
    side = lax.ppermute(prior_sample, "member", near)
    observed, *chunks = gather_observed(prior_sample, location, starts[1:], TILE)
    gathered = exchange_observed(observed)
    *chunks, gathered = lax.optimization_barrier((*chunks, gathered))
    for chunk in chunks:
        across.append(lax.ppermute(chunk, "member", far))
    gram = summed_gram(gathered, data, sigma, used, spaces)
    across[0], gram = lax.optimization_barrier((across[0], gram))
    both = lax.ppermute(across[0], "member", near)
    out = transform = gram
    result = None
    for i, (first, _) in enumerate(starts):
        now = both
        if i + 1 < len(starts):
            across[i + 1], out = lax.optimization_barrier((across[i + 1], out))
            if i == 0:
                transform = out
            else:
                result = out
            both = lax.ppermute(across[i + 1], "member", near)
        result = analysis_chunk(
            transform, prior_sample, (side, across[i], now), first, result
        )
        out = result
    return result


def solution(mesh):
    placed = (
        P("member", "space"),
        P("space", None),
        P("space", None),
        P("space", None),
        P("space"),
    )
    return jax.shard_map(
        body, mesh=mesh, in_specs=placed, out_specs=P("member", "space"), check_vma=False
    )
```

```python
import functools
import math

import jax
import jax.numpy as jnp
from jax import lax
from jax.experimental import pallas as pl
from jax.experimental.pallas import tpu as pltpu
from jax.sharding import PartitionSpec as P


def solve_lower(lower_factor, target):
    return lax.linalg.triangular_solve(lower_factor, target, left_side=True, lower=True)


def general_body(
    prior_sample,
    measured_point_location,
    measured_data,
    measurement_noise_sigma,
    measured_slots_used,
):
    exact_arithmetic = lax.Precision.HIGHEST
    anomaly_matrix, points_in_region = prior_sample.shape
    region_batches = lax.axis_size("member")
    sample_total = anomaly_matrix * region_batches
    pointwise_spread = points_in_region // region_batches
    linear_position = measured_point_location.reshape(-1)
    obs_blk = linear_position.shape[0]
    observation_deviation = obs_blk // region_batches
    propagated_grid = jnp.take(prior_sample, linear_position, axis=1).reshape(
        anomaly_matrix, region_batches, observation_deviation
    )
    prior_regions = prior_sample.reshape(anomaly_matrix, region_batches, pointwise_spread)
    prior_sample_full, integrate_dynamics = (
        lax.all_to_all(prior_regions, "member", split_axis=1, concat_axis=0, tiled=True),
        lax.all_to_all(propagated_grid, "member", split_axis=1, concat_axis=0, tiled=True),
    )
    integrate_dynamics = integrate_dynamics.reshape(sample_total, observation_deviation)
    rank = lax.axis_index("member")
    start = rank * observation_deviation
    my_value = lax.dynamic_slice_in_dim(measured_data.reshape(-1), start, observation_deviation)
    my_sigma = lax.dynamic_slice_in_dim(
        measurement_noise_sigma.reshape(-1), start, observation_deviation
    )
    slots = start + jnp.arange(observation_deviation, dtype=jnp.int32)
    valid = slots < measured_slots_used[0]
    weight = jnp.where(valid, 1.0 / my_sigma, jnp.zeros_like(my_sigma))
    sim_mean = jnp.mean(integrate_dynamics, axis=0)
    perturbed = (integrate_dynamics - sim_mean[None, :]) * weight[None, :]
    innovation = (my_value - sim_mean) * weight
    gram_loc = jnp.dot(perturbed, perturbed.T, precision=exact_arithmetic)
    cross_loc = jnp.dot(perturbed, innovation, precision=exact_arithmetic)
    gram_block, cross_block = lax.psum((gram_loc, cross_loc), "member")
    gram_all, cross = lax.psum((gram_block, cross_block), "space")
    cov_matrix = gram_all + (sample_total - 1) * jnp.eye(sample_total, dtype=jnp.float32)
    lower_factor = jnp.linalg.cholesky(cov_matrix)
    inverse = solve_lower(lower_factor, jnp.eye(sample_total, dtype=jnp.float32))
    projected = jnp.dot(inverse, cross, precision=exact_arithmetic)
    mean_weight = jnp.dot(inverse.T, projected, precision=exact_arithmetic)
    weight_matrix_update = math.sqrt(sample_total - 1) * inverse + mean_weight[None, :]
    sample_vectors = prior_sample_full.reshape(sample_total, -1)
    prior_average = jnp.mean(sample_vectors, axis=0)
    updated_sample = prior_average[None, :] + jnp.dot(
        weight_matrix_update, sample_vectors - prior_average[None, :], precision=exact_arithmetic
    )
    returned = lax.all_to_all(
        updated_sample.reshape(prior_sample_full.shape),
        "member",
        split_axis=0,
        concat_axis=1,
        tiled=True,
    )
    return returned.reshape(anomaly_matrix, points_in_region)


MESH = pl.DeviceIdType.MESH
VMEM_SPEC = pl.BlockSpec(memory_space=pltpu.VMEM)
LANES = 128
MIB = 1 << 20
SUBLANES = 8


def split2(x):
    high = x.astype(jnp.bfloat16)
    low = (x - high.astype(jnp.float32)).astype(jnp.bfloat16)
    return high, low


def dot3(a, b, dims=((1,), (0,))):
    ah, al = split2(a)
    bh, bl = split2(b)
    d = functools.partial(
        lax.dot_general, dimension_numbers=(dims, ((), ())), preferred_element_type=jnp.float32
    )
    return (d(ah, bl) + d(al, bh)) + d(ah, bh)


def flat_row(ref):
    return jnp.concatenate([ref[i : i + 1, :] for i in range(ref.shape[0])], axis=1)


PIVOTS = 4


def inverse_factor(a):
    size = a.shape[0]
    count = size // SUBLANES
    shape = (SUBLANES, size)
    m = [a[SUBLANES * i : SUBLANES * (i + 1), :] for i in range(count)]
    diag = [None] * count
    lane = lax.broadcasted_iota(jnp.int32, shape, 1)
    sub = lax.broadcasted_iota(jnp.int32, shape, 0)

    def column(x, k):
        return jnp.broadcast_to(x[:, k : k + 1], shape)

    def row(x, r):
        return jnp.broadcast_to(x[r : r + 1, :], shape)

    for k in range(0, size, PIVOTS):
        t, r = divmod(k, SUBLANES)
        inside = (lane >= k) & (lane < k + PIVOTS)
        cols = [column(m[t], k + q) for q in range(PIVOTS)]
        pivot = {(q, p): row(cols[p], r + q) for p in range(PIVOTS) for q in range(p, PIVOTS)}
        base = [
            jnp.where(inside, jnp.where(lane == k + q, 1.0, 0.0), row(m[t], r + q))
            for q in range(PIVOTS)
        ]
        inverse = []
        for p in range(PIVOTS):
            inverse.append(1.0 / pivot[p, p])
            for q in range(p + 1, PIVOTS):
                factor = pivot[q, p] * inverse[p]
                base[q] = base[q] - factor * base[p]
                for s in range(q, PIVOTS):
                    pivot[s, q] = pivot[s, q] - factor * pivot[s, p]
        for p in range(PIVOTS):
            old = diag[t]
            diag[t] = pivot[p, p] if old is None else jnp.where(sub >= r + p, pivot[p, p], old)
        for i in range(t, count):
            cols_i = cols if i == t else [column(m[i], k + q) for q in range(PIVOTS)]
            cols_i = list(cols_i)
            if i == t:
                unit = jnp.where(lane - k == sub - r, 1.0, 0.0)
                x = jnp.where(inside & (sub >= r), unit, m[i])
            else:
                x = jnp.where(inside, 0.0, m[i])
            for p in range(PIVOTS):
                mult = cols_i[p] * inverse[p]
                if i == t:
                    mult = jnp.where(sub > r + p, mult, 0.0)
                for q in range(p + 1, PIVOTS):
                    cols_i[q] = cols_i[q] - mult * pivot[q, p]
                x = x - mult * base[p]
            m[i] = x
    out = []
    for i in range(count):
        keep = lane <= sub + SUBLANES * i
        out.append(jnp.where(keep, m[i] * lax.rsqrt(diag[i]), 0.0))
    return jnp.concatenate(out, axis=0)


def eye_mask(rows, cols):
    shape = (rows, cols)
    return lax.broadcasted_iota(jnp.int32, shape, 0) == lax.broadcasted_iota(jnp.int32, shape, 1)


TILE = 512
CHUNKS = (512,) * 15 + (256,) * 2
EARLY = 6
READY = 13
GATHER = 1024


def offsets(widths):
    return [(sum(widths[:i]), w) for i, w in enumerate(widths)]


def gather_rows(x_ref, first, idx_ref, out_ref, rows, points, arrived):
    shape = (SUBLANES, LANES)
    blocks = GATHER // LANES

    def step(t, _):
        arrived(t)
        for c in range(idx_ref.shape[0]):
            index = jnp.broadcast_to(idx_ref[c : c + 1, :], shape)
            lane = jnp.bitwise_and(index, LANES - 1)
            block = jnp.right_shift(index, LANES.bit_length() - 1) - t * blocks
            hits = [block == j for j in range(blocks)]
            columns = slice(c * LANES, (c + 1) * LANES)
            for g in range(0, rows, SUBLANES):
                place = pl.ds(pl.multiple_of(first + g, SUBLANES), SUBLANES)
                got = out_ref[place, columns]
                for j in range(blocks):
                    at = pl.ds(pl.multiple_of(t * GATHER + j * LANES, LANES), LANES)
                    x = x_ref[place, at]
                    got = jnp.where(hits[j], jnp.take_along_axis(x, lane, axis=1), got)
                out_ref[place, columns] = got
        return 0

    lax.fori_loop(0, points // GATHER, step, 0)


def transform_of(low_blocks, cross, t_ref, inv_ref, w_ref):
    samples = t_ref.shape[0]
    b = LANES
    ridge = float(samples - 1)
    n = samples // b
    work = {}
    for (i, j), block in low_blocks.items():
        work[i, j] = block + jnp.where(eye_mask(b, b), ridge, 0.0) if i == j else block
    inv = {}
    low = {}
    for k in range(n):
        inv[k, k] = inverse_factor(work[k, k])
        for i in range(k + 1, n):
            low[i, k] = dot3(work[i, k], inv[k, k], ((1,), (1,)))
        for i in range(k + 1, n):
            for j in range(k + 1, i + 1):
                work[i, j] = work[i, j] - dot3(low[i, k], low[j, k], ((1,), (1,)))
        for j in range(k):
            acc = dot3(low[k, j], inv[j, j])
            for m in range(j + 1, k):
                acc = acc + dot3(low[k, m], inv[m, j])
            inv[k, j] = -dot3(inv[k, k], acc)
    zero = jnp.zeros((b, b), jnp.float32)
    full = jnp.concatenate(
        [
            jnp.concatenate([inv[i, j] if j <= i else zero for j in range(n)], axis=1)
            for i in range(n)
        ],
        axis=0,
    )
    inv_ref[...] = full
    projected = jnp.sum(full * cross, axis=1, keepdims=True)
    mean_weight = jnp.sum(full * projected, axis=0, keepdims=True)
    w_ref[...] = jnp.broadcast_to(mean_weight, w_ref.shape)
    t_ref[...] = math.sqrt(samples - 1) * full + mean_weight


def own_weights(w_ref, core):
    half = w_ref.shape[1] // 2
    rows = half // 2
    w = w_ref[:, half:]
    return jnp.where(core == 0, w[:, :rows], w[:, rows:])


def split_dot(parts, x):
    th, stacked = parts
    rows = th.shape[0]
    xh, xl = split2(x)
    dot = functools.partial(jnp.dot, preferred_element_type=jnp.float32)
    both = dot(stacked, xh)
    return (both[rows:] + dot(th, xl)) + both[:rows]


def left_parts(t):
    th, tl = split2(t)
    return th, jnp.concatenate([th, tl], axis=0)


def filter_kernel(
    spaces,
    x_hbm,
    idx_ref,
    data_ref,
    sigma_ref,
    used_ref,
    out_ref,
    xall,
    full,
    gram,
    cross,
    parts,
    cparts,
    total,
    t_ref,
    inv_ref,
    w_ref,
    sum_out,
    sum_in,
    mix_out,
    mix_in,
    ready,
    load,
    xs_send,
    xs_recv,
    fw_send,
    fw_recv,
    rs_send,
    rs_recv,
    cr_send,
    cr_recv,
    ag_send,
    ag_recv,
    pair_send,
    pair_recv,
    one_send,
    one_recv,
):
    rank = lax.axis_index("member")
    place = lax.axis_index("space")
    core = lax.rem(rank, 2)
    lower = rank < 2
    upper = rank >= 2
    side = rank + 1 - 2 * core
    across = lax.rem(rank + 2, 4)
    diagonal = lax.rem(side + 2, 4)
    rows, points = x_hbm.shape
    samples, slots = full.shape
    half = samples // 2
    stripe = gram.shape[0]
    chunk = stripe // spaces
    peers = [lax.rem(place + d, spaces) for d in range(1, spaces)]
    chunks = offsets(CHUNKS)

    def rows_of(member):
        return pl.ds(pl.multiple_of(member * rows, SUBLANES), rows)

    def remote(src, dst, sems, i, member, space):
        return pltpu.make_async_remote_copy(
            src_ref=src,
            dst_ref=dst,
            send_sem=sems[0].at[i],
            recv_sem=sems[1].at[i],
            device_id={"member": member, "space": space},
            device_id_type=MESH,
        )

    own = rows_of(rank)
    xs, fw, rs = (xs_send, xs_recv), (fw_send, fw_recv), (rs_send, rs_recv)
    cr, ag, pair, one = (
        (cr_send, cr_recv),
        (ag_send, ag_recv),
        (pair_send, pair_recv),
        (one_send, one_recv),
    )

    def stream(i):
        first, width = chunks[i]
        columns = slice(first, first + width)
        return remote(x_hbm.at[:, columns], xall.at[own, columns], xs, i, across, place)

    def arriving(i):
        first, width = chunks[i]
        columns = slice(first, first + width)
        here = xall.at[rows_of(across), columns]
        return remote(here, here, xs, i, across, place)

    def forward(i):
        first, width = chunks[i]
        columns = slice(first, first + width)
        here = xall.at[rows_of(across), columns]
        return remote(here, here, fw, i, side, place)

    def simple(ref, i, member, space=None):
        return remote(ref, ref, one, i, member, place if space is None else space)

    swap_x = simple(xall.at[own], 0, side)
    observed = simple(full.at[own], 1, across)
    observed_side = simple(full.at[own], 2, side)
    observed_far = simple(full.at[rows_of(across)], 3, side)
    swap_total = simple(total.at[core], 4, side)
    piece_rows = pl.ds(pl.multiple_of(place * chunk, SUBLANES), chunk)
    piece = total.at[core, piece_rows]
    cross_total = total.at[core, pl.ds(stripe, SUBLANES)]
    piece_far = simple(piece, 5, across)
    cross_far = simple(cross_total, 6, across)
    sums = [
        remote(sum_out, sum_in.at[core], pair, i, m, place) for i, m in ((0, across), (1, diagonal))
    ]
    mixes = [
        remote(mix_out, mix_in.at[core], pair, 2 + i, m, place)
        for i, m in ((0, across), (1, diagonal))
    ]
    spread = [remote(piece, piece, ag, d, rank, p) for d, p in enumerate(peers)]

    barrier = pltpu.get_barrier_semaphore()

    def greet(member, space):
        pl.semaphore_signal(
            barrier, inc=1, device_id={"member": member, "space": space}, device_id_type=MESH
        )

    @pl.when(upper)
    def _():
        greet(across, place)
        greet(side, place)
        for p in peers:
            greet(rank, p)

    @pl.when(lower)
    def _():
        greet(across, place)
        greet(diagonal, place)
        for p in peers:
            greet(across, p)

    def loading(t):
        columns = pl.ds(pl.multiple_of(t * GATHER, LANES), GATHER)
        return pltpu.make_async_copy(x_hbm.at[:, columns], xall.at[own, columns], load.at[t])

    for t in range(points // GATHER):
        loading(t).start()
    full[own, :] = jnp.zeros((rows, slots), jnp.float32)

    @pl.when(lower)
    def _():
        pl.semaphore_wait(barrier, 1)
        for i in range(EARLY):
            stream(i).start()

    gather_rows(
        xall, rank * rows, idx_ref, full, rows, points, lambda t: loading(t).wait()
    )

    @pl.when(upper)
    def _():
        pl.semaphore_wait(barrier, 2 * spaces + 1)
        pl.semaphore_signal(
            ready, inc=1, device_id={"member": across, "space": place}, device_id_type=MESH
        )
        observed.start()
        swap_x.start()
        sum_out[...] = jnp.sum(xall[own, :], axis=0, keepdims=True)
        for copy in sums:
            copy.start()
        for i in range(EARLY):
            arriving(i).wait_recv()
            forward(i).start()
        piece_far.wait_recv()
        cross_far.wait_recv()
        for copy in spread:
            copy.start()

    @pl.when(lower)
    def _():
        pl.semaphore_wait(ready, 1)
        observed_side.start()
        observed.wait_recv()
        observed_far.start()
        swap_x.start()
        observed_side.wait_recv()
        observed_far.wait_recv()
        slot = lax.broadcasted_iota(jnp.int32, (1, slots), 1)
        weight = jnp.where(slot < used_ref[0], 1.0 / flat_row(sigma_ref), 0.0)
        ev = full[...]
        mean = jnp.sum(ev, axis=0, keepdims=True) * (1.0 / samples)
        anomalies = (ev - mean) * weight
        innovation = (flat_row(data_ref) - mean) * weight
        first = lax.broadcasted_iota(jnp.int32, (SUBLANES, slots), 0) == 0
        extra = jnp.where(first, jnp.broadcast_to(innovation, (SUBLANES, slots)), 0.0)
        across_rows = ((1,), (1,))

        @pl.when(core == 0)
        def _():
            gram[...] = dot3(anomalies[:stripe], anomalies[:half], across_rows)
            cross[...] = dot3(extra, anomalies[:half], across_rows)

        @pl.when(core == 1)
        def _():
            top = samples - stripe
            gram[:top, :] = dot3(anomalies[stripe:], anomalies[:half], across_rows)
            gram[top:, :] = dot3(anomalies[half:], anomalies[half:], across_rows)
            cross[...] = dot3(extra, anomalies[half:], across_rows)

        scatter = [
            remote(
                gram.at[pl.ds(pl.multiple_of(p * chunk, SUBLANES), chunk)],
                parts.at[d],
                rs,
                d,
                rank,
                p,
            )
            for d, p in enumerate(peers)
        ]
        shared = [remote(cross, cparts.at[d], cr, d, rank, p) for d, p in enumerate(peers)]
        for a, b in zip(scatter, shared):
            a.start()
            b.start()
        acc = gram[piece_rows, :]
        acc_cross = cross[...]
        for d in range(spaces - 1):
            scatter[d].wait_recv()
            shared[d].wait_recv()
            acc = acc + parts[d]
            acc_cross = acc_cross + cparts[d]
        total[core, piece_rows, :] = acc
        total[core, stripe : stripe + SUBLANES, :] = acc_cross
        piece_far.start()
        cross_far.start()
        for copy in spread:
            copy.start()
        for i in range(EARLY, len(chunks)):
            stream(i).start()
        for copy in (*scatter, *shared):
            copy.wait_send()

    for copy in spread:
        copy.wait_recv()
    swap_total.start()
    swap_total.wait_recv()

    rest = stripe - half
    blocks = {
        (0, 0): total[0, :half, :],
        (1, 0): jnp.concatenate([total[0, half:stripe, :], total[1, : half - rest, :]], axis=0),
        (1, 1): total[1, half - rest : stripe, :],
    }
    cross_row = jnp.concatenate(
        [total[0, stripe : stripe + 1, :], total[1, stripe : stripe + 1, :]], axis=1
    )
    transform_of(blocks, cross_row, t_ref, inv_ref, w_ref)

    def tiles(first, last, body):
        def step(t, _):
            body(pl.ds(pl.multiple_of(t * TILE, LANES), TILE))
            return 0

        lax.fori_loop(first, last, step, 0)

    @pl.when(lower)
    def _():
        mine = left_parts(t_ref[own, :half])
        weight_sum = jnp.sum(w_ref[0:1, half:], axis=1, keepdims=True)
        swap_x.wait_recv()
        for i in range(2):
            source = core if i == 0 else 1 - core
            remote(sum_out, sum_in.at[source], pair, i, across, place).wait_recv()
            remote(mix_out, mix_in.at[source], pair, 2 + i, across, place).wait_recv()

        def body(columns):
            x = xall[:half, columns]
            mean = jnp.sum(x, axis=0, keepdims=True)
            mean = (mean + sum_in[0, :, columns] + sum_in[1, :, columns]) * (1.0 / samples)
            other = mix_in[0, :, columns] + mix_in[1, :, columns] - weight_sum * mean
            out_ref[:, columns] = split_dot(mine, x - mean) + (mean + other)

        tiles(0, points // TILE, body)
        for i in range(len(chunks)):
            stream(i).wait_send()
        observed_side.wait_send()
        observed_far.wait_send()
        piece_far.wait_send()
        cross_far.wait_send()

    @pl.when(upper)
    def _():
        mix = dot3(own_weights(w_ref, core), xall[own, :])
        mix_out[...] = mix[0:1, :]
        for copy in mixes:
            copy.start()
        mine = left_parts(t_ref[own, :])
        swap_x.wait_recv()

        def body(columns):
            x = xall[:, columns]
            mean = jnp.sum(x, axis=0, keepdims=True) * (1.0 / samples)
            out_ref[:, columns] = split_dot(mine, x - mean) + mean

        for i in range(EARLY, READY):
            arriving(i).wait_recv()
            forward(i).start()
        for i in range(EARLY):
            forward(i).wait_recv()
        tiles(0, EARLY, body)
        for i in range(EARLY, READY):
            forward(i).wait_recv()
        tiles(EARLY, READY, body)
        for i in range(READY, len(chunks)):
            arriving(i).wait_recv()
            forward(i).start()
            if i > READY:
                forward(i - 1).wait_recv()
                first, width = chunks[i - 1]
                body(slice(first, first + width))
        last = len(chunks) - 1
        forward(last).wait_recv()
        first, width = chunks[last]
        body(slice(first, first + width))
        for i in range(len(chunks)):
            forward(i).wait_send()
        observed.wait_send()
        for copy in (*sums, *mixes):
            copy.wait_send()

    swap_x.wait_send()
    swap_total.wait_send()
    for copy in spread:
        copy.wait_send()


def filtered(prior, index, data, sigma, used, spaces):
    rows, points = prior.shape
    slots = index.size
    samples = 4 * rows
    half = samples // 2
    stripe = 3 * half // 2
    f32 = jnp.float32
    dma = pltpu.SemaphoreType.DMA
    vmem = pltpu.VMEM
    chunk = stripe // spaces
    others = (spaces - 1,)
    pieces = (len(CHUNKS),)
    return pl.pallas_call(
        functools.partial(filter_kernel, spaces),
        out_shape=jax.ShapeDtypeStruct((rows, points), f32),
        in_specs=[pl.BlockSpec(memory_space=pl.ANY)]
        + [VMEM_SPEC] * 3
        + [pl.BlockSpec(memory_space=pltpu.SMEM)],
        out_specs=VMEM_SPEC,
        scratch_shapes=[
            vmem((samples, points), f32),
            vmem((samples, slots), f32),
            vmem((stripe, half), f32),
            vmem((SUBLANES, half), f32),
            vmem((spaces - 1, chunk, half), f32),
            vmem((spaces - 1, SUBLANES, half), f32),
            vmem((2, stripe + SUBLANES, half), f32),
            vmem((samples, samples), f32),
            vmem((samples, samples), f32),
            vmem((SUBLANES, samples), f32),
            vmem((1, points), f32),
            vmem((2, 1, points), f32),
            vmem((1, points), f32),
            vmem((2, 1, points), f32),
            pltpu.SemaphoreType.REGULAR,
            dma((points // GATHER,)),
            dma(pieces),
            dma(pieces),
            dma(pieces),
            dma(pieces),
            dma(others),
            dma(others),
            dma(others),
            dma(others),
            dma(others),
            dma(others),
            dma((4,)),
            dma((4,)),
            dma((7,)),
            dma((7,)),
        ],
        compiler_params=pltpu.CompilerParams(
            collective_id=0, has_side_effects=True, vmem_limit_bytes=32 * MIB
        ),
    )(prior, index, data, sigma, used)


def body(*arrays):
    prior_sample, location = arrays[:2]
    rows, points = prior_sample.shape
    members, spaces = lax.axis_size("member"), lax.axis_size("space")
    if (
        members != 4
        or rows * members != 2 * LANES
        or 3 * LANES // 2 % (SUBLANES * spaces)
        or points != sum(CHUNKS)
        or location.shape[1] != LANES
    ):
        return general_body(*arrays)
    return filtered(*arrays, spaces)


def solution(mesh):
    placed = (
        P("member", "space"),
        P("space", None),
        P("space", None),
        P("space", None),
        P("space"),
    )
    return jax.shard_map(
        body, mesh=mesh, in_specs=placed, out_specs=P("member", "space"), check_vma=False
    )
```

```python
import functools
import math

import jax
import jax.numpy as jnp
from jax import lax
from jax.experimental import pallas as pl
from jax.experimental.pallas import tpu as pltpu
from jax.sharding import PartitionSpec as P


def solve_lower(lower_factor, target):
    return lax.linalg.triangular_solve(lower_factor, target, left_side=True, lower=True)


def general_body(
    prior_sample,
    measured_point_location,
    measured_data,
    measurement_noise_sigma,
    measured_slots_used,
):
    exact_arithmetic = lax.Precision.HIGHEST
    anomaly_matrix, points_in_region = prior_sample.shape
    region_batches = lax.axis_size("member")
    sample_total = anomaly_matrix * region_batches
    pointwise_spread = points_in_region // region_batches
    linear_position = measured_point_location.reshape(-1)
    obs_blk = linear_position.shape[0]
    observation_deviation = obs_blk // region_batches
    propagated_grid = jnp.take(prior_sample, linear_position, axis=1).reshape(
        anomaly_matrix, region_batches, observation_deviation
    )
    prior_regions = prior_sample.reshape(anomaly_matrix, region_batches, pointwise_spread)
    prior_sample_full, integrate_dynamics = (
        lax.all_to_all(prior_regions, "member", split_axis=1, concat_axis=0, tiled=True),
        lax.all_to_all(propagated_grid, "member", split_axis=1, concat_axis=0, tiled=True),
    )
    integrate_dynamics = integrate_dynamics.reshape(sample_total, observation_deviation)
    rank = lax.axis_index("member")
    start = rank * observation_deviation
    my_value = lax.dynamic_slice_in_dim(measured_data.reshape(-1), start, observation_deviation)
    my_sigma = lax.dynamic_slice_in_dim(
        measurement_noise_sigma.reshape(-1), start, observation_deviation
    )
    slots = start + jnp.arange(observation_deviation, dtype=jnp.int32)
    valid = slots < measured_slots_used[0]
    weight = jnp.where(valid, 1.0 / my_sigma, jnp.zeros_like(my_sigma))
    sim_mean = jnp.mean(integrate_dynamics, axis=0)
    perturbed = (integrate_dynamics - sim_mean[None, :]) * weight[None, :]
    innovation = (my_value - sim_mean) * weight
    gram_loc = jnp.dot(perturbed, perturbed.T, precision=exact_arithmetic)
    cross_loc = jnp.dot(perturbed, innovation, precision=exact_arithmetic)
    gram_block, cross_block = lax.psum((gram_loc, cross_loc), "member")
    gram_all, cross = lax.psum((gram_block, cross_block), "space")
    cov_matrix = gram_all + (sample_total - 1) * jnp.eye(sample_total, dtype=jnp.float32)
    lower_factor = jnp.linalg.cholesky(cov_matrix)
    inverse = solve_lower(lower_factor, jnp.eye(sample_total, dtype=jnp.float32))
    projected = jnp.dot(inverse, cross, precision=exact_arithmetic)
    mean_weight = jnp.dot(inverse.T, projected, precision=exact_arithmetic)
    weight_matrix_update = math.sqrt(sample_total - 1) * inverse + mean_weight[None, :]
    sample_vectors = prior_sample_full.reshape(sample_total, -1)
    prior_average = jnp.mean(sample_vectors, axis=0)
    updated_sample = prior_average[None, :] + jnp.dot(
        weight_matrix_update, sample_vectors - prior_average[None, :], precision=exact_arithmetic
    )
    returned = lax.all_to_all(
        updated_sample.reshape(prior_sample_full.shape),
        "member",
        split_axis=0,
        concat_axis=1,
        tiled=True,
    )
    return returned.reshape(anomaly_matrix, points_in_region)


MESH = pl.DeviceIdType.MESH
VMEM_SPEC = pl.BlockSpec(memory_space=pltpu.VMEM)
LANES = 128
MIB = 1 << 20
SUBLANES = 8


def split2(x):
    high = x.astype(jnp.bfloat16)
    low = (x - high.astype(jnp.float32)).astype(jnp.bfloat16)
    return high, low


def dot3(a, b, dims=((1,), (0,))):
    ah, al = split2(a)
    bh, bl = split2(b)
    d = functools.partial(
        lax.dot_general, dimension_numbers=(dims, ((), ())), preferred_element_type=jnp.float32
    )
    return (d(ah, bl) + d(al, bh)) + d(ah, bh)


def flat_row(ref):
    return jnp.concatenate([ref[i : i + 1, :] for i in range(ref.shape[0])], axis=1)


PIVOTS = 4


def inverse_factor(a):
    size = a.shape[0]
    count = size // SUBLANES
    shape = (SUBLANES, size)
    m = [a[SUBLANES * i : SUBLANES * (i + 1), :] for i in range(count)]
    diag = [None] * count
    lane = lax.broadcasted_iota(jnp.int32, shape, 1)
    sub = lax.broadcasted_iota(jnp.int32, shape, 0)

    def column(x, k):
        return jnp.broadcast_to(x[:, k : k + 1], shape)

    def row(x, r):
        return jnp.broadcast_to(x[r : r + 1, :], shape)

    for k in range(0, size, PIVOTS):
        t, r = divmod(k, SUBLANES)
        inside = (lane >= k) & (lane < k + PIVOTS)
        cols = [column(m[t], k + q) for q in range(PIVOTS)]
        pivot = {(q, p): row(cols[p], r + q) for p in range(PIVOTS) for q in range(p, PIVOTS)}
        base = [
            jnp.where(inside, jnp.where(lane == k + q, 1.0, 0.0), row(m[t], r + q))
            for q in range(PIVOTS)
        ]
        inverse = []
        for p in range(PIVOTS):
            inverse.append(1.0 / pivot[p, p])
            for q in range(p + 1, PIVOTS):
                factor = pivot[q, p] * inverse[p]
                base[q] = base[q] - factor * base[p]
                for s in range(q, PIVOTS):
                    pivot[s, q] = pivot[s, q] - factor * pivot[s, p]
        for p in range(PIVOTS):
            old = diag[t]
            diag[t] = pivot[p, p] if old is None else jnp.where(sub >= r + p, pivot[p, p], old)
        for i in range(t, count):
            cols_i = cols if i == t else [column(m[i], k + q) for q in range(PIVOTS)]
            cols_i = list(cols_i)
            if i == t:
                unit = jnp.where(lane - k == sub - r, 1.0, 0.0)
                x = jnp.where(inside & (sub >= r), unit, m[i])
            else:
                x = jnp.where(inside, 0.0, m[i])
            for p in range(PIVOTS):
                mult = cols_i[p] * inverse[p]
                if i == t:
                    mult = jnp.where(sub > r + p, mult, 0.0)
                for q in range(p + 1, PIVOTS):
                    cols_i[q] = cols_i[q] - mult * pivot[q, p]
                x = x - mult * base[p]
            m[i] = x
    out = []
    for i in range(count):
        keep = lane <= sub + SUBLANES * i
        out.append(jnp.where(keep, m[i] * lax.rsqrt(diag[i]), 0.0))
    return jnp.concatenate(out, axis=0)


def eye_mask(rows, cols):
    shape = (rows, cols)
    return lax.broadcasted_iota(jnp.int32, shape, 0) == lax.broadcasted_iota(jnp.int32, shape, 1)


TILE = 512
CHUNKS = (512,) * 15 + (256,) * 2
EARLY = 6
READY = 13
GATHER = 1024


def offsets(widths):
    return [(sum(widths[:i]), w) for i, w in enumerate(widths)]


def gather_rows(x_ref, first, idx_ref, out_ref, rows, points, arrived):
    shape = (SUBLANES, LANES)
    blocks = GATHER // LANES

    def step(t, _):
        arrived(t)
        for c in range(idx_ref.shape[0]):
            index = jnp.broadcast_to(idx_ref[c : c + 1, :], shape)
            lane = jnp.bitwise_and(index, LANES - 1)
            block = jnp.right_shift(index, LANES.bit_length() - 1) - t * blocks
            hits = [block == j for j in range(blocks)]
            columns = slice(c * LANES, (c + 1) * LANES)
            for g in range(0, rows, SUBLANES):
                place = pl.ds(pl.multiple_of(first + g, SUBLANES), SUBLANES)
                got = out_ref[place, columns]
                for j in range(blocks):
                    at = pl.ds(pl.multiple_of(t * GATHER + j * LANES, LANES), LANES)
                    x = x_ref[place, at]
                    got = jnp.where(hits[j], jnp.take_along_axis(x, lane, axis=1), got)
                out_ref[place, columns] = got
        return 0

    lax.fori_loop(0, points // GATHER, step, 0)


def transform_of(low_blocks, cross, t_ref, inv_ref, w_ref):
    samples = t_ref.shape[0]
    b = LANES
    ridge = float(samples - 1)
    n = samples // b
    work = {}
    for (i, j), block in low_blocks.items():
        work[i, j] = block + jnp.where(eye_mask(b, b), ridge, 0.0) if i == j else block
    inv = {}
    low = {}
    for k in range(n):
        inv[k, k] = inverse_factor(work[k, k])
        for i in range(k + 1, n):
            low[i, k] = dot3(work[i, k], inv[k, k], ((1,), (1,)))
        for i in range(k + 1, n):
            for j in range(k + 1, i + 1):
                work[i, j] = work[i, j] - dot3(low[i, k], low[j, k], ((1,), (1,)))
        for j in range(k):
            acc = dot3(low[k, j], inv[j, j])
            for m in range(j + 1, k):
                acc = acc + dot3(low[k, m], inv[m, j])
            inv[k, j] = -dot3(inv[k, k], acc)
    zero = jnp.zeros((b, b), jnp.float32)
    full = jnp.concatenate(
        [
            jnp.concatenate([inv[i, j] if j <= i else zero for j in range(n)], axis=1)
            for i in range(n)
        ],
        axis=0,
    )
    inv_ref[...] = full
    projected = jnp.sum(full * cross, axis=1, keepdims=True)
    mean_weight = jnp.sum(full * projected, axis=0, keepdims=True)
    w_ref[...] = jnp.broadcast_to(mean_weight, w_ref.shape)
    t_ref[...] = math.sqrt(samples - 1) * full + mean_weight


def own_weights(w_ref, core):
    half = w_ref.shape[1] // 2
    rows = half // 2
    w = w_ref[:, half:]
    return jnp.where(core == 0, w[:, :rows], w[:, rows:])


def split_dot(parts, x):
    th, stacked = parts
    rows = th.shape[0]
    xh, xl = split2(x)
    dot = functools.partial(jnp.dot, preferred_element_type=jnp.float32)
    both = dot(stacked, xh)
    return (both[rows:] + dot(th, xl)) + both[:rows]


def left_parts(t):
    th, tl = split2(t)
    return th, jnp.concatenate([th, tl], axis=0)


def filter_kernel(
    spaces,
    x_hbm,
    idx_hbm,
    data_hbm,
    sigma_hbm,
    used_ref,
    out_ref,
    idx_ref,
    data_ref,
    sigma_ref,
    xall,
    full,
    gram,
    cross,
    parts,
    cparts,
    total,
    t_ref,
    inv_ref,
    w_ref,
    sum_out,
    sum_in,
    mix_out,
    mix_in,
    ready,
    load,
    small,
    xs_send,
    xs_recv,
    fw_send,
    fw_recv,
    rs_send,
    rs_recv,
    cr_send,
    cr_recv,
    ag_send,
    ag_recv,
    pair_send,
    pair_recv,
    one_send,
    one_recv,
):
    rank = lax.axis_index("member")
    place = lax.axis_index("space")
    core = lax.rem(rank, 2)
    lower = rank < 2
    upper = rank >= 2
    side = rank + 1 - 2 * core
    across = lax.rem(rank + 2, 4)
    diagonal = lax.rem(side + 2, 4)
    rows, points = x_hbm.shape
    samples, slots = full.shape
    half = samples // 2
    stripe = gram.shape[0]
    chunk = stripe // spaces
    peers = [lax.rem(place + d, spaces) for d in range(1, spaces)]
    chunks = offsets(CHUNKS)

    def rows_of(member):
        return pl.ds(pl.multiple_of(member * rows, SUBLANES), rows)

    def remote(src, dst, sems, i, member, space):
        return pltpu.make_async_remote_copy(
            src_ref=src,
            dst_ref=dst,
            send_sem=sems[0].at[i],
            recv_sem=sems[1].at[i],
            device_id={"member": member, "space": space},
            device_id_type=MESH,
        )

    own = rows_of(rank)
    xs, fw, rs = (xs_send, xs_recv), (fw_send, fw_recv), (rs_send, rs_recv)
    cr, ag, pair, one = (
        (cr_send, cr_recv),
        (ag_send, ag_recv),
        (pair_send, pair_recv),
        (one_send, one_recv),
    )

    def stream(i):
        first, width = chunks[i]
        columns = slice(first, first + width)
        return remote(x_hbm.at[:, columns], xall.at[own, columns], xs, i, across, place)

    def arriving(i):
        first, width = chunks[i]
        columns = slice(first, first + width)
        here = xall.at[rows_of(across), columns]
        return remote(here, here, xs, i, across, place)

    def forward(i):
        first, width = chunks[i]
        columns = slice(first, first + width)
        here = xall.at[rows_of(across), columns]
        return remote(here, here, fw, i, side, place)

    def simple(ref, i, member, space=None):
        return remote(ref, ref, one, i, member, place if space is None else space)

    swap_x = simple(xall.at[own], 0, side)
    observed = simple(full.at[own], 1, across)
    observed_side = simple(full.at[own], 2, side)
    observed_far = simple(full.at[rows_of(across)], 3, side)
    swap_total = simple(total.at[core], 4, side)
    piece_rows = pl.ds(pl.multiple_of(place * chunk, SUBLANES), chunk)
    piece = total.at[core, piece_rows]
    cross_total = total.at[core, pl.ds(stripe, SUBLANES)]
    piece_far = simple(piece, 5, across)
    cross_far = simple(cross_total, 6, across)
    sums = [
        remote(sum_out, sum_in.at[core], pair, i, m, place) for i, m in ((0, across), (1, diagonal))
    ]
    mixes = [
        remote(mix_out, mix_in.at[core], pair, 2 + i, m, place)
        for i, m in ((0, across), (1, diagonal))
    ]
    spread = [remote(piece, piece, ag, d, rank, p) for d, p in enumerate(peers)]

    barrier = pltpu.get_barrier_semaphore()

    def greet(member, space):
        pl.semaphore_signal(
            barrier, inc=1, device_id={"member": member, "space": space}, device_id_type=MESH
        )

    @pl.when(upper)
    def _():
        greet(across, place)
        greet(side, place)
        for p in peers:
            greet(rank, p)

    @pl.when(lower)
    def _():
        greet(across, place)
        greet(diagonal, place)
        for p in peers:
            greet(across, p)

    def loading(t):
        columns = pl.ds(pl.multiple_of(t * GATHER, LANES), GATHER)
        return pltpu.make_async_copy(x_hbm.at[:, columns], xall.at[own, columns], load.at[t])

    tables = [
        pltpu.make_async_copy(src, dst, small.at[i])
        for i, (src, dst) in enumerate(
            ((idx_hbm, idx_ref), (data_hbm, data_ref), (sigma_hbm, sigma_ref))
        )
    ]
    for copy in tables:
        copy.start()
    for t in range(points // GATHER):
        loading(t).start()
    full[own, :] = jnp.zeros((rows, slots), jnp.float32)

    @pl.when(lower)
    def _():
        pl.semaphore_wait(barrier, 1)
        for i in range(EARLY):
            stream(i).start()

    for copy in tables:
        copy.wait()
    gather_rows(
        xall, rank * rows, idx_ref, full, rows, points, lambda t: loading(t).wait()
    )

    @pl.when(upper)
    def _():
        pl.semaphore_wait(barrier, 2 * spaces + 1)
        pl.semaphore_signal(
            ready, inc=1, device_id={"member": across, "space": place}, device_id_type=MESH
        )
        observed.start()
        swap_x.start()
        sum_out[...] = jnp.sum(xall[own, :], axis=0, keepdims=True)
        for copy in sums:
            copy.start()
        for i in range(EARLY):
            arriving(i).wait_recv()
            forward(i).start()
        piece_far.wait_recv()
        cross_far.wait_recv()
        for copy in spread:
            copy.start()

    @pl.when(lower)
    def _():
        pl.semaphore_wait(ready, 1)
        observed_side.start()
        observed.wait_recv()
        observed_far.start()
        swap_x.start()
        observed_side.wait_recv()
        observed_far.wait_recv()
        slot = lax.broadcasted_iota(jnp.int32, (1, slots), 1)
        weight = jnp.where(slot < used_ref[0], 1.0 / flat_row(sigma_ref), 0.0)
        ev = full[...]
        mean = jnp.sum(ev, axis=0, keepdims=True) * (1.0 / samples)
        anomalies = (ev - mean) * weight
        innovation = (flat_row(data_ref) - mean) * weight
        first = lax.broadcasted_iota(jnp.int32, (SUBLANES, slots), 0) == 0
        extra = jnp.where(first, jnp.broadcast_to(innovation, (SUBLANES, slots)), 0.0)
        across_rows = ((1,), (1,))

        @pl.when(core == 0)
        def _():
            gram[...] = dot3(anomalies[:stripe], anomalies[:half], across_rows)
            cross[...] = dot3(extra, anomalies[:half], across_rows)

        @pl.when(core == 1)
        def _():
            top = samples - stripe
            gram[:top, :] = dot3(anomalies[stripe:], anomalies[:half], across_rows)
            gram[top:, :] = dot3(anomalies[half:], anomalies[half:], across_rows)
            cross[...] = dot3(extra, anomalies[half:], across_rows)

        scatter = [
            remote(
                gram.at[pl.ds(pl.multiple_of(p * chunk, SUBLANES), chunk)],
                parts.at[d],
                rs,
                d,
                rank,
                p,
            )
            for d, p in enumerate(peers)
        ]
        shared = [remote(cross, cparts.at[d], cr, d, rank, p) for d, p in enumerate(peers)]
        for a, b in zip(scatter, shared):
            a.start()
            b.start()
        acc = gram[piece_rows, :]
        acc_cross = cross[...]
        for d in range(spaces - 1):
            scatter[d].wait_recv()
            shared[d].wait_recv()
            acc = acc + parts[d]
            acc_cross = acc_cross + cparts[d]
        total[core, piece_rows, :] = acc
        total[core, stripe : stripe + SUBLANES, :] = acc_cross
        piece_far.start()
        cross_far.start()
        for copy in spread:
            copy.start()
        for i in range(EARLY, len(chunks)):
            stream(i).start()
        for copy in (*scatter, *shared):
            copy.wait_send()

    for copy in spread:
        copy.wait_recv()
    swap_total.start()
    swap_total.wait_recv()

    rest = stripe - half
    blocks = {
        (0, 0): total[0, :half, :],
        (1, 0): jnp.concatenate([total[0, half:stripe, :], total[1, : half - rest, :]], axis=0),
        (1, 1): total[1, half - rest : stripe, :],
    }
    cross_row = jnp.concatenate(
        [total[0, stripe : stripe + 1, :], total[1, stripe : stripe + 1, :]], axis=1
    )
    transform_of(blocks, cross_row, t_ref, inv_ref, w_ref)

    def tiles(first, last, body):
        def step(t, _):
            body(pl.ds(pl.multiple_of(t * TILE, LANES), TILE))
            return 0

        lax.fori_loop(first, last, step, 0)

    @pl.when(lower)
    def _():
        mine = left_parts(t_ref[own, :half])
        weight_sum = jnp.sum(w_ref[0:1, half:], axis=1, keepdims=True)
        swap_x.wait_recv()
        for i in range(2):
            source = core if i == 0 else 1 - core
            remote(sum_out, sum_in.at[source], pair, i, across, place).wait_recv()
            remote(mix_out, mix_in.at[source], pair, 2 + i, across, place).wait_recv()

        def body(columns):
            x = xall[:half, columns]
            mean = jnp.sum(x, axis=0, keepdims=True)
            mean = (mean + sum_in[0, :, columns] + sum_in[1, :, columns]) * (1.0 / samples)
            other = mix_in[0, :, columns] + mix_in[1, :, columns] - weight_sum * mean
            out_ref[:, columns] = split_dot(mine, x - mean) + (mean + other)

        tiles(0, points // TILE, body)
        for i in range(len(chunks)):
            stream(i).wait_send()
        observed_side.wait_send()
        observed_far.wait_send()
        piece_far.wait_send()
        cross_far.wait_send()

    @pl.when(upper)
    def _():
        mix = dot3(own_weights(w_ref, core), xall[own, :])
        mix_out[...] = mix[0:1, :]
        for copy in mixes:
            copy.start()
        mine = left_parts(t_ref[own, :])
        swap_x.wait_recv()

        def body(columns):
            x = xall[:, columns]
            mean = jnp.sum(x, axis=0, keepdims=True) * (1.0 / samples)
            out_ref[:, columns] = split_dot(mine, x - mean) + mean

        for i in range(EARLY, READY):
            arriving(i).wait_recv()
            forward(i).start()
        for i in range(EARLY):
            forward(i).wait_recv()
        tiles(0, EARLY, body)
        for i in range(EARLY, READY):
            forward(i).wait_recv()
        tiles(EARLY, READY, body)
        for i in range(READY, len(chunks)):
            arriving(i).wait_recv()
            forward(i).start()
            if i > READY:
                forward(i - 1).wait_recv()
                first, width = chunks[i - 1]
                body(slice(first, first + width))
        last = len(chunks) - 1
        forward(last).wait_recv()
        first, width = chunks[last]
        body(slice(first, first + width))
        for i in range(len(chunks)):
            forward(i).wait_send()
        observed.wait_send()
        for copy in (*sums, *mixes):
            copy.wait_send()

    swap_x.wait_send()
    swap_total.wait_send()
    for copy in spread:
        copy.wait_send()


def filtered(prior, index, data, sigma, used, spaces):
    rows, points = prior.shape
    slots = index.size
    samples = 4 * rows
    half = samples // 2
    stripe = 3 * half // 2
    f32 = jnp.float32
    dma = pltpu.SemaphoreType.DMA
    vmem = pltpu.VMEM
    chunk = stripe // spaces
    others = (spaces - 1,)
    pieces = (len(CHUNKS),)
    return pl.pallas_call(
        functools.partial(filter_kernel, spaces),
        out_shape=jax.ShapeDtypeStruct((rows, points), f32),
        in_specs=[pl.BlockSpec(memory_space=pltpu.HBM)] * 4
        + [pl.BlockSpec(memory_space=pltpu.SMEM)],
        out_specs=VMEM_SPEC,
        scratch_shapes=[
            vmem(index.shape, jnp.int32),
            vmem(data.shape, f32),
            vmem(sigma.shape, f32),
            vmem((samples, points), f32),
            vmem((samples, slots), f32),
            vmem((stripe, half), f32),
            vmem((SUBLANES, half), f32),
            vmem((spaces - 1, chunk, half), f32),
            vmem((spaces - 1, SUBLANES, half), f32),
            vmem((2, stripe + SUBLANES, half), f32),
            vmem((samples, samples), f32),
            vmem((samples, samples), f32),
            vmem((SUBLANES, samples), f32),
            vmem((1, points), f32),
            vmem((2, 1, points), f32),
            vmem((1, points), f32),
            vmem((2, 1, points), f32),
            pltpu.SemaphoreType.REGULAR,
            dma((points // GATHER,)),
            dma((3,)),
            dma(pieces),
            dma(pieces),
            dma(pieces),
            dma(pieces),
            dma(others),
            dma(others),
            dma(others),
            dma(others),
            dma(others),
            dma(others),
            dma((4,)),
            dma((4,)),
            dma((7,)),
            dma((7,)),
        ],
        compiler_params=pltpu.CompilerParams(
            collective_id=0, has_side_effects=True, vmem_limit_bytes=32 * MIB
        ),
    )(prior, index, data, sigma, used)


def body(*arrays):
    prior_sample, location = arrays[:2]
    rows, points = prior_sample.shape
    members, spaces = lax.axis_size("member"), lax.axis_size("space")
    if (
        members != 4
        or rows * members != 2 * LANES
        or 3 * LANES // 2 % (SUBLANES * spaces)
        or points != sum(CHUNKS)
        or location.shape[1] != LANES
    ):
        return general_body(*arrays)
    held = [pltpu.with_memory_space_constraint(a, pltpu.HBM) for a in arrays[:4]]
    return filtered(*held, arrays[4], spaces)


def solution(mesh):
    placed = (
        P("member", "space"),
        P("space", None),
        P("space", None),
        P("space", None),
        P("space"),
    )
    return jax.shard_map(
        body, mesh=mesh, in_specs=placed, out_specs=P("member", "space"), check_vma=False
    )
```

```python
import functools
import math

import jax
import jax.numpy as jnp
from jax import lax
from jax.experimental import pallas as pl
from jax.experimental.pallas import tpu as pltpu
from jax.sharding import PartitionSpec as P


def solve_lower(lower_factor, target):
    return lax.linalg.triangular_solve(lower_factor, target, left_side=True, lower=True)


def general_body(
    prior_sample,
    measured_point_location,
    measured_data,
    measurement_noise_sigma,
    measured_slots_used,
):
    exact_arithmetic = lax.Precision.HIGHEST
    anomaly_matrix, points_in_region = prior_sample.shape
    region_batches = lax.axis_size("member")
    sample_total = anomaly_matrix * region_batches
    pointwise_spread = points_in_region // region_batches
    linear_position = measured_point_location.reshape(-1)
    obs_blk = linear_position.shape[0]
    observation_deviation = obs_blk // region_batches
    propagated_grid = jnp.take(prior_sample, linear_position, axis=1).reshape(
        anomaly_matrix, region_batches, observation_deviation
    )
    prior_regions = prior_sample.reshape(anomaly_matrix, region_batches, pointwise_spread)
    prior_sample_full, integrate_dynamics = (
        lax.all_to_all(prior_regions, "member", split_axis=1, concat_axis=0, tiled=True),
        lax.all_to_all(propagated_grid, "member", split_axis=1, concat_axis=0, tiled=True),
    )
    integrate_dynamics = integrate_dynamics.reshape(sample_total, observation_deviation)
    rank = lax.axis_index("member")
    start = rank * observation_deviation
    my_value = lax.dynamic_slice_in_dim(measured_data.reshape(-1), start, observation_deviation)
    my_sigma = lax.dynamic_slice_in_dim(
        measurement_noise_sigma.reshape(-1), start, observation_deviation
    )
    slots = start + jnp.arange(observation_deviation, dtype=jnp.int32)
    valid = slots < measured_slots_used[0]
    weight = jnp.where(valid, 1.0 / my_sigma, jnp.zeros_like(my_sigma))
    sim_mean = jnp.mean(integrate_dynamics, axis=0)
    perturbed = (integrate_dynamics - sim_mean[None, :]) * weight[None, :]
    innovation = (my_value - sim_mean) * weight
    gram_loc = jnp.dot(perturbed, perturbed.T, precision=exact_arithmetic)
    cross_loc = jnp.dot(perturbed, innovation, precision=exact_arithmetic)
    gram_block, cross_block = lax.psum((gram_loc, cross_loc), "member")
    gram_all, cross = lax.psum((gram_block, cross_block), "space")
    cov_matrix = gram_all + (sample_total - 1) * jnp.eye(sample_total, dtype=jnp.float32)
    lower_factor = jnp.linalg.cholesky(cov_matrix)
    inverse = solve_lower(lower_factor, jnp.eye(sample_total, dtype=jnp.float32))
    projected = jnp.dot(inverse, cross, precision=exact_arithmetic)
    mean_weight = jnp.dot(inverse.T, projected, precision=exact_arithmetic)
    weight_matrix_update = math.sqrt(sample_total - 1) * inverse + mean_weight[None, :]
    sample_vectors = prior_sample_full.reshape(sample_total, -1)
    prior_average = jnp.mean(sample_vectors, axis=0)
    updated_sample = prior_average[None, :] + jnp.dot(
        weight_matrix_update, sample_vectors - prior_average[None, :], precision=exact_arithmetic
    )
    returned = lax.all_to_all(
        updated_sample.reshape(prior_sample_full.shape),
        "member",
        split_axis=0,
        concat_axis=1,
        tiled=True,
    )
    return returned.reshape(anomaly_matrix, points_in_region)


MESH = pl.DeviceIdType.MESH
VMEM_SPEC = pl.BlockSpec(memory_space=pltpu.VMEM)
LANES = 128
MIB = 1 << 20
SUBLANES = 8


def split2(x):
    high = x.astype(jnp.bfloat16)
    low = (x - high.astype(jnp.float32)).astype(jnp.bfloat16)
    return high, low


def dot3(a, b, dims=((1,), (0,))):
    ah, al = split2(a)
    bh, bl = split2(b)
    d = functools.partial(
        lax.dot_general, dimension_numbers=(dims, ((), ())), preferred_element_type=jnp.float32
    )
    return (d(ah, bl) + d(al, bh)) + d(ah, bh)


def flat_row(ref):
    return jnp.concatenate([ref[i : i + 1, :] for i in range(ref.shape[0])], axis=1)


PIVOTS = 4


def inverse_factor(a):
    size = a.shape[0]
    count = size // SUBLANES
    shape = (SUBLANES, size)
    m = [a[SUBLANES * i : SUBLANES * (i + 1), :] for i in range(count)]
    diag = [None] * count
    lane = lax.broadcasted_iota(jnp.int32, shape, 1)
    sub = lax.broadcasted_iota(jnp.int32, shape, 0)

    def column(x, k):
        return jnp.broadcast_to(x[:, k : k + 1], shape)

    def row(x, r):
        return jnp.broadcast_to(x[r : r + 1, :], shape)

    for k in range(0, size, PIVOTS):
        t, r = divmod(k, SUBLANES)
        inside = (lane >= k) & (lane < k + PIVOTS)
        cols = [column(m[t], k + q) for q in range(PIVOTS)]
        pivot = {(q, p): row(cols[p], r + q) for p in range(PIVOTS) for q in range(p, PIVOTS)}
        base = [
            jnp.where(inside, jnp.where(lane == k + q, 1.0, 0.0), row(m[t], r + q))
            for q in range(PIVOTS)
        ]
        inverse = []
        for p in range(PIVOTS):
            inverse.append(1.0 / pivot[p, p])
            for q in range(p + 1, PIVOTS):
                factor = pivot[q, p] * inverse[p]
                base[q] = base[q] - factor * base[p]
                for s in range(q, PIVOTS):
                    pivot[s, q] = pivot[s, q] - factor * pivot[s, p]
        for p in range(PIVOTS):
            old = diag[t]
            diag[t] = pivot[p, p] if old is None else jnp.where(sub >= r + p, pivot[p, p], old)
        for i in range(t, count):
            cols_i = cols if i == t else [column(m[i], k + q) for q in range(PIVOTS)]
            cols_i = list(cols_i)
            if i == t:
                unit = jnp.where(lane - k == sub - r, 1.0, 0.0)
                x = jnp.where(inside & (sub >= r), unit, m[i])
            else:
                x = jnp.where(inside, 0.0, m[i])
            for p in range(PIVOTS):
                mult = cols_i[p] * inverse[p]
                if i == t:
                    mult = jnp.where(sub > r + p, mult, 0.0)
                for q in range(p + 1, PIVOTS):
                    cols_i[q] = cols_i[q] - mult * pivot[q, p]
                x = x - mult * base[p]
            m[i] = x
    out = []
    for i in range(count):
        keep = lane <= sub + SUBLANES * i
        out.append(jnp.where(keep, m[i] * lax.rsqrt(diag[i]), 0.0))
    return jnp.concatenate(out, axis=0)


def eye_mask(rows, cols):
    shape = (rows, cols)
    return lax.broadcasted_iota(jnp.int32, shape, 0) == lax.broadcasted_iota(jnp.int32, shape, 1)


TILE = 512
CHUNKS = (512,) * 14
TAIL = (512, 256, 256)
EARLY = 6
READY = 13
LOADS = 2
GATHER = 1024


def offsets(widths):
    return [(sum(widths[:i]), w) for i, w in enumerate(widths)]


def gather_rows(x_ref, first, idx_ref, out_ref, rows, begin, end):
    shape = (SUBLANES, LANES)
    blocks = GATHER // LANES

    def step(t, _):
        for c in range(idx_ref.shape[0]):
            index = jnp.broadcast_to(idx_ref[c : c + 1, :], shape)
            lane = jnp.bitwise_and(index, LANES - 1)
            block = jnp.right_shift(index, LANES.bit_length() - 1) - t * blocks
            hits = [block == j for j in range(blocks)]
            columns = slice(c * LANES, (c + 1) * LANES)
            for g in range(0, rows, SUBLANES):
                place = pl.ds(pl.multiple_of(first + g, SUBLANES), SUBLANES)
                got = out_ref[place, columns]
                for j in range(blocks):
                    at = pl.ds(pl.multiple_of(t * GATHER + j * LANES, LANES), LANES)
                    x = x_ref[place, at]
                    got = jnp.where(hits[j], jnp.take_along_axis(x, lane, axis=1), got)
                out_ref[place, columns] = got
        return 0

    lax.fori_loop(begin // GATHER, end // GATHER, step, 0)


def transform_of(low_blocks, cross, t_ref, inv_ref, w_ref):
    samples = t_ref.shape[0]
    b = LANES
    ridge = float(samples - 1)
    n = samples // b
    work = {}
    for (i, j), block in low_blocks.items():
        work[i, j] = block + jnp.where(eye_mask(b, b), ridge, 0.0) if i == j else block
    inv = {}
    low = {}
    for k in range(n):
        inv[k, k] = inverse_factor(work[k, k])
        for i in range(k + 1, n):
            low[i, k] = dot3(work[i, k], inv[k, k], ((1,), (1,)))
        for i in range(k + 1, n):
            for j in range(k + 1, i + 1):
                work[i, j] = work[i, j] - dot3(low[i, k], low[j, k], ((1,), (1,)))
        for j in range(k):
            acc = dot3(low[k, j], inv[j, j])
            for m in range(j + 1, k):
                acc = acc + dot3(low[k, m], inv[m, j])
            inv[k, j] = -dot3(inv[k, k], acc)
    zero = jnp.zeros((b, b), jnp.float32)
    full = jnp.concatenate(
        [
            jnp.concatenate([inv[i, j] if j <= i else zero for j in range(n)], axis=1)
            for i in range(n)
        ],
        axis=0,
    )
    inv_ref[...] = full
    projected = jnp.sum(full * cross, axis=1, keepdims=True)
    mean_weight = jnp.sum(full * projected, axis=0, keepdims=True)
    w_ref[...] = jnp.broadcast_to(mean_weight, w_ref.shape)
    t_ref[...] = math.sqrt(samples - 1) * full + mean_weight


def own_weights(w_ref, core):
    half = w_ref.shape[1] // 2
    rows = half // 2
    w = w_ref[:, half:]
    return jnp.where(core == 0, w[:, :rows], w[:, rows:])


def split_dot(parts, x):
    th, stacked = parts
    rows = th.shape[0]
    xh, xl = split2(x)
    dot = functools.partial(jnp.dot, preferred_element_type=jnp.float32)
    both = dot(stacked, xh)
    return (both[rows:] + dot(th, xl)) + both[:rows]


def left_parts(t):
    th, tl = split2(t)
    return th, jnp.concatenate([th, tl], axis=0)


def filter_kernel(
    spaces,
    x_hbm,
    idx_hbm,
    data_hbm,
    sigma_hbm,
    used_ref,
    out_ref,
    idx_ref,
    data_ref,
    sigma_ref,
    xall,
    full,
    gram,
    cross,
    parts,
    cparts,
    total,
    t_ref,
    inv_ref,
    w_ref,
    sum_out,
    sum_in,
    mix_out,
    mix_in,
    y_out,
    y_in,
    ready,
    load,
    small,
    xs_send,
    xs_recv,
    fw_send,
    fw_recv,
    rs_send,
    rs_recv,
    cr_send,
    cr_recv,
    ag_send,
    ag_recv,
    pair_send,
    pair_recv,
    one_send,
    one_recv,
    y_send,
    y_recv,
):
    rank = lax.axis_index("member")
    place = lax.axis_index("space")
    core = lax.rem(rank, 2)
    lower = rank < 2
    upper = rank >= 2
    side = rank + 1 - 2 * core
    across = lax.rem(rank + 2, 4)
    diagonal = lax.rem(side + 2, 4)
    rows, points = x_hbm.shape
    samples, slots = full.shape
    half = samples // 2
    stripe = gram.shape[0]
    chunk = stripe // spaces
    peers = [lax.rem(place + d, spaces) for d in range(1, spaces)]
    chunks = offsets(CHUNKS)
    tails = offsets(TAIL)
    tail_first = sum(CHUNKS)
    last_tail = len(TAIL) - 1

    def rows_of(member):
        return pl.ds(pl.multiple_of(member * rows, SUBLANES), rows)

    def remote(src, dst, sems, i, member, space):
        return pltpu.make_async_remote_copy(
            src_ref=src,
            dst_ref=dst,
            send_sem=sems[0].at[i],
            recv_sem=sems[1].at[i],
            device_id={"member": member, "space": space},
            device_id_type=MESH,
        )

    own = rows_of(rank)
    xs, fw, rs = (xs_send, xs_recv), (fw_send, fw_recv), (rs_send, rs_recv)
    cr, ag, pair, one = (
        (cr_send, cr_recv),
        (ag_send, ag_recv),
        (pair_send, pair_recv),
        (one_send, one_recv),
    )

    def stream(i):
        first, width = chunks[i]
        columns = slice(first, first + width)
        return remote(xall.at[own, columns], xall.at[own, columns], xs, i, across, place)

    def arriving(i):
        first, width = chunks[i]
        columns = slice(first, first + width)
        here = xall.at[rows_of(across), columns]
        return remote(here, here, xs, i, across, place)

    def forward(i):
        first, width = chunks[i]
        columns = slice(first, first + width)
        here = xall.at[rows_of(across), columns]
        return remote(here, here, fw, i, side, place)

    def tail_copy(i, target, lane, sender):
        first, width = tails[i]
        columns = slice(first, first + width)
        return pltpu.make_async_remote_copy(
            src_ref=y_out.at[target, :, columns],
            dst_ref=y_in.at[:, columns],
            send_sem=y_send.at[sender],
            recv_sem=y_recv.at[i],
            device_id={"member": lane, "space": place},
            device_id_type=MESH,
        )

    def simple(ref, i, member, space=None):
        return remote(ref, ref, one, i, member, place if space is None else space)

    swap_x = simple(xall.at[own], 0, side)
    observed = simple(full.at[own], 1, across)
    observed_side = simple(full.at[own], 2, side)
    observed_far = simple(full.at[rows_of(across)], 3, side)
    swap_total = simple(total.at[core], 4, side)
    piece_rows = pl.ds(pl.multiple_of(place * chunk, SUBLANES), chunk)
    piece = total.at[core, piece_rows]
    cross_total = total.at[core, pl.ds(stripe, SUBLANES)]
    piece_far = simple(piece, 5, across)
    cross_far = simple(cross_total, 6, across)
    sums = [
        remote(sum_out, sum_in.at[core], pair, i, m, place) for i, m in ((0, across), (1, diagonal))
    ]
    mixes = [
        remote(mix_out, mix_in.at[core], pair, 2 + i, m, place)
        for i, m in ((0, across), (1, diagonal))
    ]
    spread = [remote(piece, piece, ag, d, rank, p) for d, p in enumerate(peers)]

    barrier = pltpu.get_barrier_semaphore()

    def greet(member, space):
        pl.semaphore_signal(
            barrier, inc=1, device_id={"member": member, "space": space}, device_id_type=MESH
        )

    @pl.when(upper)
    def _():
        greet(across, place)
        greet(side, place)
        for p in peers:
            greet(rank, p)

    @pl.when(lower)
    def _():
        greet(across, place)
        greet(diagonal, place)
        for p in peers:
            greet(across, p)

    def loading(t):
        columns = slice(t * part, (t + 1) * part)
        return pltpu.make_async_copy(x_hbm.at[:, columns], xall.at[own, columns], load.at[t])

    part = points // LOADS

    tables = [
        pltpu.make_async_copy(src, dst, small.at[i])
        for i, (src, dst) in enumerate(
            ((idx_hbm, idx_ref), (data_hbm, data_ref), (sigma_hbm, sigma_ref))
        )
    ]
    for copy in tables:
        copy.start()
    for t in range(LOADS):
        loading(t).start()
    full[own, :] = jnp.zeros((rows, slots), jnp.float32)

    @pl.when(lower)
    def _():
        pl.semaphore_wait(barrier, 1)

    loading(0).wait()

    @pl.when(lower)
    def _():
        for i in range(EARLY):
            stream(i).start()

    for copy in tables:
        copy.wait()
    gather_rows(xall, rank * rows, idx_ref, full, rows, 0, part)
    for t in range(1, LOADS):
        loading(t).wait()
        gather_rows(xall, rank * rows, idx_ref, full, rows, t * part, (t + 1) * part)

    @pl.when(upper)
    def _():
        pl.semaphore_wait(barrier, 2 * spaces + 1)
        pl.semaphore_signal(
            ready, inc=1, device_id={"member": across, "space": place}, device_id_type=MESH
        )
        observed.start()
        swap_x.start()
        sum_out[...] = jnp.sum(xall[own, :], axis=0, keepdims=True)
        for copy in sums:
            copy.start()
        for i in range(EARLY):
            arriving(i).wait_recv()
            forward(i).start()
        piece_far.wait_recv()
        cross_far.wait_recv()
        for copy in spread:
            copy.start()

    @pl.when(lower)
    def _():
        pl.semaphore_wait(ready, 1)
        observed_side.start()
        observed.wait_recv()
        observed_far.start()
        swap_x.start()
        observed_side.wait_recv()
        observed_far.wait_recv()
        slot = lax.broadcasted_iota(jnp.int32, (1, slots), 1)
        weight = jnp.where(slot < used_ref[0], 1.0 / flat_row(sigma_ref), 0.0)
        ev = full[...]
        mean = jnp.sum(ev, axis=0, keepdims=True) * (1.0 / samples)
        anomalies = (ev - mean) * weight
        innovation = (flat_row(data_ref) - mean) * weight
        first = lax.broadcasted_iota(jnp.int32, (SUBLANES, slots), 0) == 0
        extra = jnp.where(first, jnp.broadcast_to(innovation, (SUBLANES, slots)), 0.0)
        across_rows = ((1,), (1,))

        @pl.when(core == 0)
        def _():
            gram[...] = dot3(anomalies[:stripe], anomalies[:half], across_rows)
            cross[...] = dot3(extra, anomalies[:half], across_rows)

        @pl.when(core == 1)
        def _():
            top = samples - stripe
            gram[:top, :] = dot3(anomalies[stripe:], anomalies[:half], across_rows)
            gram[top:, :] = dot3(anomalies[half:], anomalies[half:], across_rows)
            cross[...] = dot3(extra, anomalies[half:], across_rows)

        scatter = [
            remote(
                gram.at[pl.ds(pl.multiple_of(p * chunk, SUBLANES), chunk)],
                parts.at[d],
                rs,
                d,
                rank,
                p,
            )
            for d, p in enumerate(peers)
        ]
        shared = [remote(cross, cparts.at[d], cr, d, rank, p) for d, p in enumerate(peers)]
        for a, b in zip(scatter, shared):
            a.start()
            b.start()
        acc = gram[piece_rows, :]
        acc_cross = cross[...]
        for d in range(spaces - 1):
            scatter[d].wait_recv()
            shared[d].wait_recv()
            acc = acc + parts[d]
            acc_cross = acc_cross + cparts[d]
        total[core, piece_rows, :] = acc
        total[core, stripe : stripe + SUBLANES, :] = acc_cross
        piece_far.start()
        cross_far.start()
        for copy in spread:
            copy.start()
        for i in range(EARLY, len(chunks)):
            stream(i).start()
        for copy in (*scatter, *shared):
            copy.wait_send()

    for copy in spread:
        copy.wait_recv()
    swap_total.start()
    swap_total.wait_recv()

    rest = stripe - half
    blocks = {
        (0, 0): total[0, :half, :],
        (1, 0): jnp.concatenate([total[0, half:stripe, :], total[1, : half - rest, :]], axis=0),
        (1, 1): total[1, half - rest : stripe, :],
    }
    cross_row = jnp.concatenate(
        [total[0, stripe : stripe + 1, :], total[1, stripe : stripe + 1, :]], axis=1
    )
    transform_of(blocks, cross_row, t_ref, inv_ref, w_ref)

    def tiles(first, last, body):
        def step(t, _):
            body(pl.ds(pl.multiple_of(t * TILE, LANES), TILE))
            return 0

        lax.fori_loop(first, last, step, 0)

    @pl.when(lower)
    def _():
        swap_x.wait_recv()
        for i in range(2):
            source = core if i == 0 else 1 - core
            remote(sum_out, sum_in.at[source], pair, i, across, place).wait_recv()

        def product(target, first, width):
            at = rows_of(target + 2)
            columns = slice(tail_first + first, tail_first + first + width)
            x = xall[:half, columns]
            mean = jnp.sum(x, axis=0, keepdims=True)
            mean = (mean + sum_in[0, :, columns] + sum_in[1, :, columns]) * (1.0 / samples)
            scale = 1.0 - jnp.sum(t_ref[at, half:], axis=1, keepdims=True)
            y = split_dot(left_parts(t_ref[at, :half]), x - mean)
            y_out[target, :, first : first + width] = y + scale * mean

        for i in range(last_tail):
            product(core, *tails[i])
            tail_copy(i, core, across, i).start()

        @pl.when(core == 1)
        def _():
            for target, lane, sender in ((1, 3, last_tail), (0, 2, last_tail + 1)):
                product(target, *tails[last_tail])
                tail_copy(last_tail, target, lane, sender).start()

        mine = left_parts(t_ref[own, :half])
        weight_sum = jnp.sum(w_ref[0:1, half:], axis=1, keepdims=True)
        for i in range(2):
            source = core if i == 0 else 1 - core
            remote(mix_out, mix_in.at[source], pair, 2 + i, across, place).wait_recv()

        def body(columns):
            x = xall[:half, columns]
            mean = jnp.sum(x, axis=0, keepdims=True)
            mean = (mean + sum_in[0, :, columns] + sum_in[1, :, columns]) * (1.0 / samples)
            other = mix_in[0, :, columns] + mix_in[1, :, columns] - weight_sum * mean
            out_ref[:, columns] = split_dot(mine, x - mean) + (mean + other)

        tiles(0, points // TILE, body)
        for i in range(len(chunks)):
            stream(i).wait_send()
        observed_side.wait_send()
        observed_far.wait_send()
        piece_far.wait_send()
        cross_far.wait_send()
        for i in range(last_tail):
            tail_copy(i, core, across, i).wait_send()

        @pl.when(core == 1)
        def _():
            for target, lane, sender in ((1, 3, last_tail), (0, 2, last_tail + 1)):
                tail_copy(last_tail, target, lane, sender).wait_send()

    @pl.when(upper)
    def _():
        mix = dot3(own_weights(w_ref, core), xall[own, :])
        mix_out[...] = mix[0:1, :]
        for copy in mixes:
            copy.start()
        mine = left_parts(t_ref[own, :])
        swap_x.wait_recv()

        def body(columns):
            x = xall[:, columns]
            mean = jnp.sum(x, axis=0, keepdims=True) * (1.0 / samples)
            out_ref[:, columns] = split_dot(mine, x - mean) + mean

        for i in range(EARLY, READY):
            arriving(i).wait_recv()
            forward(i).start()
        for i in range(EARLY):
            forward(i).wait_recv()
        tiles(0, EARLY, body)
        for i in range(EARLY, READY):
            forward(i).wait_recv()
        tiles(EARLY, READY, body)
        near = left_parts(t_ref[own, half:])

        def local(columns):
            out_ref[:, columns] = split_dot(near, xall[half:, columns])

        for i in range(READY, len(chunks)):
            arriving(i).wait_recv()
            forward(i).start()
        tiles(tail_first // TILE, points // TILE, local)
        for i in range(READY, len(chunks)):
            forward(i).wait_recv()
        tiles(READY, len(chunks), body)
        for i in range(len(tails)):
            first, width = tails[i]
            tail_copy(i, core, across, i).wait_recv()
            columns = slice(tail_first + first, tail_first + first + width)
            out_ref[:, columns] = out_ref[:, columns] + y_in[:, first : first + width]
        for i in range(len(chunks)):
            forward(i).wait_send()
        observed.wait_send()
        for copy in (*sums, *mixes):
            copy.wait_send()

    swap_x.wait_send()
    swap_total.wait_send()
    for copy in spread:
        copy.wait_send()


def filtered(prior, index, data, sigma, used, spaces):
    rows, points = prior.shape
    slots = index.size
    samples = 4 * rows
    half = samples // 2
    stripe = 3 * half // 2
    f32 = jnp.float32
    dma = pltpu.SemaphoreType.DMA
    vmem = pltpu.VMEM
    chunk = stripe // spaces
    others = (spaces - 1,)
    pieces = (len(CHUNKS),)
    return pl.pallas_call(
        functools.partial(filter_kernel, spaces),
        out_shape=jax.ShapeDtypeStruct((rows, points), f32),
        in_specs=[pl.BlockSpec(memory_space=pltpu.HBM)] * 4
        + [pl.BlockSpec(memory_space=pltpu.SMEM)],
        out_specs=VMEM_SPEC,
        scratch_shapes=[
            vmem(index.shape, jnp.int32),
            vmem(data.shape, f32),
            vmem(sigma.shape, f32),
            vmem((samples, points), f32),
            vmem((samples, slots), f32),
            vmem((stripe, half), f32),
            vmem((SUBLANES, half), f32),
            vmem((spaces - 1, chunk, half), f32),
            vmem((spaces - 1, SUBLANES, half), f32),
            vmem((2, stripe + SUBLANES, half), f32),
            vmem((samples, samples), f32),
            vmem((samples, samples), f32),
            vmem((SUBLANES, samples), f32),
            vmem((1, points), f32),
            vmem((2, 1, points), f32),
            vmem((1, points), f32),
            vmem((2, 1, points), f32),
            vmem((2, rows, sum(TAIL)), f32),
            vmem((rows, sum(TAIL)), f32),
            pltpu.SemaphoreType.REGULAR,
            dma((LOADS,)),
            dma((3,)),
            dma(pieces),
            dma(pieces),
            dma(pieces),
            dma(pieces),
            dma(others),
            dma(others),
            dma(others),
            dma(others),
            dma(others),
            dma(others),
            dma((4,)),
            dma((4,)),
            dma((7,)),
            dma((7,)),
            dma((len(TAIL) + 1,)),
            dma((len(TAIL),)),
        ],
        compiler_params=pltpu.CompilerParams(
            collective_id=0, has_side_effects=True, vmem_limit_bytes=32 * MIB
        ),
    )(prior, index, data, sigma, used)


def body(*arrays):
    prior_sample, location = arrays[:2]
    rows, points = prior_sample.shape
    members, spaces = lax.axis_size("member"), lax.axis_size("space")
    if (
        members != 4
        or rows * members != 2 * LANES
        or 3 * LANES // 2 % (SUBLANES * spaces)
        or points != sum(CHUNKS) + sum(TAIL)
        or location.shape[1] != LANES
    ):
        return general_body(*arrays)
    held = [pltpu.with_memory_space_constraint(a, pltpu.HBM) for a in arrays[:4]]
    return filtered(*held, arrays[4], spaces)


def solution(mesh):
    placed = (
        P("member", "space"),
        P("space", None),
        P("space", None),
        P("space", None),
        P("space"),
    )
    return jax.shard_map(
        body, mesh=mesh, in_specs=placed, out_specs=P("member", "space"), check_vma=False
    )
```

```python
import functools
import math

import jax
import jax.numpy as jnp
from jax import lax
from jax.experimental import pallas as pl
from jax.experimental.pallas import tpu as pltpu
from jax.sharding import PartitionSpec as P


def solve_lower(lower_factor, target):
    return lax.linalg.triangular_solve(lower_factor, target, left_side=True, lower=True)


def general_body(
    prior_sample,
    measured_point_location,
    measured_data,
    measurement_noise_sigma,
    measured_slots_used,
):
    exact_arithmetic = lax.Precision.HIGHEST
    anomaly_matrix, points_in_region = prior_sample.shape
    region_batches = lax.axis_size("member")
    sample_total = anomaly_matrix * region_batches
    pointwise_spread = points_in_region // region_batches
    linear_position = measured_point_location.reshape(-1)
    obs_blk = linear_position.shape[0]
    observation_deviation = obs_blk // region_batches
    propagated_grid = jnp.take(prior_sample, linear_position, axis=1).reshape(
        anomaly_matrix, region_batches, observation_deviation
    )
    prior_regions = prior_sample.reshape(anomaly_matrix, region_batches, pointwise_spread)
    prior_sample_full, integrate_dynamics = (
        lax.all_to_all(prior_regions, "member", split_axis=1, concat_axis=0, tiled=True),
        lax.all_to_all(propagated_grid, "member", split_axis=1, concat_axis=0, tiled=True),
    )
    integrate_dynamics = integrate_dynamics.reshape(sample_total, observation_deviation)
    rank = lax.axis_index("member")
    start = rank * observation_deviation
    my_value = lax.dynamic_slice_in_dim(measured_data.reshape(-1), start, observation_deviation)
    my_sigma = lax.dynamic_slice_in_dim(
        measurement_noise_sigma.reshape(-1), start, observation_deviation
    )
    slots = start + jnp.arange(observation_deviation, dtype=jnp.int32)
    valid = slots < measured_slots_used[0]
    weight = jnp.where(valid, 1.0 / my_sigma, jnp.zeros_like(my_sigma))
    sim_mean = jnp.mean(integrate_dynamics, axis=0)
    perturbed = (integrate_dynamics - sim_mean[None, :]) * weight[None, :]
    innovation = (my_value - sim_mean) * weight
    gram_loc = jnp.dot(perturbed, perturbed.T, precision=exact_arithmetic)
    cross_loc = jnp.dot(perturbed, innovation, precision=exact_arithmetic)
    gram_block, cross_block = lax.psum((gram_loc, cross_loc), "member")
    gram_all, cross = lax.psum((gram_block, cross_block), "space")
    cov_matrix = gram_all + (sample_total - 1) * jnp.eye(sample_total, dtype=jnp.float32)
    lower_factor = jnp.linalg.cholesky(cov_matrix)
    inverse = solve_lower(lower_factor, jnp.eye(sample_total, dtype=jnp.float32))
    projected = jnp.dot(inverse, cross, precision=exact_arithmetic)
    mean_weight = jnp.dot(inverse.T, projected, precision=exact_arithmetic)
    weight_matrix_update = math.sqrt(sample_total - 1) * inverse + mean_weight[None, :]
    sample_vectors = prior_sample_full.reshape(sample_total, -1)
    prior_average = jnp.mean(sample_vectors, axis=0)
    updated_sample = prior_average[None, :] + jnp.dot(
        weight_matrix_update, sample_vectors - prior_average[None, :], precision=exact_arithmetic
    )
    returned = lax.all_to_all(
        updated_sample.reshape(prior_sample_full.shape),
        "member",
        split_axis=0,
        concat_axis=1,
        tiled=True,
    )
    return returned.reshape(anomaly_matrix, points_in_region)


MESH = pl.DeviceIdType.MESH
VMEM_SPEC = pl.BlockSpec(memory_space=pltpu.VMEM)
LANES = 128
MIB = 1 << 20
SUBLANES = 8


def split2(x):
    high = x.astype(jnp.bfloat16)
    low = (x - high.astype(jnp.float32)).astype(jnp.bfloat16)
    return high, low


def dot3(a, b, dims=((1,), (0,))):
    ah, al = split2(a)
    bh, bl = split2(b)
    d = functools.partial(
        lax.dot_general, dimension_numbers=(dims, ((), ())), preferred_element_type=jnp.float32
    )
    return (d(ah, bl) + d(al, bh)) + d(ah, bh)


def flat_row(ref):
    return jnp.concatenate([ref[i : i + 1, :] for i in range(ref.shape[0])], axis=1)


PIVOTS = 4


def inverse_factor(a):
    size = a.shape[0]
    count = size // SUBLANES
    shape = (SUBLANES, size)
    m = [a[SUBLANES * i : SUBLANES * (i + 1), :] for i in range(count)]
    diag = [None] * count
    lane = lax.broadcasted_iota(jnp.int32, shape, 1)
    sub = lax.broadcasted_iota(jnp.int32, shape, 0)

    def column(x, k):
        return jnp.broadcast_to(x[:, k : k + 1], shape)

    def row(x, r):
        return jnp.broadcast_to(x[r : r + 1, :], shape)

    for k in range(0, size, PIVOTS):
        t, r = divmod(k, SUBLANES)
        inside = (lane >= k) & (lane < k + PIVOTS)
        cols = [column(m[t], k + q) for q in range(PIVOTS)]
        pivot = {(q, p): row(cols[p], r + q) for p in range(PIVOTS) for q in range(p, PIVOTS)}
        base = [
            jnp.where(inside, jnp.where(lane == k + q, 1.0, 0.0), row(m[t], r + q))
            for q in range(PIVOTS)
        ]
        inverse = []
        for p in range(PIVOTS):
            inverse.append(1.0 / pivot[p, p])
            for q in range(p + 1, PIVOTS):
                factor = pivot[q, p] * inverse[p]
                base[q] = base[q] - factor * base[p]
                for s in range(q, PIVOTS):
                    pivot[s, q] = pivot[s, q] - factor * pivot[s, p]
        for p in range(PIVOTS):
            old = diag[t]
            diag[t] = pivot[p, p] if old is None else jnp.where(sub >= r + p, pivot[p, p], old)
        for i in range(t, count):
            cols_i = cols if i == t else [column(m[i], k + q) for q in range(PIVOTS)]
            cols_i = list(cols_i)
            if i == t:
                unit = jnp.where(lane - k == sub - r, 1.0, 0.0)
                x = jnp.where(inside & (sub >= r), unit, m[i])
            else:
                x = jnp.where(inside, 0.0, m[i])
            for p in range(PIVOTS):
                mult = cols_i[p] * inverse[p]
                if i == t:
                    mult = jnp.where(sub > r + p, mult, 0.0)
                for q in range(p + 1, PIVOTS):
                    cols_i[q] = cols_i[q] - mult * pivot[q, p]
                x = x - mult * base[p]
            m[i] = x
    out = []
    for i in range(count):
        keep = lane <= sub + SUBLANES * i
        out.append(jnp.where(keep, m[i] * lax.rsqrt(diag[i]), 0.0))
    return jnp.concatenate(out, axis=0)


def eye_mask(rows, cols):
    shape = (rows, cols)
    return lax.broadcasted_iota(jnp.int32, shape, 0) == lax.broadcasted_iota(jnp.int32, shape, 1)


TILE = 512
CHUNKS = (512,) * 14
TAIL = (512, 256, 256)
EARLY = 6
READY = 13
LOADS = 2
GATHER = 1024


def offsets(widths):
    return [(sum(widths[:i]), w) for i, w in enumerate(widths)]


def gather_rows(x_ref, first, idx_ref, out_ref, rows, begin, end):
    shape = (SUBLANES, LANES)
    blocks = GATHER // LANES

    def step(t, _):
        for c in range(idx_ref.shape[0]):
            index = jnp.broadcast_to(idx_ref[c : c + 1, :], shape)
            lane = jnp.bitwise_and(index, LANES - 1)
            block = jnp.right_shift(index, LANES.bit_length() - 1) - t * blocks
            hits = [block == j for j in range(blocks)]
            columns = slice(c * LANES, (c + 1) * LANES)
            for g in range(0, rows, SUBLANES):
                place = pl.ds(pl.multiple_of(first + g, SUBLANES), SUBLANES)
                got = out_ref[place, columns]
                for j in range(blocks):
                    at = pl.ds(pl.multiple_of(t * GATHER + j * LANES, LANES), LANES)
                    x = x_ref[place, at]
                    got = jnp.where(hits[j], jnp.take_along_axis(x, lane, axis=1), got)
                out_ref[place, columns] = got
        return 0

    lax.fori_loop(begin // GATHER, end // GATHER, step, 0)


def transform_of(low_blocks, cross, t_ref, inv_ref, w_ref):
    samples = t_ref.shape[0]
    b = LANES
    ridge = float(samples - 1)
    n = samples // b
    work = {}
    for (i, j), block in low_blocks.items():
        work[i, j] = block + jnp.where(eye_mask(b, b), ridge, 0.0) if i == j else block
    inv = {}
    low = {}
    for k in range(n):
        inv[k, k] = inverse_factor(work[k, k])
        for i in range(k + 1, n):
            low[i, k] = dot3(work[i, k], inv[k, k], ((1,), (1,)))
        for i in range(k + 1, n):
            for j in range(k + 1, i + 1):
                work[i, j] = work[i, j] - dot3(low[i, k], low[j, k], ((1,), (1,)))
        for j in range(k):
            acc = dot3(low[k, j], inv[j, j])
            for m in range(j + 1, k):
                acc = acc + dot3(low[k, m], inv[m, j])
            inv[k, j] = -dot3(inv[k, k], acc)
    zero = jnp.zeros((b, b), jnp.float32)
    full = jnp.concatenate(
        [
            jnp.concatenate([inv[i, j] if j <= i else zero for j in range(n)], axis=1)
            for i in range(n)
        ],
        axis=0,
    )
    inv_ref[...] = full
    projected = jnp.sum(full * cross, axis=1, keepdims=True)
    mean_weight = jnp.sum(full * projected, axis=0, keepdims=True)
    w_ref[...] = jnp.broadcast_to(mean_weight, w_ref.shape)
    t_ref[...] = math.sqrt(samples - 1) * full + mean_weight


def own_weights(w_ref, core):
    half = w_ref.shape[1] // 2
    rows = half // 2
    w = w_ref[:, half:]
    return jnp.where(core == 0, w[:, :rows], w[:, rows:])


def split_dot(parts, x):
    th, stacked = parts
    rows = th.shape[0]
    xh, xl = split2(x)
    dot = functools.partial(jnp.dot, preferred_element_type=jnp.float32)
    both = dot(stacked, xh)
    return (both[rows:] + dot(th, xl)) + both[:rows]


def left_parts(t):
    th, tl = split2(t)
    return th, jnp.concatenate([th, tl], axis=0)


def filter_kernel(
    spaces,
    x_hbm,
    idx_hbm,
    data_hbm,
    sigma_hbm,
    used_ref,
    out_ref,
    idx_ref,
    data_ref,
    sigma_ref,
    xall,
    full,
    gram,
    cross,
    parts,
    cparts,
    total,
    t_ref,
    inv_ref,
    w_ref,
    sum_out,
    sum_in,
    mix_out,
    mix_in,
    y_out,
    y_in,
    ready,
    load,
    small,
    xs_send,
    xs_recv,
    fw_send,
    fw_recv,
    rs_send,
    rs_recv,
    cr_send,
    cr_recv,
    ag_send,
    ag_recv,
    pair_send,
    pair_recv,
    one_send,
    one_recv,
    y_send,
    y_recv,
):
    rank = lax.axis_index("member")
    place = lax.axis_index("space")
    core = lax.rem(rank, 2)
    lower = rank < 2
    upper = rank >= 2
    side = rank + 1 - 2 * core
    across = lax.rem(rank + 2, 4)
    diagonal = lax.rem(side + 2, 4)
    rows, points = x_hbm.shape
    samples, slots = full.shape
    half = samples // 2
    stripe = gram.shape[0]
    chunk = stripe // spaces
    peers = [lax.rem(place + d, spaces) for d in range(1, spaces)]
    chunks = offsets(CHUNKS)
    tails = offsets(TAIL)
    tail_first = sum(CHUNKS)
    last_tail = len(TAIL) - 1

    def rows_of(member):
        return pl.ds(pl.multiple_of(member * rows, SUBLANES), rows)

    def remote(src, dst, sems, i, member, space):
        return pltpu.make_async_remote_copy(
            src_ref=src,
            dst_ref=dst,
            send_sem=sems[0].at[i],
            recv_sem=sems[1].at[i],
            device_id={"member": member, "space": space},
            device_id_type=MESH,
        )

    own = rows_of(rank)
    xs, fw, rs = (xs_send, xs_recv), (fw_send, fw_recv), (rs_send, rs_recv)
    cr, ag, pair, one = (
        (cr_send, cr_recv),
        (ag_send, ag_recv),
        (pair_send, pair_recv),
        (one_send, one_recv),
    )

    def stream(i):
        first, width = chunks[i]
        columns = slice(first, first + width)
        return remote(xall.at[own, columns], xall.at[own, columns], xs, i, across, place)

    def arriving(i):
        first, width = chunks[i]
        columns = slice(first, first + width)
        here = xall.at[rows_of(across), columns]
        return remote(here, here, xs, i, across, place)

    def forward(i):
        first, width = chunks[i]
        columns = slice(first, first + width)
        here = xall.at[rows_of(across), columns]
        return remote(here, here, fw, i, side, place)

    def tail_copy(i, target, lane, sender):
        first, width = tails[i]
        columns = slice(first, first + width)
        return pltpu.make_async_remote_copy(
            src_ref=y_out.at[target, :, columns],
            dst_ref=y_in.at[:, columns],
            send_sem=y_send.at[sender],
            recv_sem=y_recv.at[i],
            device_id={"member": lane, "space": place},
            device_id_type=MESH,
        )

    def simple(ref, i, member, space=None):
        return remote(ref, ref, one, i, member, place if space is None else space)

    swap_x = simple(xall.at[own], 0, side)
    observed = simple(full.at[own], 1, across)
    observed_side = simple(full.at[own], 2, side)
    observed_far = simple(full.at[rows_of(across)], 3, side)
    swap_total = simple(total.at[core], 4, side)
    piece_rows = pl.ds(pl.multiple_of(place * chunk, SUBLANES), chunk)
    piece = total.at[core, piece_rows]
    cross_total = total.at[core, pl.ds(stripe, SUBLANES)]
    piece_far = simple(piece, 5, across)
    cross_far = simple(cross_total, 6, across)
    sums = [
        remote(sum_out, sum_in.at[core], pair, i, m, place) for i, m in ((0, across), (1, diagonal))
    ]
    mixes = [
        remote(mix_out, mix_in.at[core], pair, 2 + i, m, place)
        for i, m in ((0, across), (1, diagonal))
    ]
    spread = [remote(piece, piece, ag, d, rank, p) for d, p in enumerate(peers)]

    barrier = pltpu.get_barrier_semaphore()

    def greet(member, space):
        pl.semaphore_signal(
            barrier, inc=1, device_id={"member": member, "space": space}, device_id_type=MESH
        )

    @pl.when(upper)
    def _():
        greet(across, place)
        greet(side, place)
        for p in peers:
            greet(rank, p)

    @pl.when(lower)
    def _():
        greet(across, place)
        greet(diagonal, place)
        for p in peers:
            greet(across, p)

    def loading(t):
        columns = slice(t * part, (t + 1) * part)
        return pltpu.make_async_copy(x_hbm.at[:, columns], xall.at[own, columns], load.at[t])

    part = points // LOADS

    tables = [
        pltpu.make_async_copy(src, dst, small.at[i])
        for i, (src, dst) in enumerate(
            ((idx_hbm, idx_ref), (data_hbm, data_ref), (sigma_hbm, sigma_ref))
        )
    ]
    for copy in tables:
        copy.start()
    for t in range(LOADS):
        loading(t).start()
    full[own, :] = jnp.zeros((rows, slots), jnp.float32)

    @pl.when(lower)
    def _():
        pl.semaphore_wait(barrier, 1)

    loading(0).wait()

    @pl.when(lower)
    def _():
        for i in range(EARLY):
            stream(i).start()

    for copy in tables:
        copy.wait()
    gather_rows(xall, rank * rows, idx_ref, full, rows, 0, part)
    for t in range(1, LOADS):
        loading(t).wait()
        gather_rows(xall, rank * rows, idx_ref, full, rows, t * part, (t + 1) * part)

    @pl.when(upper)
    def _():
        pl.semaphore_wait(barrier, 2 * spaces + 1)
        pl.semaphore_signal(
            ready, inc=1, device_id={"member": across, "space": place}, device_id_type=MESH
        )
        observed.start()
        swap_x.start()
        sum_out[...] = jnp.sum(xall[own, :], axis=0, keepdims=True)
        for copy in sums:
            copy.start()
        for i in range(EARLY):
            arriving(i).wait_recv()
            forward(i).start()
        piece_far.wait_recv()
        cross_far.wait_recv()
        for copy in spread:
            copy.start()

    @pl.when(lower)
    def _():
        pl.semaphore_wait(ready, 1)
        observed_side.start()
        observed.wait_recv()
        observed_far.start()
        swap_x.start()
        observed_side.wait_recv()
        observed_far.wait_recv()
        slot = lax.broadcasted_iota(jnp.int32, (1, slots), 1)
        weight = jnp.where(slot < used_ref[0], 1.0 / flat_row(sigma_ref), 0.0)
        ev = full[...]
        mean = jnp.sum(ev, axis=0, keepdims=True) * (1.0 / samples)
        anomalies = (ev - mean) * weight
        innovation = (flat_row(data_ref) - mean) * weight
        first = lax.broadcasted_iota(jnp.int32, (SUBLANES, slots), 0) == 0
        extra = jnp.where(first, jnp.broadcast_to(innovation, (SUBLANES, slots)), 0.0)
        across_rows = ((1,), (1,))

        @pl.when(core == 0)
        def _():
            gram[...] = dot3(anomalies[:stripe], anomalies[:half], across_rows)
            cross[...] = dot3(extra, anomalies[:half], across_rows)

        @pl.when(core == 1)
        def _():
            top = samples - stripe
            gram[:top, :] = dot3(anomalies[stripe:], anomalies[:half], across_rows)
            gram[top:, :] = dot3(anomalies[half:], anomalies[half:], across_rows)
            cross[...] = dot3(extra, anomalies[half:], across_rows)

        scatter = [
            remote(
                gram.at[pl.ds(pl.multiple_of(p * chunk, SUBLANES), chunk)],
                parts.at[d],
                rs,
                d,
                rank,
                p,
            )
            for d, p in enumerate(peers)
        ]
        shared = [remote(cross, cparts.at[d], cr, d, rank, p) for d, p in enumerate(peers)]
        for a, b in zip(scatter, shared):
            a.start()
            b.start()
        acc = gram[piece_rows, :]
        acc_cross = cross[...]
        for d in range(spaces - 1):
            scatter[d].wait_recv()
            shared[d].wait_recv()
            acc = acc + parts[d]
            acc_cross = acc_cross + cparts[d]
        total[core, piece_rows, :] = acc
        total[core, stripe : stripe + SUBLANES, :] = acc_cross
        piece_far.start()
        cross_far.start()
        for copy in spread:
            copy.start()
        for i in range(EARLY, len(chunks)):
            stream(i).start()
        for copy in (*scatter, *shared):
            copy.wait_send()

    for copy in spread:
        copy.wait_recv()
    swap_total.start()
    swap_total.wait_recv()

    rest = stripe - half
    blocks = {
        (0, 0): total[0, :half, :],
        (1, 0): jnp.concatenate([total[0, half:stripe, :], total[1, : half - rest, :]], axis=0),
        (1, 1): total[1, half - rest : stripe, :],
    }
    cross_row = jnp.concatenate(
        [total[0, stripe : stripe + 1, :], total[1, stripe : stripe + 1, :]], axis=1
    )
    transform_of(blocks, cross_row, t_ref, inv_ref, w_ref)

    def tiles(first, last, body):
        def step(t, _):
            body(pl.ds(pl.multiple_of(t * TILE, LANES), TILE))
            return 0

        lax.fori_loop(first, last, step, 0)

    @pl.when(lower)
    def _():
        swap_x.wait_recv()
        for i in range(2):
            source = core if i == 0 else 1 - core
            remote(sum_out, sum_in.at[source], pair, i, across, place).wait_recv()

        def product(target, first, width):
            at = rows_of(target + 2)
            columns = slice(tail_first + first, tail_first + first + width)
            x = xall[:half, columns]
            mean = jnp.sum(x, axis=0, keepdims=True)
            mean = (mean + sum_in[0, :, columns] + sum_in[1, :, columns]) * (1.0 / samples)
            scale = 1.0 - jnp.sum(t_ref[at, half:], axis=1, keepdims=True)
            y = split_dot(left_parts(t_ref[at, :half]), x - mean)
            y_out[target, :, first : first + width] = y + scale * mean

        for i in range(last_tail):
            product(core, *tails[i])
            tail_copy(i, core, across, i).start()

        @pl.when(core == 1)
        def _():
            for target, lane, sender in ((1, 3, last_tail), (0, 2, last_tail + 1)):
                product(target, *tails[last_tail])
                tail_copy(last_tail, target, lane, sender).start()

        mine = left_parts(t_ref[own, :half])
        weight_sum = jnp.sum(w_ref[0:1, half:], axis=1, keepdims=True)

        def body(columns):
            x = xall[:half, columns]
            mean = jnp.sum(x, axis=0, keepdims=True)
            mean = (mean + sum_in[0, :, columns] + sum_in[1, :, columns]) * (1.0 / samples)
            out_ref[:, columns] = split_dot(mine, x - mean) + (1.0 - weight_sum) * mean

        tiles(0, points // TILE, body)
        for i in range(2):
            source = core if i == 0 else 1 - core
            remote(mix_out, mix_in.at[source], pair, 2 + i, across, place).wait_recv()

        def mixed(columns):
            other = mix_in[0, :, columns] + mix_in[1, :, columns]
            out_ref[:, columns] = out_ref[:, columns] + other

        tiles(0, points // TILE, mixed)
        for i in range(len(chunks)):
            stream(i).wait_send()
        observed_side.wait_send()
        observed_far.wait_send()
        piece_far.wait_send()
        cross_far.wait_send()
        for i in range(last_tail):
            tail_copy(i, core, across, i).wait_send()

        @pl.when(core == 1)
        def _():
            for target, lane, sender in ((1, 3, last_tail), (0, 2, last_tail + 1)):
                tail_copy(last_tail, target, lane, sender).wait_send()

    @pl.when(upper)
    def _():
        mix = dot3(own_weights(w_ref, core), xall[own, :])
        mix_out[...] = mix[0:1, :]
        for copy in mixes:
            copy.start()
        mine = left_parts(t_ref[own, :])
        swap_x.wait_recv()

        def body(columns):
            x = xall[:, columns]
            mean = jnp.sum(x, axis=0, keepdims=True) * (1.0 / samples)
            out_ref[:, columns] = split_dot(mine, x - mean) + mean

        for i in range(EARLY, READY):
            arriving(i).wait_recv()
            forward(i).start()
        for i in range(EARLY):
            forward(i).wait_recv()
        tiles(0, EARLY, body)
        for i in range(EARLY, READY):
            forward(i).wait_recv()
        tiles(EARLY, READY, body)
        near = left_parts(t_ref[own, half:])

        def local(columns):
            out_ref[:, columns] = split_dot(near, xall[half:, columns])

        for i in range(READY, len(chunks)):
            arriving(i).wait_recv()
            forward(i).start()
        tiles(tail_first // TILE, points // TILE, local)
        for i in range(READY, len(chunks)):
            forward(i).wait_recv()
        tiles(READY, len(chunks), body)
        for i in range(len(tails)):
            first, width = tails[i]
            tail_copy(i, core, across, i).wait_recv()
            columns = slice(tail_first + first, tail_first + first + width)
            out_ref[:, columns] = out_ref[:, columns] + y_in[:, first : first + width]
        for i in range(len(chunks)):
            forward(i).wait_send()
        observed.wait_send()
        for copy in (*sums, *mixes):
            copy.wait_send()

    swap_x.wait_send()
    swap_total.wait_send()
    for copy in spread:
        copy.wait_send()


def filtered(prior, index, data, sigma, used, spaces):
    rows, points = prior.shape
    slots = index.size
    samples = 4 * rows
    half = samples // 2
    stripe = 3 * half // 2
    f32 = jnp.float32
    dma = pltpu.SemaphoreType.DMA
    vmem = pltpu.VMEM
    chunk = stripe // spaces
    others = (spaces - 1,)
    pieces = (len(CHUNKS),)
    return pl.pallas_call(
        functools.partial(filter_kernel, spaces),
        out_shape=jax.ShapeDtypeStruct((rows, points), f32),
        in_specs=[pl.BlockSpec(memory_space=pltpu.HBM)] * 4
        + [pl.BlockSpec(memory_space=pltpu.SMEM)],
        out_specs=VMEM_SPEC,
        scratch_shapes=[
            vmem(index.shape, jnp.int32),
            vmem(data.shape, f32),
            vmem(sigma.shape, f32),
            vmem((samples, points), f32),
            vmem((samples, slots), f32),
            vmem((stripe, half), f32),
            vmem((SUBLANES, half), f32),
            vmem((spaces - 1, chunk, half), f32),
            vmem((spaces - 1, SUBLANES, half), f32),
            vmem((2, stripe + SUBLANES, half), f32),
            vmem((samples, samples), f32),
            vmem((samples, samples), f32),
            vmem((SUBLANES, samples), f32),
            vmem((1, points), f32),
            vmem((2, 1, points), f32),
            vmem((1, points), f32),
            vmem((2, 1, points), f32),
            vmem((2, rows, sum(TAIL)), f32),
            vmem((rows, sum(TAIL)), f32),
            pltpu.SemaphoreType.REGULAR,
            dma((LOADS,)),
            dma((3,)),
            dma(pieces),
            dma(pieces),
            dma(pieces),
            dma(pieces),
            dma(others),
            dma(others),
            dma(others),
            dma(others),
            dma(others),
            dma(others),
            dma((4,)),
            dma((4,)),
            dma((7,)),
            dma((7,)),
            dma((len(TAIL) + 1,)),
            dma((len(TAIL),)),
        ],
        compiler_params=pltpu.CompilerParams(
            collective_id=0, has_side_effects=True, vmem_limit_bytes=32 * MIB
        ),
    )(prior, index, data, sigma, used)


def body(*arrays):
    prior_sample, location = arrays[:2]
    rows, points = prior_sample.shape
    members, spaces = lax.axis_size("member"), lax.axis_size("space")
    if (
        members != 4
        or rows * members != 2 * LANES
        or 3 * LANES // 2 % (SUBLANES * spaces)
        or points != sum(CHUNKS) + sum(TAIL)
        or location.shape[1] != LANES
    ):
        return general_body(*arrays)
    held = [pltpu.with_memory_space_constraint(a, pltpu.HBM) for a in arrays[:4]]
    return filtered(*held, arrays[4], spaces)


def solution(mesh):
    placed = (
        P("member", "space"),
        P("space", None),
        P("space", None),
        P("space", None),
        P("space"),
    )
    return jax.shard_map(
        body, mesh=mesh, in_specs=placed, out_specs=P("member", "space"), check_vma=False
    )
```

```python
import functools
import math

import jax
import jax.numpy as jnp
from jax import lax
from jax.experimental import pallas as pl
from jax.experimental.pallas import tpu as pltpu
from jax.sharding import PartitionSpec as P


def solve_lower(lower_factor, target):
    return lax.linalg.triangular_solve(lower_factor, target, left_side=True, lower=True)


def general_body(
    prior_sample,
    measured_point_location,
    measured_data,
    measurement_noise_sigma,
    measured_slots_used,
):
    exact_arithmetic = lax.Precision.HIGHEST
    anomaly_matrix, points_in_region = prior_sample.shape
    region_batches = lax.axis_size("member")
    sample_total = anomaly_matrix * region_batches
    pointwise_spread = points_in_region // region_batches
    linear_position = measured_point_location.reshape(-1)
    obs_blk = linear_position.shape[0]
    observation_deviation = obs_blk // region_batches
    propagated_grid = jnp.take(prior_sample, linear_position, axis=1).reshape(
        anomaly_matrix, region_batches, observation_deviation
    )
    prior_regions = prior_sample.reshape(anomaly_matrix, region_batches, pointwise_spread)
    prior_sample_full, integrate_dynamics = (
        lax.all_to_all(prior_regions, "member", split_axis=1, concat_axis=0, tiled=True),
        lax.all_to_all(propagated_grid, "member", split_axis=1, concat_axis=0, tiled=True),
    )
    integrate_dynamics = integrate_dynamics.reshape(sample_total, observation_deviation)
    rank = lax.axis_index("member")
    start = rank * observation_deviation
    my_value = lax.dynamic_slice_in_dim(measured_data.reshape(-1), start, observation_deviation)
    my_sigma = lax.dynamic_slice_in_dim(
        measurement_noise_sigma.reshape(-1), start, observation_deviation
    )
    slots = start + jnp.arange(observation_deviation, dtype=jnp.int32)
    valid = slots < measured_slots_used[0]
    weight = jnp.where(valid, 1.0 / my_sigma, jnp.zeros_like(my_sigma))
    sim_mean = jnp.mean(integrate_dynamics, axis=0)
    perturbed = (integrate_dynamics - sim_mean[None, :]) * weight[None, :]
    innovation = (my_value - sim_mean) * weight
    gram_loc = jnp.dot(perturbed, perturbed.T, precision=exact_arithmetic)
    cross_loc = jnp.dot(perturbed, innovation, precision=exact_arithmetic)
    gram_block, cross_block = lax.psum((gram_loc, cross_loc), "member")
    gram_all, cross = lax.psum((gram_block, cross_block), "space")
    cov_matrix = gram_all + (sample_total - 1) * jnp.eye(sample_total, dtype=jnp.float32)
    lower_factor = jnp.linalg.cholesky(cov_matrix)
    inverse = solve_lower(lower_factor, jnp.eye(sample_total, dtype=jnp.float32))
    projected = jnp.dot(inverse, cross, precision=exact_arithmetic)
    mean_weight = jnp.dot(inverse.T, projected, precision=exact_arithmetic)
    weight_matrix_update = math.sqrt(sample_total - 1) * inverse + mean_weight[None, :]
    sample_vectors = prior_sample_full.reshape(sample_total, -1)
    prior_average = jnp.mean(sample_vectors, axis=0)
    updated_sample = prior_average[None, :] + jnp.dot(
        weight_matrix_update, sample_vectors - prior_average[None, :], precision=exact_arithmetic
    )
    returned = lax.all_to_all(
        updated_sample.reshape(prior_sample_full.shape),
        "member",
        split_axis=0,
        concat_axis=1,
        tiled=True,
    )
    return returned.reshape(anomaly_matrix, points_in_region)


MESH = pl.DeviceIdType.MESH
VMEM_SPEC = pl.BlockSpec(memory_space=pltpu.VMEM)
LANES = 128
MIB = 1 << 20
SUBLANES = 8


def split2(x):
    high = x.astype(jnp.bfloat16)
    low = (x - high.astype(jnp.float32)).astype(jnp.bfloat16)
    return high, low


def dot3(a, b, dims=((1,), (0,))):
    ah, al = split2(a)
    bh, bl = split2(b)
    d = functools.partial(
        lax.dot_general, dimension_numbers=(dims, ((), ())), preferred_element_type=jnp.float32
    )
    return (d(ah, bl) + d(al, bh)) + d(ah, bh)


def flat_row(ref):
    return jnp.concatenate([ref[i : i + 1, :] for i in range(ref.shape[0])], axis=1)


PIVOTS = 4


def inverse_factor(a):
    size = a.shape[0]
    count = size // SUBLANES
    shape = (SUBLANES, size)
    m = [a[SUBLANES * i : SUBLANES * (i + 1), :] for i in range(count)]
    diag = [None] * count
    lane = lax.broadcasted_iota(jnp.int32, shape, 1)
    sub = lax.broadcasted_iota(jnp.int32, shape, 0)

    def column(x, k):
        return jnp.broadcast_to(x[:, k : k + 1], shape)

    def row(x, r):
        return jnp.broadcast_to(x[r : r + 1, :], shape)

    for k in range(0, size, PIVOTS):
        t, r = divmod(k, SUBLANES)
        inside = (lane >= k) & (lane < k + PIVOTS)
        cols = [column(m[t], k + q) for q in range(PIVOTS)]
        pivot = {(q, p): row(cols[p], r + q) for p in range(PIVOTS) for q in range(p, PIVOTS)}
        base = [
            jnp.where(inside, jnp.where(lane == k + q, 1.0, 0.0), row(m[t], r + q))
            for q in range(PIVOTS)
        ]
        inverse = []
        for p in range(PIVOTS):
            inverse.append(1.0 / pivot[p, p])
            for q in range(p + 1, PIVOTS):
                factor = pivot[q, p] * inverse[p]
                base[q] = base[q] - factor * base[p]
                for s in range(q, PIVOTS):
                    pivot[s, q] = pivot[s, q] - factor * pivot[s, p]
        for p in range(PIVOTS):
            old = diag[t]
            diag[t] = pivot[p, p] if old is None else jnp.where(sub >= r + p, pivot[p, p], old)
        for i in range(t, count):
            cols_i = cols if i == t else [column(m[i], k + q) for q in range(PIVOTS)]
            cols_i = list(cols_i)
            if i == t:
                unit = jnp.where(lane - k == sub - r, 1.0, 0.0)
                x = jnp.where(inside & (sub >= r), unit, m[i])
            else:
                x = jnp.where(inside, 0.0, m[i])
            for p in range(PIVOTS):
                mult = cols_i[p] * inverse[p]
                if i == t:
                    mult = jnp.where(sub > r + p, mult, 0.0)
                for q in range(p + 1, PIVOTS):
                    cols_i[q] = cols_i[q] - mult * pivot[q, p]
                x = x - mult * base[p]
            m[i] = x
    out = []
    for i in range(count):
        keep = lane <= sub + SUBLANES * i
        out.append(jnp.where(keep, m[i] * lax.rsqrt(diag[i]), 0.0))
    return jnp.concatenate(out, axis=0)


def eye_mask(rows, cols):
    shape = (rows, cols)
    return lax.broadcasted_iota(jnp.int32, shape, 0) == lax.broadcasted_iota(jnp.int32, shape, 1)


TILE = 512
CHUNKS = (3072, 2048, 1536, 512)
TAIL = (768, 256)
EARLY = 1
LOADS = 2
GATHER = 1024


def offsets(widths):
    return [(sum(widths[:i]), w) for i, w in enumerate(widths)]


def gather_rows(x_ref, first, idx_ref, out_ref, rows, begin, end):
    shape = (SUBLANES, LANES)
    blocks = GATHER // LANES

    def step(t, _):
        for c in range(idx_ref.shape[0]):
            index = jnp.broadcast_to(idx_ref[c : c + 1, :], shape)
            lane = jnp.bitwise_and(index, LANES - 1)
            block = jnp.right_shift(index, LANES.bit_length() - 1) - t * blocks
            hits = [block == j for j in range(blocks)]
            columns = slice(c * LANES, (c + 1) * LANES)
            for g in range(0, rows, SUBLANES):
                place = pl.ds(pl.multiple_of(first + g, SUBLANES), SUBLANES)
                got = out_ref[place, columns]
                for j in range(blocks):
                    at = pl.ds(pl.multiple_of(t * GATHER + j * LANES, LANES), LANES)
                    x = x_ref[place, at]
                    got = jnp.where(hits[j], jnp.take_along_axis(x, lane, axis=1), got)
                out_ref[place, columns] = got
        return 0

    lax.fori_loop(begin // GATHER, end // GATHER, step, 0)


def transform_of(low_blocks, cross, t_ref, inv_ref, w_ref):
    samples = t_ref.shape[0]
    b = LANES
    ridge = float(samples - 1)
    n = samples // b
    work = {}
    for (i, j), block in low_blocks.items():
        work[i, j] = block + jnp.where(eye_mask(b, b), ridge, 0.0) if i == j else block
    inv = {}
    low = {}
    for k in range(n):
        inv[k, k] = inverse_factor(work[k, k])
        for i in range(k + 1, n):
            low[i, k] = dot3(work[i, k], inv[k, k], ((1,), (1,)))
        for i in range(k + 1, n):
            for j in range(k + 1, i + 1):
                work[i, j] = work[i, j] - dot3(low[i, k], low[j, k], ((1,), (1,)))
        for j in range(k):
            acc = dot3(low[k, j], inv[j, j])
            for m in range(j + 1, k):
                acc = acc + dot3(low[k, m], inv[m, j])
            inv[k, j] = -dot3(inv[k, k], acc)
    zero = jnp.zeros((b, b), jnp.float32)
    full = jnp.concatenate(
        [
            jnp.concatenate([inv[i, j] if j <= i else zero for j in range(n)], axis=1)
            for i in range(n)
        ],
        axis=0,
    )
    inv_ref[...] = full
    projected = jnp.sum(full * cross, axis=1, keepdims=True)
    mean_weight = jnp.sum(full * projected, axis=0, keepdims=True)
    w_ref[...] = jnp.broadcast_to(mean_weight, w_ref.shape)
    t_ref[...] = math.sqrt(samples - 1) * full + mean_weight


def own_weights(w_ref, core):
    half = w_ref.shape[1] // 2
    rows = half // 2
    w = w_ref[:, half:]
    return jnp.where(core == 0, w[:, :rows], w[:, rows:])


def split_dot(parts, x):
    th, stacked = parts
    rows = th.shape[0]
    xh, xl = split2(x)
    dot = functools.partial(jnp.dot, preferred_element_type=jnp.float32)
    both = dot(stacked, xh)
    return (both[rows:] + dot(th, xl)) + both[:rows]


def left_parts(t):
    th, tl = split2(t)
    return th, jnp.concatenate([th, tl], axis=0)


def filter_kernel(
    spaces,
    x_hbm,
    idx_hbm,
    data_hbm,
    sigma_hbm,
    used_ref,
    out_ref,
    idx_ref,
    data_ref,
    sigma_ref,
    xall,
    full,
    gram,
    cross,
    parts,
    total,
    t_ref,
    inv_ref,
    w_ref,
    sum_out,
    sum_in,
    mix_out,
    mix_in,
    y_out,
    y_in,
    ready,
    load,
    small,
    stream_send,
    stream_recv,
    forward_send,
    forward_recv,
    tail_send,
    tail_recv,
    reduce_sems,
    spread_sems,
    sum_sems,
    mix_sems,
    swap_sems,
    total_sems,
    observed_recv,
    side_recv,
    piece_recv,
    misc_send,
):
    rank = lax.axis_index("member")
    place = lax.axis_index("space")
    core = lax.rem(rank, 2)
    lower = rank < 2
    upper = rank >= 2
    side = rank + 1 - 2 * core
    across = lax.rem(rank + 2, 4)
    diagonal = lax.rem(side + 2, 4)
    rows, points = x_hbm.shape
    samples, slots = full.shape
    half = samples // 2
    stripe = gram.shape[0]
    chunk = stripe // spaces
    peers = [lax.rem(place + d, spaces) for d in range(1, spaces)]
    chunks = offsets(CHUNKS)
    tails = offsets(TAIL)
    tail_first = sum(CHUNKS)
    last_tail = len(TAIL) - 1

    def rows_of(member):
        return pl.ds(pl.multiple_of(member * rows, SUBLANES), rows)

    def remote(src, dst, sent, received, member, space):
        return pltpu.make_async_remote_copy(
            src_ref=src,
            dst_ref=dst,
            send_sem=sent,
            recv_sem=received,
            device_id={"member": member, "space": space},
            device_id_type=MESH,
        )

    def pending(ref, sem):
        return remote(ref, ref, sem, sem, side, place)

    def total_bytes(count):
        bands = next(n for n in range(samples // SUBLANES, 0, -1) if count % n == 0)
        return xall.at[: bands * SUBLANES, : count // bands * LANES]

    own = rows_of(rank)

    def stream(i):
        first, width = chunks[i]
        here = xall.at[own, first : first + width]
        return remote(here, here, stream_send, stream_recv.at[i], across, place)

    def arrived(i):
        first, width = chunks[i]
        return xall.at[rows_of(across), first : first + width]

    def arriving(i):
        return pending(arrived(i), stream_recv.at[i])

    def forward(i):
        here = arrived(i)
        return remote(here, here, forward_send, forward_recv.at[i], side, place)

    def tail_copy(i, target, lane):
        first, width = tails[i]
        columns = slice(first, first + width)
        return remote(
            y_out.at[target, :, columns],
            y_in.at[:, columns],
            tail_send,
            tail_recv.at[i],
            lane,
            place,
        )

    def tail_waiting(i):
        first, width = tails[i]
        return pending(y_in.at[:, first : first + width], tail_recv.at[i])

    def simple(ref, sent, received, member):
        return remote(ref, ref, sent, received, member, place)

    swap_x = simple(xall.at[own], swap_sems.at[0], swap_sems.at[1], side)
    swap_total = simple(total.at[core], total_sems.at[0], total_sems.at[1], side)
    observed = simple(full.at[own], misc_send, observed_recv, across)
    observed_side = simple(full.at[own], misc_send, side_recv, side)
    observed_far = simple(full.at[rows_of(across)], misc_send, side_recv, side)
    piece_rows = pl.ds(pl.multiple_of(place * chunk, SUBLANES), chunk)
    piece = total.at[core, piece_rows]
    cross_total = total.at[core, pl.ds(stripe, SUBLANES)]
    piece_far = simple(piece, misc_send, piece_recv, across)
    cross_far = simple(cross_total, misc_send, piece_recv, across)
    sums, mixes = [
        [remote(out, into.at[core], sems.at[0], sems.at[1], m, place) for m in (across, diagonal)]
        for out, into, sems in ((sum_out, sum_in, sum_sems), (mix_out, mix_in, mix_sems))
    ]
    spread = [
        remote(piece, piece, spread_sems.at[0], spread_sems.at[1], rank, p) for p in peers
    ]
    others = total.at[core, : (spaces - 1) * chunk]

    barrier = pltpu.get_barrier_semaphore()

    def greet(member, space):
        pl.semaphore_signal(
            barrier, inc=1, device_id={"member": member, "space": space}, device_id_type=MESH
        )

    @pl.when(upper)
    def _():
        greet(across, place)
        greet(side, place)
        for p in peers:
            greet(rank, p)

    @pl.when(lower)
    def _():
        greet(across, place)
        greet(diagonal, place)
        for p in peers:
            greet(across, p)

    def loading(t):
        columns = slice(t * part, (t + 1) * part)
        return pltpu.make_async_copy(x_hbm.at[:, columns], xall.at[own, columns], load.at[t])

    part = points // LOADS

    tables = [
        pltpu.make_async_copy(src, dst, small.at[i])
        for i, (src, dst) in enumerate(
            ((idx_hbm, idx_ref), (data_hbm, data_ref), (sigma_hbm, sigma_ref))
        )
    ]
    for copy in tables:
        copy.start()
    for t in range(LOADS):
        loading(t).start()
    full[own, :] = jnp.zeros((rows, slots), jnp.float32)

    @pl.when(lower)
    def _():
        pl.semaphore_wait(barrier, 1)

    loading(0).wait()

    @pl.when(lower)
    def _():
        for i in range(EARLY):
            stream(i).start()

    for copy in tables:
        copy.wait()
    gather_rows(xall, rank * rows, idx_ref, full, rows, 0, part)
    for t in range(1, LOADS):
        loading(t).wait()
        gather_rows(xall, rank * rows, idx_ref, full, rows, t * part, (t + 1) * part)

    @pl.when(upper)
    def _():
        pl.semaphore_wait(barrier, 2 * spaces + 1)
        pl.semaphore_signal(
            ready, inc=1, device_id={"member": across, "space": place}, device_id_type=MESH
        )
        observed.start()
        swap_x.start()
        sum_out[...] = jnp.sum(xall[own, :], axis=0, keepdims=True)
        for copy in sums:
            copy.start()
        for i in range(EARLY):
            arriving(i).wait_recv()
            forward(i).start()
        pending(total.at[core, : chunk + SUBLANES], piece_recv).wait_recv()
        for copy in spread:
            copy.start()

    @pl.when(lower)
    def _():
        pl.semaphore_wait(ready, 1)
        observed_side.start()
        observed.wait_recv()
        observed_far.start()
        swap_x.start()
        pending(full.at[:half], side_recv).wait_recv()
        slot = lax.broadcasted_iota(jnp.int32, (1, slots), 1)
        weight = jnp.where(slot < used_ref[0], 1.0 / flat_row(sigma_ref), 0.0)
        ev = full[...]
        mean = jnp.sum(ev, axis=0, keepdims=True) * (1.0 / samples)
        anomalies = (ev - mean) * weight
        innovation = (flat_row(data_ref) - mean) * weight
        first = lax.broadcasted_iota(jnp.int32, (SUBLANES, slots), 0) == 0
        extra = jnp.where(first, jnp.broadcast_to(innovation, (SUBLANES, slots)), 0.0)
        across_rows = ((1,), (1,))

        @pl.when(core == 0)
        def _():
            gram[...] = dot3(anomalies[:stripe], anomalies[:half], across_rows)
            cross[...] = dot3(extra, anomalies[:half], across_rows)

        @pl.when(core == 1)
        def _():
            top = samples - stripe
            gram[:top, :] = dot3(anomalies[stripe:], anomalies[:half], across_rows)
            gram[top:, :] = dot3(anomalies[half:], anomalies[half:], across_rows)
            cross[...] = dot3(extra, anomalies[half:], across_rows)

        scatter = []
        for d, p in enumerate(peers):
            source = gram.at[pl.ds(pl.multiple_of(p * chunk, SUBLANES), chunk)]
            for src, dst in (
                (source, parts.at[d, :chunk]),
                (cross, parts.at[d, pl.ds(chunk, SUBLANES)]),
            ):
                scatter.append(remote(src, dst, reduce_sems.at[0], reduce_sems.at[1], rank, p))
        for copy in scatter:
            copy.start()
        acc = gram[piece_rows, :]
        acc_cross = cross[...]
        pending(parts, reduce_sems.at[1]).wait_recv()
        for d in range(spaces - 1):
            acc = acc + parts[d, :chunk, :]
            acc_cross = acc_cross + parts[d, chunk:, :]
        total[core, piece_rows, :] = acc
        total[core, stripe : stripe + SUBLANES, :] = acc_cross
        piece_far.start()
        cross_far.start()
        for copy in spread:
            copy.start()
        for i in range(EARLY, len(chunks)):
            stream(i).start()
        pending(parts, reduce_sems.at[0]).wait_send()

    pending(others, spread_sems.at[1]).wait_recv()
    swap_total.start()
    swap_total.wait_recv()

    rest = stripe - half
    blocks = {
        (0, 0): total[0, :half, :],
        (1, 0): jnp.concatenate([total[0, half:stripe, :], total[1, : half - rest, :]], axis=0),
        (1, 1): total[1, half - rest : stripe, :],
    }
    cross_row = jnp.concatenate(
        [total[0, stripe : stripe + 1, :], total[1, stripe : stripe + 1, :]], axis=1
    )
    transform_of(blocks, cross_row, t_ref, inv_ref, w_ref)

    def tiles(first, last, body):
        def step(t, _):
            body(pl.ds(pl.multiple_of(t * TILE, LANES), TILE))
            return 0

        lax.fori_loop(first, last, step, 0)

    @pl.when(lower)
    def _():
        swap_x.wait_recv()
        pending(sum_in, sum_sems.at[1]).wait_recv()

        def product(target, first, width):
            at = rows_of(target + 2)
            columns = slice(tail_first + first, tail_first + first + width)
            x = xall[:half, columns]
            mean = jnp.sum(x, axis=0, keepdims=True)
            mean = (mean + sum_in[0, :, columns] + sum_in[1, :, columns]) * (1.0 / samples)
            scale = 1.0 - jnp.sum(t_ref[at, half:], axis=1, keepdims=True)
            y = split_dot(left_parts(t_ref[at, :half]), x - mean)
            y_out[target, :, first : first + width] = y + scale * mean

        for i in range(last_tail):
            product(core, *tails[i])
            tail_copy(i, core, across).start()

        @pl.when(core == 1)
        def _():
            for target, lane in ((1, 3), (0, 2)):
                product(target, *tails[last_tail])
                tail_copy(last_tail, target, lane).start()

        mine = left_parts(t_ref[own, :half])
        weight_sum = jnp.sum(w_ref[0:1, half:], axis=1, keepdims=True)

        def body(columns):
            x = xall[:half, columns]
            mean = jnp.sum(x, axis=0, keepdims=True)
            mean = (mean + sum_in[0, :, columns] + sum_in[1, :, columns]) * (1.0 / samples)
            out_ref[:, columns] = split_dot(mine, x - mean) + (1.0 - weight_sum) * mean

        tiles(0, points // TILE, body)
        pending(mix_in, mix_sems.at[1]).wait_recv()

        def mixed(columns):
            other = mix_in[0, :, columns] + mix_in[1, :, columns]
            out_ref[:, columns] = out_ref[:, columns] + other

        tiles(0, points // TILE, mixed)
        pending(xall.at[own, :tail_first], stream_send).wait_send()
        slots_tiles = 2 * rows * slots // (LANES * SUBLANES)
        tiles_sent = slots_tiles + chunk // SUBLANES + 1
        pending(total_bytes(tiles_sent), misc_send).wait_send()
        single = sum(TAIL[:last_tail])

        @pl.when(core == 0)
        def _():
            pending(y_out.at[0, :, :single], tail_send).wait_send()

        @pl.when(core == 1)
        def _():
            pending(y_out.at[:, :, : single // 2 + TAIL[last_tail]], tail_send).wait_send()

    @pl.when(upper)
    def _():
        mix = dot3(own_weights(w_ref, core), xall[own, :])
        mix_out[...] = mix[0:1, :]
        for copy in mixes:
            copy.start()
        mine = left_parts(t_ref[own, :])
        swap_x.wait_recv()

        def body(columns):
            x = xall[:, columns]
            mean = jnp.sum(x, axis=0, keepdims=True) * (1.0 / samples)
            out_ref[:, columns] = split_dot(mine, x - mean) + mean

        near = left_parts(t_ref[own, half:])

        def local(columns):
            out_ref[:, columns] = split_dot(near, xall[half:, columns])

        def done(i):
            forward(i).wait_recv()
            first, width = chunks[i]
            tiles(first // TILE, (first + width) // TILE, body)

        arriving(1).wait_recv()
        forward(1).start()
        done(0)
        arriving(2).wait_recv()
        forward(2).start()
        done(1)
        arriving(3).wait_recv()
        forward(3).start()
        done(2)
        tiles(tail_first // TILE, points // TILE, local)
        done(3)
        for i in range(len(tails)):
            first, width = tails[i]
            tail_waiting(i).wait_recv()
            columns = slice(tail_first + first, tail_first + first + width)
            out_ref[:, columns] = out_ref[:, columns] + y_in[:, first : first + width]
        pending(xall.at[rows_of(across), :tail_first], forward_send).wait_send()
        observed.wait_send()
        pending(sum_in, sum_sems.at[0]).wait_send()
        pending(mix_in, mix_sems.at[0]).wait_send()

    swap_x.wait_send()
    swap_total.wait_send()
    pending(others, spread_sems.at[0]).wait_send()


def filtered(prior, index, data, sigma, used, spaces):
    rows, points = prior.shape
    slots = index.size
    samples = 4 * rows
    half = samples // 2
    stripe = 3 * half // 2
    f32 = jnp.float32
    dma = pltpu.SemaphoreType.DMA
    vmem = pltpu.VMEM
    chunk = stripe // spaces
    pieces = (len(CHUNKS),)
    return pl.pallas_call(
        functools.partial(filter_kernel, spaces),
        out_shape=jax.ShapeDtypeStruct((rows, points), f32),
        in_specs=[pl.BlockSpec(memory_space=pltpu.HBM)] * 4
        + [pl.BlockSpec(memory_space=pltpu.SMEM)],
        out_specs=VMEM_SPEC,
        scratch_shapes=[
            vmem(index.shape, jnp.int32),
            vmem(data.shape, f32),
            vmem(sigma.shape, f32),
            vmem((samples, points), f32),
            vmem((samples, slots), f32),
            vmem((stripe, half), f32),
            vmem((SUBLANES, half), f32),
            vmem((spaces - 1, chunk + SUBLANES, half), f32),
            vmem((2, stripe + SUBLANES, half), f32),
            vmem((samples, samples), f32),
            vmem((samples, samples), f32),
            vmem((SUBLANES, samples), f32),
            vmem((1, points), f32),
            vmem((2, 1, points), f32),
            vmem((1, points), f32),
            vmem((2, 1, points), f32),
            vmem((2, rows, sum(TAIL)), f32),
            vmem((rows, sum(TAIL)), f32),
            pltpu.SemaphoreType.REGULAR,
            dma((LOADS,)),
            dma((3,)),
            dma(()),
            dma(pieces),
            dma(()),
            dma(pieces),
            dma(()),
            dma((len(TAIL),)),
            dma((2,)),
            dma((2,)),
            dma((2,)),
            dma((2,)),
            dma((2,)),
            dma((2,)),
            dma(()),
            dma(()),
            dma(()),
            dma(()),
        ],
        compiler_params=pltpu.CompilerParams(
            collective_id=0, has_side_effects=True, vmem_limit_bytes=32 * MIB
        ),
    )(prior, index, data, sigma, used)


def body(*arrays):
    prior_sample, location = arrays[:2]
    rows, points = prior_sample.shape
    members, spaces = lax.axis_size("member"), lax.axis_size("space")
    if (
        members != 4
        or rows * members != 2 * LANES
        or 3 * LANES // 2 % (SUBLANES * spaces)
        or points != sum(CHUNKS) + sum(TAIL)
        or location.shape[1] != LANES
    ):
        return general_body(*arrays)
    held = [pltpu.with_memory_space_constraint(a, pltpu.HBM) for a in arrays[:4]]
    return filtered(*held, arrays[4], spaces)


def solution(mesh):
    placed = (
        P("member", "space"),
        P("space", None),
        P("space", None),
        P("space", None),
        P("space"),
    )
    return jax.shard_map(
        body, mesh=mesh, in_specs=placed, out_specs=P("member", "space"), check_vma=False
    )
```

```python
import functools
import math

import jax
import jax.numpy as jnp
from jax import lax
from jax.experimental import pallas as pl
from jax.experimental.pallas import tpu as pltpu
from jax.sharding import PartitionSpec as P


def solve_lower(lower_factor, target):
    return lax.linalg.triangular_solve(lower_factor, target, left_side=True, lower=True)


def general_body(
    prior_sample,
    measured_point_location,
    measured_data,
    measurement_noise_sigma,
    measured_slots_used,
):
    exact_arithmetic = lax.Precision.HIGHEST
    anomaly_matrix, points_in_region = prior_sample.shape
    region_batches = lax.axis_size("member")
    sample_total = anomaly_matrix * region_batches
    pointwise_spread = points_in_region // region_batches
    linear_position = measured_point_location.reshape(-1)
    obs_blk = linear_position.shape[0]
    observation_deviation = obs_blk // region_batches
    propagated_grid = jnp.take(prior_sample, linear_position, axis=1).reshape(
        anomaly_matrix, region_batches, observation_deviation
    )
    prior_regions = prior_sample.reshape(anomaly_matrix, region_batches, pointwise_spread)
    prior_sample_full, integrate_dynamics = (
        lax.all_to_all(prior_regions, "member", split_axis=1, concat_axis=0, tiled=True),
        lax.all_to_all(propagated_grid, "member", split_axis=1, concat_axis=0, tiled=True),
    )
    integrate_dynamics = integrate_dynamics.reshape(sample_total, observation_deviation)
    rank = lax.axis_index("member")
    start = rank * observation_deviation
    my_value = lax.dynamic_slice_in_dim(measured_data.reshape(-1), start, observation_deviation)
    my_sigma = lax.dynamic_slice_in_dim(
        measurement_noise_sigma.reshape(-1), start, observation_deviation
    )
    slots = start + jnp.arange(observation_deviation, dtype=jnp.int32)
    valid = slots < measured_slots_used[0]
    weight = jnp.where(valid, 1.0 / my_sigma, jnp.zeros_like(my_sigma))
    sim_mean = jnp.mean(integrate_dynamics, axis=0)
    perturbed = (integrate_dynamics - sim_mean[None, :]) * weight[None, :]
    innovation = (my_value - sim_mean) * weight
    gram_loc = jnp.dot(perturbed, perturbed.T, precision=exact_arithmetic)
    cross_loc = jnp.dot(perturbed, innovation, precision=exact_arithmetic)
    gram_block, cross_block = lax.psum((gram_loc, cross_loc), "member")
    gram_all, cross = lax.psum((gram_block, cross_block), "space")
    cov_matrix = gram_all + (sample_total - 1) * jnp.eye(sample_total, dtype=jnp.float32)
    lower_factor = jnp.linalg.cholesky(cov_matrix)
    inverse = solve_lower(lower_factor, jnp.eye(sample_total, dtype=jnp.float32))
    projected = jnp.dot(inverse, cross, precision=exact_arithmetic)
    mean_weight = jnp.dot(inverse.T, projected, precision=exact_arithmetic)
    weight_matrix_update = math.sqrt(sample_total - 1) * inverse + mean_weight[None, :]
    sample_vectors = prior_sample_full.reshape(sample_total, -1)
    prior_average = jnp.mean(sample_vectors, axis=0)
    updated_sample = prior_average[None, :] + jnp.dot(
        weight_matrix_update, sample_vectors - prior_average[None, :], precision=exact_arithmetic
    )
    returned = lax.all_to_all(
        updated_sample.reshape(prior_sample_full.shape),
        "member",
        split_axis=0,
        concat_axis=1,
        tiled=True,
    )
    return returned.reshape(anomaly_matrix, points_in_region)


MESH = pl.DeviceIdType.MESH
VMEM_SPEC = pl.BlockSpec(memory_space=pltpu.VMEM)
LANES = 128
MIB = 1 << 20
SUBLANES = 8


def split2(x):
    high = x.astype(jnp.bfloat16)
    low = (x - high.astype(jnp.float32)).astype(jnp.bfloat16)
    return high, low


def dot3(a, b, dims=((1,), (0,))):
    ah, al = split2(a)
    bh, bl = split2(b)
    d = functools.partial(
        lax.dot_general, dimension_numbers=(dims, ((), ())), preferred_element_type=jnp.float32
    )
    return (d(ah, bl) + d(al, bh)) + d(ah, bh)


def flat_row(ref):
    return jnp.concatenate([ref[i : i + 1, :] for i in range(ref.shape[0])], axis=1)


PIVOTS = 4


def inverse_factor(a):
    size = a.shape[0]
    count = size // SUBLANES
    shape = (SUBLANES, size)
    m = [a[SUBLANES * i : SUBLANES * (i + 1), :] for i in range(count)]
    diag = [None] * count
    lane = lax.broadcasted_iota(jnp.int32, shape, 1)
    sub = lax.broadcasted_iota(jnp.int32, shape, 0)

    def column(x, k):
        return jnp.broadcast_to(x[:, k : k + 1], shape)

    def row(x, r):
        return jnp.broadcast_to(x[r : r + 1, :], shape)

    for k in range(0, size, PIVOTS):
        t, r = divmod(k, SUBLANES)
        inside = (lane >= k) & (lane < k + PIVOTS)
        cols = [column(m[t], k + q) for q in range(PIVOTS)]
        pivot = {(q, p): row(cols[p], r + q) for p in range(PIVOTS) for q in range(p, PIVOTS)}
        base = [
            jnp.where(inside, jnp.where(lane == k + q, 1.0, 0.0), row(m[t], r + q))
            for q in range(PIVOTS)
        ]
        inverse = []
        for p in range(PIVOTS):
            inverse.append(1.0 / pivot[p, p])
            for q in range(p + 1, PIVOTS):
                factor = pivot[q, p] * inverse[p]
                base[q] = base[q] - factor * base[p]
                for s in range(q, PIVOTS):
                    pivot[s, q] = pivot[s, q] - factor * pivot[s, p]
        for p in range(PIVOTS):
            old = diag[t]
            diag[t] = pivot[p, p] if old is None else jnp.where(sub >= r + p, pivot[p, p], old)
        for i in range(t, count):
            cols_i = cols if i == t else [column(m[i], k + q) for q in range(PIVOTS)]
            cols_i = list(cols_i)
            if i == t:
                unit = jnp.where(lane - k == sub - r, 1.0, 0.0)
                x = jnp.where(inside & (sub >= r), unit, m[i])
            else:
                x = jnp.where(inside, 0.0, m[i])
            for p in range(PIVOTS):
                mult = cols_i[p] * inverse[p]
                if i == t:
                    mult = jnp.where(sub > r + p, mult, 0.0)
                for q in range(p + 1, PIVOTS):
                    cols_i[q] = cols_i[q] - mult * pivot[q, p]
                x = x - mult * base[p]
            m[i] = x
    out = []
    for i in range(count):
        keep = lane <= sub + SUBLANES * i
        out.append(jnp.where(keep, m[i] * lax.rsqrt(diag[i]), 0.0))
    return jnp.concatenate(out, axis=0)


def eye_mask(rows, cols):
    shape = (rows, cols)
    return lax.broadcasted_iota(jnp.int32, shape, 0) == lax.broadcasted_iota(jnp.int32, shape, 1)


TILE = 1024
CHUNKS = (3072, 3072, 1024)
TAIL = (768, 256)
EARLY = 1
LOADS = 2
GATHER = 1024


def offsets(widths):
    return [(sum(widths[:i]), w) for i, w in enumerate(widths)]


def gather_rows(x_ref, first, idx_ref, out_ref, rows, begin, end):
    shape = (SUBLANES, LANES)
    blocks = GATHER // LANES

    def step(t, _):
        for c in range(idx_ref.shape[0]):
            index = jnp.broadcast_to(idx_ref[c : c + 1, :], shape)
            lane = jnp.bitwise_and(index, LANES - 1)
            block = jnp.right_shift(index, LANES.bit_length() - 1) - t * blocks
            hits = [block == j for j in range(blocks)]
            columns = slice(c * LANES, (c + 1) * LANES)
            for g in range(0, rows, SUBLANES):
                place = pl.ds(pl.multiple_of(first + g, SUBLANES), SUBLANES)
                got = out_ref[place, columns]
                for j in range(blocks):
                    at = pl.ds(pl.multiple_of(t * GATHER + j * LANES, LANES), LANES)
                    x = x_ref[place, at]
                    got = jnp.where(hits[j], jnp.take_along_axis(x, lane, axis=1), got)
                out_ref[place, columns] = got
        return 0

    lax.fori_loop(begin // GATHER, end // GATHER, step, 0)


def transform_of(low_blocks, cross, t_ref, inv_ref, w_ref):
    samples = t_ref.shape[0]
    b = LANES
    ridge = float(samples - 1)
    n = samples // b
    work = {}
    for (i, j), block in low_blocks.items():
        work[i, j] = block + jnp.where(eye_mask(b, b), ridge, 0.0) if i == j else block
    inv = {}
    low = {}
    for k in range(n):
        inv[k, k] = inverse_factor(work[k, k])
        for i in range(k + 1, n):
            low[i, k] = dot3(work[i, k], inv[k, k], ((1,), (1,)))
        for i in range(k + 1, n):
            for j in range(k + 1, i + 1):
                work[i, j] = work[i, j] - dot3(low[i, k], low[j, k], ((1,), (1,)))
        for j in range(k):
            acc = dot3(low[k, j], inv[j, j])
            for m in range(j + 1, k):
                acc = acc + dot3(low[k, m], inv[m, j])
            inv[k, j] = -dot3(inv[k, k], acc)
    zero = jnp.zeros((b, b), jnp.float32)
    full = jnp.concatenate(
        [
            jnp.concatenate([inv[i, j] if j <= i else zero for j in range(n)], axis=1)
            for i in range(n)
        ],
        axis=0,
    )
    inv_ref[...] = full
    projected = jnp.sum(full * cross, axis=1, keepdims=True)
    mean_weight = jnp.sum(full * projected, axis=0, keepdims=True)
    w_ref[...] = jnp.broadcast_to(mean_weight, w_ref.shape)
    t_ref[...] = math.sqrt(samples - 1) * full + mean_weight


def own_weights(w_ref, core):
    half = w_ref.shape[1] // 2
    rows = half // 2
    w = w_ref[:, half:]
    return jnp.where(core == 0, w[:, :rows], w[:, rows:])


def split_dot(parts, x):
    th, stacked = parts
    rows = th.shape[0]
    xh, xl = split2(x)
    dot = functools.partial(jnp.dot, preferred_element_type=jnp.float32)
    both = dot(stacked, xh)
    return (both[rows:] + dot(th, xl)) + both[:rows]


def left_parts(t):
    th, tl = split2(t)
    return th, jnp.concatenate([th, tl], axis=0)


def filter_kernel(
    spaces,
    x_hbm,
    idx_hbm,
    data_hbm,
    sigma_hbm,
    used_ref,
    out_ref,
    idx_ref,
    data_ref,
    sigma_ref,
    xall,
    full,
    gram,
    cross,
    parts,
    total,
    t_ref,
    inv_ref,
    w_ref,
    sum_out,
    sum_in,
    mix_out,
    mix_in,
    y_out,
    y_in,
    ready,
    load,
    small,
    stream_send,
    stream_recv,
    forward_send,
    forward_recv,
    tail_send,
    tail_recv,
    reduce_sems,
    spread_sems,
    sum_sems,
    mix_sems,
    swap_sems,
    total_sems,
    observed_recv,
    side_recv,
    piece_recv,
    misc_send,
):
    rank = lax.axis_index("member")
    place = lax.axis_index("space")
    core = lax.rem(rank, 2)
    lower = rank < 2
    upper = rank >= 2
    side = rank + 1 - 2 * core
    across = lax.rem(rank + 2, 4)
    diagonal = lax.rem(side + 2, 4)
    rows, points = x_hbm.shape
    samples, slots = full.shape
    half = samples // 2
    stripe = gram.shape[0]
    chunk = stripe // spaces
    peers = [lax.rem(place + d, spaces) for d in range(1, spaces)]
    chunks = offsets(CHUNKS)
    tails = offsets(TAIL)
    tail_first = sum(CHUNKS)
    last_tail = len(TAIL) - 1

    def rows_of(member):
        return pl.ds(pl.multiple_of(member * rows, SUBLANES), rows)

    def remote(src, dst, sent, received, member, space):
        return pltpu.make_async_remote_copy(
            src_ref=src,
            dst_ref=dst,
            send_sem=sent,
            recv_sem=received,
            device_id={"member": member, "space": space},
            device_id_type=MESH,
        )

    def pending(ref, sem):
        return remote(ref, ref, sem, sem, side, place)

    def total_bytes(count):
        bands = next(n for n in range(samples // SUBLANES, 0, -1) if count % n == 0)
        return xall.at[: bands * SUBLANES, : count // bands * LANES]

    own = rows_of(rank)

    def stream(i):
        first, width = chunks[i]
        here = xall.at[own, first : first + width]
        return remote(here, here, stream_send, stream_recv.at[i], across, place)

    def arrived(i):
        first, width = chunks[i]
        return xall.at[rows_of(across), first : first + width]

    def arriving(i):
        return pending(arrived(i), stream_recv.at[i])

    def forward(i):
        here = arrived(i)
        return remote(here, here, forward_send, forward_recv.at[i], side, place)

    def tail_copy(i, target, lane):
        first, width = tails[i]
        columns = slice(first, first + width)
        return remote(
            y_out.at[target, :, columns],
            y_in.at[:, columns],
            tail_send,
            tail_recv.at[i],
            lane,
            place,
        )

    def tail_waiting(i):
        first, width = tails[i]
        return pending(y_in.at[:, first : first + width], tail_recv.at[i])

    def simple(ref, sent, received, member):
        return remote(ref, ref, sent, received, member, place)

    swap_x = simple(xall.at[own], swap_sems.at[0], swap_sems.at[1], side)
    swap_total = simple(total.at[core], total_sems.at[0], total_sems.at[1], side)
    observed = simple(full.at[own], misc_send, observed_recv, across)
    observed_side = simple(full.at[own], misc_send, side_recv, side)
    observed_far = simple(full.at[rows_of(across)], misc_send, side_recv, side)
    piece_rows = pl.ds(pl.multiple_of(place * chunk, SUBLANES), chunk)
    piece = total.at[core, piece_rows]
    cross_total = total.at[core, pl.ds(stripe, SUBLANES)]
    piece_far = simple(piece, misc_send, piece_recv, across)
    cross_far = simple(cross_total, misc_send, piece_recv, across)
    sums, mixes = [
        [remote(out, into.at[core], sems.at[0], sems.at[1], m, place) for m in (across, diagonal)]
        for out, into, sems in ((sum_out, sum_in, sum_sems), (mix_out, mix_in, mix_sems))
    ]
    spread = [
        remote(piece, piece, spread_sems.at[0], spread_sems.at[1], rank, p) for p in peers
    ]
    others = total.at[core, : (spaces - 1) * chunk]

    barrier = pltpu.get_barrier_semaphore()

    def greet(member, space):
        pl.semaphore_signal(
            barrier, inc=1, device_id={"member": member, "space": space}, device_id_type=MESH
        )

    @pl.when(upper)
    def _():
        greet(across, place)
        greet(side, place)
        for p in peers:
            greet(rank, p)

    @pl.when(lower)
    def _():
        greet(across, place)
        greet(diagonal, place)
        for p in peers:
            greet(across, p)

    def loading(t):
        columns = slice(t * part, (t + 1) * part)
        return pltpu.make_async_copy(x_hbm.at[:, columns], xall.at[own, columns], load.at[t])

    part = points // LOADS

    tables = [
        pltpu.make_async_copy(src, dst, small.at[i])
        for i, (src, dst) in enumerate(
            ((idx_hbm, idx_ref), (data_hbm, data_ref), (sigma_hbm, sigma_ref))
        )
    ]
    for copy in tables:
        copy.start()
    for t in range(LOADS):
        loading(t).start()
    full[own, :] = jnp.zeros((rows, slots), jnp.float32)

    @pl.when(lower)
    def _():
        pl.semaphore_wait(barrier, 1)

    loading(0).wait()

    @pl.when(lower)
    def _():
        for i in range(EARLY):
            stream(i).start()

    for copy in tables:
        copy.wait()
    gather_rows(xall, rank * rows, idx_ref, full, rows, 0, part)
    for t in range(1, LOADS):
        loading(t).wait()
        gather_rows(xall, rank * rows, idx_ref, full, rows, t * part, (t + 1) * part)

    @pl.when(upper)
    def _():
        pl.semaphore_wait(barrier, 2 * spaces + 1)
        pl.semaphore_signal(
            ready, inc=1, device_id={"member": across, "space": place}, device_id_type=MESH
        )
        observed.start()
        swap_x.start()
        sum_out[...] = jnp.sum(xall[own, :], axis=0, keepdims=True)
        for copy in sums:
            copy.start()
        for i in range(EARLY):
            arriving(i).wait_recv()
            forward(i).start()
        pending(total.at[core, : chunk + SUBLANES], piece_recv).wait_recv()
        for copy in spread:
            copy.start()

    @pl.when(lower)
    def _():
        pl.semaphore_wait(ready, 1)
        observed_side.start()
        observed.wait_recv()
        observed_far.start()
        swap_x.start()
        pending(full.at[:half], side_recv).wait_recv()
        slot = lax.broadcasted_iota(jnp.int32, (1, slots), 1)
        weight = jnp.where(slot < used_ref[0], 1.0 / flat_row(sigma_ref), 0.0)
        ev = full[...]
        mean = jnp.sum(ev, axis=0, keepdims=True) * (1.0 / samples)
        anomalies = (ev - mean) * weight
        innovation = (flat_row(data_ref) - mean) * weight
        first = lax.broadcasted_iota(jnp.int32, (SUBLANES, slots), 0) == 0
        extra = jnp.where(first, jnp.broadcast_to(innovation, (SUBLANES, slots)), 0.0)
        across_rows = ((1,), (1,))

        @pl.when(core == 0)
        def _():
            gram[...] = dot3(anomalies[:stripe], anomalies[:half], across_rows)
            cross[...] = dot3(extra, anomalies[:half], across_rows)

        @pl.when(core == 1)
        def _():
            top = samples - stripe
            gram[:top, :] = dot3(anomalies[stripe:], anomalies[:half], across_rows)
            gram[top:, :] = dot3(anomalies[half:], anomalies[half:], across_rows)
            cross[...] = dot3(extra, anomalies[half:], across_rows)

        scatter = []
        for d, p in enumerate(peers):
            source = gram.at[pl.ds(pl.multiple_of(p * chunk, SUBLANES), chunk)]
            for src, dst in (
                (source, parts.at[d, :chunk]),
                (cross, parts.at[d, pl.ds(chunk, SUBLANES)]),
            ):
                scatter.append(remote(src, dst, reduce_sems.at[0], reduce_sems.at[1], rank, p))
        for copy in scatter:
            copy.start()
        acc = gram[piece_rows, :]
        acc_cross = cross[...]
        pending(parts, reduce_sems.at[1]).wait_recv()
        for d in range(spaces - 1):
            acc = acc + parts[d, :chunk, :]
            acc_cross = acc_cross + parts[d, chunk:, :]
        total[core, piece_rows, :] = acc
        total[core, stripe : stripe + SUBLANES, :] = acc_cross
        piece_far.start()
        cross_far.start()
        for copy in spread:
            copy.start()
        for i in range(EARLY, len(chunks)):
            stream(i).start()
        pending(parts, reduce_sems.at[0]).wait_send()

    pending(others, spread_sems.at[1]).wait_recv()
    swap_total.start()
    swap_total.wait_recv()

    rest = stripe - half
    blocks = {
        (0, 0): total[0, :half, :],
        (1, 0): jnp.concatenate([total[0, half:stripe, :], total[1, : half - rest, :]], axis=0),
        (1, 1): total[1, half - rest : stripe, :],
    }
    cross_row = jnp.concatenate(
        [total[0, stripe : stripe + 1, :], total[1, stripe : stripe + 1, :]], axis=1
    )
    transform_of(blocks, cross_row, t_ref, inv_ref, w_ref)

    def tiles(first, last, body):
        def step(t, _):
            body(pl.ds(pl.multiple_of(t * TILE, LANES), TILE))
            return 0

        lax.fori_loop(first, last, step, 0)

    @pl.when(lower)
    def _():
        swap_x.wait_recv()
        pending(sum_in, sum_sems.at[1]).wait_recv()

        def product(target, first, width):
            at = rows_of(target + 2)
            columns = slice(tail_first + first, tail_first + first + width)
            x = xall[:half, columns]
            mean = jnp.sum(x, axis=0, keepdims=True)
            mean = (mean + sum_in[0, :, columns] + sum_in[1, :, columns]) * (1.0 / samples)
            scale = 1.0 - jnp.sum(t_ref[at, half:], axis=1, keepdims=True)
            y = split_dot(left_parts(t_ref[at, :half]), x - mean)
            y_out[target, :, first : first + width] = y + scale * mean

        for i in range(last_tail):
            product(core, *tails[i])
            tail_copy(i, core, across).start()

        @pl.when(core == 1)
        def _():
            for target, lane in ((1, 3), (0, 2)):
                product(target, *tails[last_tail])
                tail_copy(last_tail, target, lane).start()

        mine = left_parts(t_ref[own, :half])
        weight_sum = jnp.sum(w_ref[0:1, half:], axis=1, keepdims=True)

        def body(columns):
            x = xall[:half, columns]
            mean = jnp.sum(x, axis=0, keepdims=True)
            mean = (mean + sum_in[0, :, columns] + sum_in[1, :, columns]) * (1.0 / samples)
            out_ref[:, columns] = split_dot(mine, x - mean) + (1.0 - weight_sum) * mean

        tiles(0, points // TILE, body)
        pending(mix_in, mix_sems.at[1]).wait_recv()

        def mixed(columns):
            other = mix_in[0, :, columns] + mix_in[1, :, columns]
            out_ref[:, columns] = out_ref[:, columns] + other

        tiles(0, points // TILE, mixed)
        pending(xall.at[own, :tail_first], stream_send).wait_send()
        slots_tiles = 2 * rows * slots // (LANES * SUBLANES)
        tiles_sent = slots_tiles + chunk // SUBLANES + 1
        pending(total_bytes(tiles_sent), misc_send).wait_send()
        single = sum(TAIL[:last_tail])

        @pl.when(core == 0)
        def _():
            pending(y_out.at[0, :, :single], tail_send).wait_send()

        @pl.when(core == 1)
        def _():
            pending(y_out.at[:, :, : single // 2 + TAIL[last_tail]], tail_send).wait_send()

    @pl.when(upper)
    def _():
        arriving(1).wait_recv()
        forward(1).start()
        mix = dot3(own_weights(w_ref, core), xall[own, :])
        mix_out[...] = mix[0:1, :]
        for copy in mixes:
            copy.start()
        mine = left_parts(t_ref[own, :])
        swap_x.wait_recv()

        def body(columns):
            x = xall[:, columns]
            mean = jnp.sum(x, axis=0, keepdims=True) * (1.0 / samples)
            out_ref[:, columns] = split_dot(mine, x - mean) + mean

        near = left_parts(t_ref[own, half:])

        def local(columns):
            out_ref[:, columns] = split_dot(near, xall[half:, columns])

        def done(i):
            forward(i).wait_recv()
            first, width = chunks[i]
            tiles(first // TILE, (first + width) // TILE, body)

        done(0)
        arriving(2).wait_recv()
        forward(2).start()
        done(1)
        tiles(tail_first // TILE, points // TILE, local)
        done(2)
        for i in range(len(tails)):
            first, width = tails[i]
            tail_waiting(i).wait_recv()
            columns = slice(tail_first + first, tail_first + first + width)
            out_ref[:, columns] = out_ref[:, columns] + y_in[:, first : first + width]
        pending(xall.at[rows_of(across), :tail_first], forward_send).wait_send()
        observed.wait_send()
        pending(sum_in, sum_sems.at[0]).wait_send()
        pending(mix_in, mix_sems.at[0]).wait_send()

    swap_x.wait_send()
    swap_total.wait_send()
    pending(others, spread_sems.at[0]).wait_send()


def filtered(prior, index, data, sigma, used, spaces):
    rows, points = prior.shape
    slots = index.size
    samples = 4 * rows
    half = samples // 2
    stripe = 3 * half // 2
    f32 = jnp.float32
    dma = pltpu.SemaphoreType.DMA
    vmem = pltpu.VMEM
    chunk = stripe // spaces
    pieces = (len(CHUNKS),)
    return pl.pallas_call(
        functools.partial(filter_kernel, spaces),
        out_shape=jax.ShapeDtypeStruct((rows, points), f32),
        in_specs=[pl.BlockSpec(memory_space=pltpu.HBM)] * 4
        + [pl.BlockSpec(memory_space=pltpu.SMEM)],
        out_specs=VMEM_SPEC,
        scratch_shapes=[
            vmem(index.shape, jnp.int32),
            vmem(data.shape, f32),
            vmem(sigma.shape, f32),
            vmem((samples, points), f32),
            vmem((samples, slots), f32),
            vmem((stripe, half), f32),
            vmem((SUBLANES, half), f32),
            vmem((spaces - 1, chunk + SUBLANES, half), f32),
            vmem((2, stripe + SUBLANES, half), f32),
            vmem((samples, samples), f32),
            vmem((samples, samples), f32),
            vmem((SUBLANES, samples), f32),
            vmem((1, points), f32),
            vmem((2, 1, points), f32),
            vmem((1, points), f32),
            vmem((2, 1, points), f32),
            vmem((2, rows, sum(TAIL)), f32),
            vmem((rows, sum(TAIL)), f32),
            pltpu.SemaphoreType.REGULAR,
            dma((LOADS,)),
            dma((3,)),
            dma(()),
            dma(pieces),
            dma(()),
            dma(pieces),
            dma(()),
            dma((len(TAIL),)),
            dma((2,)),
            dma((2,)),
            dma((2,)),
            dma((2,)),
            dma((2,)),
            dma((2,)),
            dma(()),
            dma(()),
            dma(()),
            dma(()),
        ],
        compiler_params=pltpu.CompilerParams(
            collective_id=0, has_side_effects=True, vmem_limit_bytes=32 * MIB
        ),
    )(prior, index, data, sigma, used)


def body(*arrays):
    prior_sample, location = arrays[:2]
    rows, points = prior_sample.shape
    members, spaces = lax.axis_size("member"), lax.axis_size("space")
    if (
        members != 4
        or rows * members != 2 * LANES
        or 3 * LANES // 2 % (SUBLANES * spaces)
        or points != sum(CHUNKS) + sum(TAIL)
        or location.shape[1] != LANES
    ):
        return general_body(*arrays)
    held = [pltpu.with_memory_space_constraint(a, pltpu.HBM) for a in arrays[:4]]
    return filtered(*held, arrays[4], spaces)


def solution(mesh):
    placed = (
        P("member", "space"),
        P("space", None),
        P("space", None),
        P("space", None),
        P("space"),
    )
    return jax.shard_map(
        body, mesh=mesh, in_specs=placed, out_specs=P("member", "space"), check_vma=False
    )
```

```python
import functools
import math

import jax
import jax.numpy as jnp
from jax import lax
from jax.experimental import pallas as pl
from jax.experimental.pallas import tpu as pltpu
from jax.sharding import PartitionSpec as P


def solve_lower(lower_factor, target):
    return lax.linalg.triangular_solve(lower_factor, target, left_side=True, lower=True)


def general_body(
    prior_sample,
    measured_point_location,
    measured_data,
    measurement_noise_sigma,
    measured_slots_used,
):
    exact_arithmetic = lax.Precision.HIGHEST
    anomaly_matrix, points_in_region = prior_sample.shape
    region_batches = lax.axis_size("member")
    sample_total = anomaly_matrix * region_batches
    pointwise_spread = points_in_region // region_batches
    linear_position = measured_point_location.reshape(-1)
    obs_blk = linear_position.shape[0]
    observation_deviation = obs_blk // region_batches
    propagated_grid = jnp.take(prior_sample, linear_position, axis=1).reshape(
        anomaly_matrix, region_batches, observation_deviation
    )
    prior_regions = prior_sample.reshape(anomaly_matrix, region_batches, pointwise_spread)
    prior_sample_full, integrate_dynamics = (
        lax.all_to_all(prior_regions, "member", split_axis=1, concat_axis=0, tiled=True),
        lax.all_to_all(propagated_grid, "member", split_axis=1, concat_axis=0, tiled=True),
    )
    integrate_dynamics = integrate_dynamics.reshape(sample_total, observation_deviation)
    rank = lax.axis_index("member")
    start = rank * observation_deviation
    my_value = lax.dynamic_slice_in_dim(measured_data.reshape(-1), start, observation_deviation)
    my_sigma = lax.dynamic_slice_in_dim(
        measurement_noise_sigma.reshape(-1), start, observation_deviation
    )
    slots = start + jnp.arange(observation_deviation, dtype=jnp.int32)
    valid = slots < measured_slots_used[0]
    weight = jnp.where(valid, 1.0 / my_sigma, jnp.zeros_like(my_sigma))
    sim_mean = jnp.mean(integrate_dynamics, axis=0)
    perturbed = (integrate_dynamics - sim_mean[None, :]) * weight[None, :]
    innovation = (my_value - sim_mean) * weight
    gram_loc = jnp.dot(perturbed, perturbed.T, precision=exact_arithmetic)
    cross_loc = jnp.dot(perturbed, innovation, precision=exact_arithmetic)
    gram_block, cross_block = lax.psum((gram_loc, cross_loc), "member")
    gram_all, cross = lax.psum((gram_block, cross_block), "space")
    cov_matrix = gram_all + (sample_total - 1) * jnp.eye(sample_total, dtype=jnp.float32)
    lower_factor = jnp.linalg.cholesky(cov_matrix)
    inverse = solve_lower(lower_factor, jnp.eye(sample_total, dtype=jnp.float32))
    projected = jnp.dot(inverse, cross, precision=exact_arithmetic)
    mean_weight = jnp.dot(inverse.T, projected, precision=exact_arithmetic)
    weight_matrix_update = math.sqrt(sample_total - 1) * inverse + mean_weight[None, :]
    sample_vectors = prior_sample_full.reshape(sample_total, -1)
    prior_average = jnp.mean(sample_vectors, axis=0)
    updated_sample = prior_average[None, :] + jnp.dot(
        weight_matrix_update, sample_vectors - prior_average[None, :], precision=exact_arithmetic
    )
    returned = lax.all_to_all(
        updated_sample.reshape(prior_sample_full.shape),
        "member",
        split_axis=0,
        concat_axis=1,
        tiled=True,
    )
    return returned.reshape(anomaly_matrix, points_in_region)


MESH = pl.DeviceIdType.MESH
VMEM_SPEC = pl.BlockSpec(memory_space=pltpu.VMEM)
LANES = 128
MIB = 1 << 20
SUBLANES = 8


def split2(x):
    high = x.astype(jnp.bfloat16)
    low = (x - high.astype(jnp.float32)).astype(jnp.bfloat16)
    return high, low


def dot3(a, b, dims=((1,), (0,))):
    ah, al = split2(a)
    bh, bl = split2(b)
    d = functools.partial(
        lax.dot_general, dimension_numbers=(dims, ((), ())), preferred_element_type=jnp.float32
    )
    return (d(ah, bl) + d(al, bh)) + d(ah, bh)


def flat_row(ref):
    return jnp.concatenate([ref[i : i + 1, :] for i in range(ref.shape[0])], axis=1)


PIVOTS = 4


def inverse_factor(a):
    size = a.shape[0]
    count = size // SUBLANES
    shape = (SUBLANES, size)
    m = [a[SUBLANES * i : SUBLANES * (i + 1), :] for i in range(count)]
    diag = [None] * count
    lane = lax.broadcasted_iota(jnp.int32, shape, 1)
    sub = lax.broadcasted_iota(jnp.int32, shape, 0)

    def column(x, k):
        return jnp.broadcast_to(x[:, k : k + 1], shape)

    def row(x, r):
        return jnp.broadcast_to(x[r : r + 1, :], shape)

    for k in range(0, size, PIVOTS):
        t, r = divmod(k, SUBLANES)
        inside = (lane >= k) & (lane < k + PIVOTS)
        cols = [column(m[t], k + q) for q in range(PIVOTS)]
        pivot = {(q, p): row(cols[p], r + q) for p in range(PIVOTS) for q in range(p, PIVOTS)}
        base = [
            jnp.where(inside, jnp.where(lane == k + q, 1.0, 0.0), row(m[t], r + q))
            for q in range(PIVOTS)
        ]
        inverse = []
        for p in range(PIVOTS):
            inverse.append(1.0 / pivot[p, p])
            for q in range(p + 1, PIVOTS):
                factor = pivot[q, p] * inverse[p]
                base[q] = base[q] - factor * base[p]
                for s in range(q, PIVOTS):
                    pivot[s, q] = pivot[s, q] - factor * pivot[s, p]
        for p in range(PIVOTS):
            old = diag[t]
            diag[t] = pivot[p, p] if old is None else jnp.where(sub >= r + p, pivot[p, p], old)
        for i in range(t, count):
            cols_i = cols if i == t else [column(m[i], k + q) for q in range(PIVOTS)]
            cols_i = list(cols_i)
            if i == t:
                unit = jnp.where(lane - k == sub - r, 1.0, 0.0)
                x = jnp.where(inside & (sub >= r), unit, m[i])
            else:
                x = jnp.where(inside, 0.0, m[i])
            for p in range(PIVOTS):
                mult = cols_i[p] * inverse[p]
                if i == t:
                    mult = jnp.where(sub > r + p, mult, 0.0)
                for q in range(p + 1, PIVOTS):
                    cols_i[q] = cols_i[q] - mult * pivot[q, p]
                x = x - mult * base[p]
            m[i] = x
    out = []
    for i in range(count):
        keep = lane <= sub + SUBLANES * i
        out.append(jnp.where(keep, m[i] * lax.rsqrt(diag[i]), 0.0))
    return jnp.concatenate(out, axis=0)


def eye_mask(rows, cols):
    shape = (rows, cols)
    return lax.broadcasted_iota(jnp.int32, shape, 0) == lax.broadcasted_iota(jnp.int32, shape, 1)


TILE = 1024
CHUNKS = (3072, 3072, 1024)
TAIL = (768, 256)
EARLY = 1
LOADS = 2
GATHER = 1024


def offsets(widths):
    return [(sum(widths[:i]), w) for i, w in enumerate(widths)]


def gather_rows(x_ref, first, idx_ref, out_ref, rows, begin, end):
    shape = (SUBLANES, LANES)
    blocks = GATHER // LANES

    def step(t, _):
        for c in range(idx_ref.shape[0]):
            index = jnp.broadcast_to(idx_ref[c : c + 1, :], shape)
            lane = jnp.bitwise_and(index, LANES - 1)
            block = jnp.right_shift(index, LANES.bit_length() - 1) - t * blocks
            hits = [block == j for j in range(blocks)]
            columns = slice(c * LANES, (c + 1) * LANES)
            for g in range(0, rows, SUBLANES):
                place = pl.ds(pl.multiple_of(first + g, SUBLANES), SUBLANES)
                got = out_ref[place, columns]
                for j in range(blocks):
                    at = pl.ds(pl.multiple_of(t * GATHER + j * LANES, LANES), LANES)
                    x = x_ref[place, at]
                    got = jnp.where(hits[j], jnp.take_along_axis(x, lane, axis=1), got)
                out_ref[place, columns] = got
        return 0

    lax.fori_loop(begin // GATHER, end // GATHER, step, 0)


def transform_of(low_blocks, cross, t_ref, inv_ref, w_ref):
    samples = t_ref.shape[0]
    b = LANES
    ridge = float(samples - 1)
    n = samples // b
    work = {}
    for (i, j), block in low_blocks.items():
        work[i, j] = block + jnp.where(eye_mask(b, b), ridge, 0.0) if i == j else block
    inv = {}
    low = {}
    for k in range(n):
        inv[k, k] = inverse_factor(work[k, k])
        for i in range(k + 1, n):
            low[i, k] = dot3(work[i, k], inv[k, k], ((1,), (1,)))
        for i in range(k + 1, n):
            for j in range(k + 1, i + 1):
                work[i, j] = work[i, j] - dot3(low[i, k], low[j, k], ((1,), (1,)))
        for j in range(k):
            acc = dot3(low[k, j], inv[j, j])
            for m in range(j + 1, k):
                acc = acc + dot3(low[k, m], inv[m, j])
            inv[k, j] = -dot3(inv[k, k], acc)
    zero = jnp.zeros((b, b), jnp.float32)
    full = jnp.concatenate(
        [
            jnp.concatenate([inv[i, j] if j <= i else zero for j in range(n)], axis=1)
            for i in range(n)
        ],
        axis=0,
    )
    inv_ref[...] = full
    projected = jnp.sum(full * cross, axis=1, keepdims=True)
    mean_weight = jnp.sum(full * projected, axis=0, keepdims=True)
    w_ref[...] = jnp.broadcast_to(mean_weight, w_ref.shape)
    t_ref[...] = math.sqrt(samples - 1) * full + mean_weight


def own_weights(w_ref, core):
    half = w_ref.shape[1] // 2
    rows = half // 2
    w = w_ref[:, half:]
    return jnp.where(core == 0, w[:, :rows], w[:, rows:])


def split_dot(parts, x):
    th, stacked = parts
    rows = th.shape[0]
    xh, xl = split2(x)
    dot = functools.partial(jnp.dot, preferred_element_type=jnp.float32)
    both = dot(stacked, xh)
    return (both[rows:] + dot(th, xl)) + both[:rows]


def left_parts(t):
    th, tl = split2(t)
    return th, jnp.concatenate([th, tl], axis=0)


def filter_kernel(
    spaces,
    x_hbm,
    idx_hbm,
    data_hbm,
    sigma_hbm,
    used_ref,
    out_ref,
    idx_ref,
    data_ref,
    sigma_ref,
    xall,
    full,
    gram,
    cross,
    parts,
    total,
    t_ref,
    inv_ref,
    w_ref,
    sum_out,
    sum_in,
    mix_out,
    mix_in,
    y_out,
    y_in,
    ready,
    load,
    small,
    sent,
    both_sent,
    stream_recv,
    forward_recv,
    tail_send,
    tail_recv,
    reduce_recv,
    spread_recv,
    sum_recv,
    mix_recv,
    swap_recv,
    total_recv,
    observed_recv,
    side_recv,
    piece_recv,
):
    rank = lax.axis_index("member")
    place = lax.axis_index("space")
    core = lax.rem(rank, 2)
    lower = rank < 2
    upper = rank >= 2
    side = rank + 1 - 2 * core
    across = lax.rem(rank + 2, 4)
    diagonal = lax.rem(side + 2, 4)
    rows, points = x_hbm.shape
    samples, slots = full.shape
    half = samples // 2
    stripe = gram.shape[0]
    chunk = stripe // spaces
    peers = [lax.rem(place + d, spaces) for d in range(1, spaces)]
    chunks = offsets(CHUNKS)
    tails = offsets(TAIL)
    tail_first = sum(CHUNKS)
    last_tail = len(TAIL) - 1

    def rows_of(member):
        return pl.ds(pl.multiple_of(member * rows, SUBLANES), rows)

    def remote(src, dst, sent, received, member, space):
        return pltpu.make_async_remote_copy(
            src_ref=src,
            dst_ref=dst,
            send_sem=sent,
            recv_sem=received,
            device_id={"member": member, "space": space},
            device_id_type=MESH,
        )

    def pending(ref, sem):
        return remote(ref, ref, sem, sem, side, place)

    def total_bytes(values):
        count = values // (SUBLANES * LANES)
        bands = next(n for n in range(samples // SUBLANES, 0, -1) if count % n == 0)
        return xall.at[: bands * SUBLANES, : count // bands * LANES]

    own = rows_of(rank)

    def stream(i):
        first, width = chunks[i]
        here = xall.at[own, first : first + width]
        return remote(here, here, sent, stream_recv.at[i], across, place)

    def arrived(i):
        first, width = chunks[i]
        return xall.at[rows_of(across), first : first + width]

    def arriving(i):
        return pending(arrived(i), stream_recv.at[i])

    def forward(i):
        here = arrived(i)
        return remote(here, here, sent, forward_recv.at[i], side, place)

    def tail_copy(i, target, lane):
        first, width = tails[i]
        columns = slice(first, first + width)
        return remote(
            y_out.at[target, :, columns],
            y_in.at[:, columns],
            tail_send,
            tail_recv.at[i],
            lane,
            place,
        )

    def tail_waiting(i):
        first, width = tails[i]
        return pending(y_in.at[:, first : first + width], tail_recv.at[i])

    def simple(ref, sent, received, member):
        return remote(ref, ref, sent, received, member, place)

    swap_x = simple(xall.at[own], both_sent, swap_recv, side)
    swap_total = simple(total.at[core], both_sent, total_recv, side)
    observed = simple(full.at[own], sent, observed_recv, across)
    observed_side = simple(full.at[own], sent, side_recv, side)
    observed_far = simple(full.at[rows_of(across)], sent, side_recv, side)
    piece_rows = pl.ds(pl.multiple_of(place * chunk, SUBLANES), chunk)
    piece = total.at[core, piece_rows]
    cross_total = total.at[core, pl.ds(stripe, SUBLANES)]
    piece_far = simple(piece, sent, piece_recv, across)
    cross_far = simple(cross_total, sent, piece_recv, across)
    sums, mixes = [
        [remote(out, into.at[core], sent, sem, m, place) for m in (across, diagonal)]
        for out, into, sem in ((sum_out, sum_in, sum_recv), (mix_out, mix_in, mix_recv))
    ]
    spread = [
        remote(piece, piece, both_sent, spread_recv, rank, p) for p in peers
    ]
    others = total.at[core, : (spaces - 1) * chunk]

    barrier = pltpu.get_barrier_semaphore()

    def greet(member, space):
        pl.semaphore_signal(
            barrier, inc=1, device_id={"member": member, "space": space}, device_id_type=MESH
        )

    @pl.when(upper)
    def _():
        greet(across, place)
        greet(side, place)
        for p in peers:
            greet(rank, p)

    @pl.when(lower)
    def _():
        greet(across, place)
        greet(diagonal, place)
        for p in peers:
            greet(across, p)

    def loading(t):
        columns = slice(t * part, (t + 1) * part)
        return pltpu.make_async_copy(x_hbm.at[:, columns], xall.at[own, columns], load.at[t])

    part = points // LOADS

    tables = [
        pltpu.make_async_copy(src, dst, small.at[i])
        for i, (src, dst) in enumerate(
            ((idx_hbm, idx_ref), (data_hbm, data_ref), (sigma_hbm, sigma_ref))
        )
    ]
    for copy in tables:
        copy.start()
    for t in range(LOADS):
        loading(t).start()
    full[own, :] = jnp.zeros((rows, slots), jnp.float32)

    @pl.when(lower)
    def _():
        pl.semaphore_wait(barrier, 1)

    loading(0).wait()

    @pl.when(lower)
    def _():
        for i in range(EARLY):
            stream(i).start()

    for copy in tables:
        copy.wait()
    gather_rows(xall, rank * rows, idx_ref, full, rows, 0, part)
    for t in range(1, LOADS):
        loading(t).wait()
        gather_rows(xall, rank * rows, idx_ref, full, rows, t * part, (t + 1) * part)

    @pl.when(upper)
    def _():
        pl.semaphore_wait(barrier, 2 * spaces + 1)
        pl.semaphore_signal(
            ready, inc=1, device_id={"member": across, "space": place}, device_id_type=MESH
        )
        observed.start()
        swap_x.start()
        sum_out[...] = jnp.sum(xall[own, :], axis=0, keepdims=True)
        for copy in sums:
            copy.start()
        for i in range(EARLY):
            arriving(i).wait_recv()
            forward(i).start()
        pending(total.at[core, : chunk + SUBLANES], piece_recv).wait_recv()
        for copy in spread:
            copy.start()

    @pl.when(lower)
    def _():
        pl.semaphore_wait(ready, 1)
        observed_side.start()
        observed.wait_recv()
        observed_far.start()
        swap_x.start()
        pending(full.at[:half], side_recv).wait_recv()
        slot = lax.broadcasted_iota(jnp.int32, (1, slots), 1)
        weight = jnp.where(slot < used_ref[0], 1.0 / flat_row(sigma_ref), 0.0)
        ev = full[...]
        mean = jnp.sum(ev, axis=0, keepdims=True) * (1.0 / samples)
        anomalies = (ev - mean) * weight
        innovation = (flat_row(data_ref) - mean) * weight
        first = lax.broadcasted_iota(jnp.int32, (SUBLANES, slots), 0) == 0
        extra = jnp.where(first, jnp.broadcast_to(innovation, (SUBLANES, slots)), 0.0)
        across_rows = ((1,), (1,))

        @pl.when(core == 0)
        def _():
            gram[...] = dot3(anomalies[:stripe], anomalies[:half], across_rows)
            cross[...] = dot3(extra, anomalies[:half], across_rows)

        @pl.when(core == 1)
        def _():
            top = samples - stripe
            gram[:top, :] = dot3(anomalies[stripe:], anomalies[:half], across_rows)
            gram[top:, :] = dot3(anomalies[half:], anomalies[half:], across_rows)
            cross[...] = dot3(extra, anomalies[half:], across_rows)

        scatter = []
        for d, p in enumerate(peers):
            source = gram.at[pl.ds(pl.multiple_of(p * chunk, SUBLANES), chunk)]
            for src, dst in (
                (source, parts.at[d, :chunk]),
                (cross, parts.at[d, pl.ds(chunk, SUBLANES)]),
            ):
                scatter.append(remote(src, dst, sent, reduce_recv, rank, p))
        for copy in scatter:
            copy.start()
        acc = gram[piece_rows, :]
        acc_cross = cross[...]
        pending(parts, reduce_recv).wait_recv()
        for d in range(spaces - 1):
            acc = acc + parts[d, :chunk, :]
            acc_cross = acc_cross + parts[d, chunk:, :]
        total[core, piece_rows, :] = acc
        total[core, stripe : stripe + SUBLANES, :] = acc_cross
        piece_far.start()
        cross_far.start()
        for copy in spread:
            copy.start()
        for i in range(EARLY, len(chunks)):
            stream(i).start()

    pending(others, spread_recv).wait_recv()
    swap_total.start()
    swap_total.wait_recv()

    rest = stripe - half
    blocks = {
        (0, 0): total[0, :half, :],
        (1, 0): jnp.concatenate([total[0, half:stripe, :], total[1, : half - rest, :]], axis=0),
        (1, 1): total[1, half - rest : stripe, :],
    }
    cross_row = jnp.concatenate(
        [total[0, stripe : stripe + 1, :], total[1, stripe : stripe + 1, :]], axis=1
    )
    transform_of(blocks, cross_row, t_ref, inv_ref, w_ref)

    def tiles(first, last, body):
        def step(t, _):
            body(pl.ds(pl.multiple_of(t * TILE, LANES), TILE))
            return 0

        lax.fori_loop(first, last, step, 0)

    @pl.when(lower)
    def _():
        swap_x.wait_recv()
        pending(sum_in, sum_recv).wait_recv()

        def product(target, first, width):
            at = rows_of(target + 2)
            columns = slice(tail_first + first, tail_first + first + width)
            x = xall[:half, columns]
            mean = jnp.sum(x, axis=0, keepdims=True)
            mean = (mean + sum_in[0, :, columns] + sum_in[1, :, columns]) * (1.0 / samples)
            scale = 1.0 - jnp.sum(t_ref[at, half:], axis=1, keepdims=True)
            y = split_dot(left_parts(t_ref[at, :half]), x - mean)
            y_out[target, :, first : first + width] = y + scale * mean

        for i in range(last_tail):
            product(core, *tails[i])
            tail_copy(i, core, across).start()

        @pl.when(core == 1)
        def _():
            for target, lane in ((1, 3), (0, 2)):
                product(target, *tails[last_tail])
                tail_copy(last_tail, target, lane).start()

        mine = left_parts(t_ref[own, :half])
        weight_sum = jnp.sum(w_ref[0:1, half:], axis=1, keepdims=True)

        def body(columns):
            x = xall[:half, columns]
            mean = jnp.sum(x, axis=0, keepdims=True)
            mean = (mean + sum_in[0, :, columns] + sum_in[1, :, columns]) * (1.0 / samples)
            out_ref[:, columns] = split_dot(mine, x - mean) + (1.0 - weight_sum) * mean

        tiles(0, points // TILE, body)
        pending(mix_in, mix_recv).wait_recv()

        def mixed(columns):
            other = mix_in[0, :, columns] + mix_in[1, :, columns]
            out_ref[:, columns] = out_ref[:, columns] + other

        tiles(0, points // TILE, mixed)
        pieces_sent = spaces * (chunk + SUBLANES) * half
        pending(
            total_bytes(rows * tail_first + 2 * rows * slots + pieces_sent), sent
        ).wait_send()
        single = sum(TAIL[:last_tail])

        @pl.when(core == 0)
        def _():
            pending(y_out.at[0, :, :single], tail_send).wait_send()

        @pl.when(core == 1)
        def _():
            pending(y_out.at[:, :, : single // 2 + TAIL[last_tail]], tail_send).wait_send()

    @pl.when(upper)
    def _():
        arriving(1).wait_recv()
        forward(1).start()
        mix = dot3(own_weights(w_ref, core), xall[own, :])
        mix_out[...] = mix[0:1, :]
        for copy in mixes:
            copy.start()
        mine = left_parts(t_ref[own, :])
        swap_x.wait_recv()

        def body(columns):
            x = xall[:, columns]
            mean = jnp.sum(x, axis=0, keepdims=True) * (1.0 / samples)
            out_ref[:, columns] = split_dot(mine, x - mean) + mean

        near = left_parts(t_ref[own, half:])

        def local(columns):
            out_ref[:, columns] = split_dot(near, xall[half:, columns])

        def done(i):
            forward(i).wait_recv()
            first, width = chunks[i]
            tiles(first // TILE, (first + width) // TILE, body)

        done(0)
        arriving(2).wait_recv()
        forward(2).start()
        done(1)
        tiles(tail_first // TILE, points // TILE, local)
        done(2)
        for i in range(len(tails)):
            first, width = tails[i]
            tail_waiting(i).wait_recv()
            columns = slice(tail_first + first, tail_first + first + width)
            out_ref[:, columns] = out_ref[:, columns] + y_in[:, first : first + width]
        pending(total_bytes(rows * tail_first + rows * slots + 4 * points), sent).wait_send()

    both_parts = rows * points + (stripe + SUBLANES) * half + (spaces - 1) * chunk * half
    pending(total_bytes(both_parts), both_sent).wait_send()


def filtered(prior, index, data, sigma, used, spaces):
    rows, points = prior.shape
    slots = index.size
    samples = 4 * rows
    half = samples // 2
    stripe = 3 * half // 2
    f32 = jnp.float32
    dma = pltpu.SemaphoreType.DMA
    vmem = pltpu.VMEM
    chunk = stripe // spaces
    pieces = (len(CHUNKS),)
    return pl.pallas_call(
        functools.partial(filter_kernel, spaces),
        out_shape=jax.ShapeDtypeStruct((rows, points), f32),
        in_specs=[pl.BlockSpec(memory_space=pltpu.HBM)] * 4
        + [pl.BlockSpec(memory_space=pltpu.SMEM)],
        out_specs=VMEM_SPEC,
        scratch_shapes=[
            vmem(index.shape, jnp.int32),
            vmem(data.shape, f32),
            vmem(sigma.shape, f32),
            vmem((samples, points), f32),
            vmem((samples, slots), f32),
            vmem((stripe, half), f32),
            vmem((SUBLANES, half), f32),
            vmem((spaces - 1, chunk + SUBLANES, half), f32),
            vmem((2, stripe + SUBLANES, half), f32),
            vmem((samples, samples), f32),
            vmem((samples, samples), f32),
            vmem((SUBLANES, samples), f32),
            vmem((1, points), f32),
            vmem((2, 1, points), f32),
            vmem((1, points), f32),
            vmem((2, 1, points), f32),
            vmem((2, rows, sum(TAIL)), f32),
            vmem((rows, sum(TAIL)), f32),
            pltpu.SemaphoreType.REGULAR,
            dma((LOADS,)),
            dma((3,)),
            dma(()),
            dma(()),
            dma(pieces),
            dma(pieces),
            dma(()),
            dma((len(TAIL),)),
            dma(()),
            dma(()),
            dma(()),
            dma(()),
            dma(()),
            dma(()),
            dma(()),
            dma(()),
            dma(()),
        ],
        compiler_params=pltpu.CompilerParams(
            collective_id=0, has_side_effects=True, vmem_limit_bytes=32 * MIB
        ),
    )(prior, index, data, sigma, used)


def body(*arrays):
    prior_sample, location = arrays[:2]
    rows, points = prior_sample.shape
    members, spaces = lax.axis_size("member"), lax.axis_size("space")
    if (
        members != 4
        or rows * members != 2 * LANES
        or 3 * LANES // 2 % (SUBLANES * spaces)
        or points != sum(CHUNKS) + sum(TAIL)
        or location.shape[1] != LANES
    ):
        return general_body(*arrays)
    held = [pltpu.with_memory_space_constraint(a, pltpu.HBM) for a in arrays[:4]]
    return filtered(*held, arrays[4], spaces)


def solution(mesh):
    placed = (
        P("member", "space"),
        P("space", None),
        P("space", None),
        P("space", None),
        P("space"),
    )
    return jax.shard_map(
        body, mesh=mesh, in_specs=placed, out_specs=P("member", "space"), check_vma=False
    )
```

```python
import functools
import math

import jax
import jax.numpy as jnp
from jax import lax
from jax.experimental import pallas as pl
from jax.experimental.pallas import tpu as pltpu
from jax.sharding import PartitionSpec as P


def solve_lower(lower_factor, target):
    return lax.linalg.triangular_solve(lower_factor, target, left_side=True, lower=True)


def general_body(
    prior_sample,
    measured_point_location,
    measured_data,
    measurement_noise_sigma,
    measured_slots_used,
):
    exact_arithmetic = lax.Precision.HIGHEST
    anomaly_matrix, points_in_region = prior_sample.shape
    region_batches = lax.axis_size("member")
    sample_total = anomaly_matrix * region_batches
    pointwise_spread = points_in_region // region_batches
    linear_position = measured_point_location.reshape(-1)
    obs_blk = linear_position.shape[0]
    observation_deviation = obs_blk // region_batches
    propagated_grid = jnp.take(prior_sample, linear_position, axis=1).reshape(
        anomaly_matrix, region_batches, observation_deviation
    )
    prior_regions = prior_sample.reshape(anomaly_matrix, region_batches, pointwise_spread)
    prior_sample_full, integrate_dynamics = (
        lax.all_to_all(prior_regions, "member", split_axis=1, concat_axis=0, tiled=True),
        lax.all_to_all(propagated_grid, "member", split_axis=1, concat_axis=0, tiled=True),
    )
    integrate_dynamics = integrate_dynamics.reshape(sample_total, observation_deviation)
    rank = lax.axis_index("member")
    start = rank * observation_deviation
    my_value = lax.dynamic_slice_in_dim(measured_data.reshape(-1), start, observation_deviation)
    my_sigma = lax.dynamic_slice_in_dim(
        measurement_noise_sigma.reshape(-1), start, observation_deviation
    )
    slots = start + jnp.arange(observation_deviation, dtype=jnp.int32)
    valid = slots < measured_slots_used[0]
    weight = jnp.where(valid, 1.0 / my_sigma, jnp.zeros_like(my_sigma))
    sim_mean = jnp.mean(integrate_dynamics, axis=0)
    perturbed = (integrate_dynamics - sim_mean[None, :]) * weight[None, :]
    innovation = (my_value - sim_mean) * weight
    gram_loc = jnp.dot(perturbed, perturbed.T, precision=exact_arithmetic)
    cross_loc = jnp.dot(perturbed, innovation, precision=exact_arithmetic)
    gram_block, cross_block = lax.psum((gram_loc, cross_loc), "member")
    gram_all, cross = lax.psum((gram_block, cross_block), "space")
    cov_matrix = gram_all + (sample_total - 1) * jnp.eye(sample_total, dtype=jnp.float32)
    lower_factor = jnp.linalg.cholesky(cov_matrix)
    inverse = solve_lower(lower_factor, jnp.eye(sample_total, dtype=jnp.float32))
    projected = jnp.dot(inverse, cross, precision=exact_arithmetic)
    mean_weight = jnp.dot(inverse.T, projected, precision=exact_arithmetic)
    weight_matrix_update = math.sqrt(sample_total - 1) * inverse + mean_weight[None, :]
    sample_vectors = prior_sample_full.reshape(sample_total, -1)
    prior_average = jnp.mean(sample_vectors, axis=0)
    updated_sample = prior_average[None, :] + jnp.dot(
        weight_matrix_update, sample_vectors - prior_average[None, :], precision=exact_arithmetic
    )
    returned = lax.all_to_all(
        updated_sample.reshape(prior_sample_full.shape),
        "member",
        split_axis=0,
        concat_axis=1,
        tiled=True,
    )
    return returned.reshape(anomaly_matrix, points_in_region)


MESH = pl.DeviceIdType.MESH
VMEM_SPEC = pl.BlockSpec(memory_space=pltpu.VMEM)
LANES = 128
MIB = 1 << 20
SUBLANES = 8


def split2(x):
    high = x.astype(jnp.bfloat16)
    low = (x - high.astype(jnp.float32)).astype(jnp.bfloat16)
    return high, low


def dot3(a, b, dims=((1,), (0,))):
    ah, al = split2(a)
    bh, bl = split2(b)
    d = functools.partial(
        lax.dot_general, dimension_numbers=(dims, ((), ())), preferred_element_type=jnp.float32
    )
    return (d(ah, bl) + d(al, bh)) + d(ah, bh)


def flat_row(ref):
    return jnp.concatenate([ref[i : i + 1, :] for i in range(ref.shape[0])], axis=1)


PIVOTS = 4


def inverse_factor(a):
    size = a.shape[0]
    count = size // SUBLANES
    shape = (SUBLANES, size)
    m = [a[SUBLANES * i : SUBLANES * (i + 1), :] for i in range(count)]
    diag = [None] * count
    lane = lax.broadcasted_iota(jnp.int32, shape, 1)
    sub = lax.broadcasted_iota(jnp.int32, shape, 0)

    def column(x, k):
        return jnp.broadcast_to(x[:, k : k + 1], shape)

    def row(x, r):
        return jnp.broadcast_to(x[r : r + 1, :], shape)

    for k in range(0, size, PIVOTS):
        t, r = divmod(k, SUBLANES)
        inside = (lane >= k) & (lane < k + PIVOTS)
        cols = [column(m[t], k + q) for q in range(PIVOTS)]
        pivot = {(q, p): row(cols[p], r + q) for p in range(PIVOTS) for q in range(p, PIVOTS)}
        base = [
            jnp.where(inside, jnp.where(lane == k + q, 1.0, 0.0), row(m[t], r + q))
            for q in range(PIVOTS)
        ]
        inverse = []
        for p in range(PIVOTS):
            inverse.append(1.0 / pivot[p, p])
            for q in range(p + 1, PIVOTS):
                factor = pivot[q, p] * inverse[p]
                base[q] = base[q] - factor * base[p]
                for s in range(q, PIVOTS):
                    pivot[s, q] = pivot[s, q] - factor * pivot[s, p]
        for p in range(PIVOTS):
            old = diag[t]
            diag[t] = pivot[p, p] if old is None else jnp.where(sub >= r + p, pivot[p, p], old)
        for i in range(t, count):
            cols_i = cols if i == t else [column(m[i], k + q) for q in range(PIVOTS)]
            cols_i = list(cols_i)
            if i == t:
                unit = jnp.where(lane - k == sub - r, 1.0, 0.0)
                x = jnp.where(inside & (sub >= r), unit, m[i])
            else:
                x = jnp.where(inside, 0.0, m[i])
            for p in range(PIVOTS):
                mult = cols_i[p] * inverse[p]
                if i == t:
                    mult = jnp.where(sub > r + p, mult, 0.0)
                for q in range(p + 1, PIVOTS):
                    cols_i[q] = cols_i[q] - mult * pivot[q, p]
                x = x - mult * base[p]
            m[i] = x
    out = []
    for i in range(count):
        keep = lane <= sub + SUBLANES * i
        out.append(jnp.where(keep, m[i] * lax.rsqrt(diag[i]), 0.0))
    return jnp.concatenate(out, axis=0)


def eye_mask(rows, cols):
    shape = (rows, cols)
    return lax.broadcasted_iota(jnp.int32, shape, 0) == lax.broadcasted_iota(jnp.int32, shape, 1)


TILE = 1024
CHUNKS = (3072, 3072, 1024)
TAIL = (768, 256)
EARLY = 1
LOADS = 2
GATHER = 1024


def offsets(widths):
    return [(sum(widths[:i]), w) for i, w in enumerate(widths)]


def gather_rows(x_ref, first, idx_ref, out_ref, rows, begin, end):
    shape = (SUBLANES, LANES)
    blocks = GATHER // LANES

    def step(t, _):
        for c in range(idx_ref.shape[0]):
            index = jnp.broadcast_to(idx_ref[c : c + 1, :], shape)
            lane = jnp.bitwise_and(index, LANES - 1)
            block = jnp.right_shift(index, LANES.bit_length() - 1) - t * blocks
            hits = [block == j for j in range(blocks)]
            columns = slice(c * LANES, (c + 1) * LANES)
            for g in range(0, rows, SUBLANES):
                place = pl.ds(pl.multiple_of(first + g, SUBLANES), SUBLANES)
                got = out_ref[place, columns]
                for j in range(blocks):
                    at = pl.ds(pl.multiple_of(t * GATHER + j * LANES, LANES), LANES)
                    x = x_ref[place, at]
                    got = jnp.where(hits[j], jnp.take_along_axis(x, lane, axis=1), got)
                out_ref[place, columns] = got
        return 0

    lax.fori_loop(begin // GATHER, end // GATHER, step, 0)


def transform_of(low_blocks, cross, t_ref, inv_ref, w_ref):
    samples = t_ref.shape[0]
    b = LANES
    ridge = float(samples - 1)
    n = samples // b
    work = {}
    for (i, j), block in low_blocks.items():
        work[i, j] = block + jnp.where(eye_mask(b, b), ridge, 0.0) if i == j else block
    inv = {}
    low = {}
    for k in range(n):
        inv[k, k] = inverse_factor(work[k, k])
        for i in range(k + 1, n):
            low[i, k] = dot3(work[i, k], inv[k, k], ((1,), (1,)))
        for i in range(k + 1, n):
            for j in range(k + 1, i + 1):
                work[i, j] = work[i, j] - dot3(low[i, k], low[j, k], ((1,), (1,)))
        for j in range(k):
            acc = dot3(low[k, j], inv[j, j])
            for m in range(j + 1, k):
                acc = acc + dot3(low[k, m], inv[m, j])
            inv[k, j] = -dot3(inv[k, k], acc)
    zero = jnp.zeros((b, b), jnp.float32)
    full = jnp.concatenate(
        [
            jnp.concatenate([inv[i, j] if j <= i else zero for j in range(n)], axis=1)
            for i in range(n)
        ],
        axis=0,
    )
    inv_ref[...] = full
    projected = jnp.sum(full * cross, axis=1, keepdims=True)
    mean_weight = jnp.sum(full * projected, axis=0, keepdims=True)
    w_ref[...] = jnp.broadcast_to(mean_weight, w_ref.shape)
    t_ref[...] = math.sqrt(samples - 1) * full + mean_weight


def own_weights(w_ref, core):
    half = w_ref.shape[1] // 2
    rows = half // 2
    w = w_ref[:, half:]
    return jnp.where(core == 0, w[:, :rows], w[:, rows:])


def split_dot(parts, x):
    th, stacked = parts
    rows = th.shape[0]
    xh, xl = split2(x)
    dot = functools.partial(jnp.dot, preferred_element_type=jnp.float32)
    both = dot(stacked, xh)
    return (both[rows:] + dot(th, xl)) + both[:rows]


def left_parts(t):
    th, tl = split2(t)
    return th, jnp.concatenate([th, tl], axis=0)


def filter_kernel(
    spaces,
    x_hbm,
    idx_hbm,
    data_hbm,
    sigma_hbm,
    used_ref,
    out_ref,
    idx_ref,
    data_ref,
    sigma_ref,
    xall,
    full,
    gram,
    cross,
    parts,
    total,
    t_ref,
    inv_ref,
    w_ref,
    sum_out,
    sum_in,
    mix_out,
    mix_in,
    y_out,
    y_in,
    ready,
    load,
    small,
    sent,
    both_sent,
    stream_recv,
    forward_recv,
    tail_send,
    tail_recv,
    reduce_recv,
    spread_recv,
    sum_recv,
    mix_recv,
    swap_recv,
    total_recv,
    observed_recv,
    side_recv,
    piece_recv,
):
    rank = lax.axis_index("member")
    place = lax.axis_index("space")
    core = lax.rem(rank, 2)
    lower = rank < 2
    upper = rank >= 2
    side = rank + 1 - 2 * core
    across = lax.rem(rank + 2, 4)
    diagonal = lax.rem(side + 2, 4)
    rows, points = x_hbm.shape
    samples, slots = full.shape
    half = samples // 2
    stripe = gram.shape[0]
    chunk = stripe // spaces
    peers = [lax.rem(place + d, spaces) for d in range(1, spaces)]
    chunks = offsets(CHUNKS)
    tails = offsets(TAIL)
    tail_first = sum(CHUNKS)
    last_tail = len(TAIL) - 1

    def rows_of(member):
        return pl.ds(pl.multiple_of(member * rows, SUBLANES), rows)

    def remote(src, dst, sent, received, member, space):
        return pltpu.make_async_remote_copy(
            src_ref=src,
            dst_ref=dst,
            send_sem=sent,
            recv_sem=received,
            device_id={"member": member, "space": space},
            device_id_type=MESH,
        )

    def pending(ref, sem):
        return remote(ref, ref, sem, sem, side, place)

    def total_bytes(values):
        count = values // (SUBLANES * LANES)
        bands = next(n for n in range(samples // SUBLANES, 0, -1) if count % n == 0)
        return xall.at[: bands * SUBLANES, : count // bands * LANES]

    own = rows_of(rank)

    def stream(i):
        first, width = chunks[i]
        here = xall.at[own, first : first + width]
        return remote(here, here, sent, stream_recv.at[i], across, place)

    def arrived(i):
        first, width = chunks[i]
        return xall.at[rows_of(across), first : first + width]

    def arriving(i):
        return pending(arrived(i), stream_recv.at[i])

    def forward(i):
        here = arrived(i)
        return remote(here, here, sent, forward_recv.at[i], side, place)

    def tail_copy(i, target, lane):
        first, width = tails[i]
        columns = slice(first, first + width)
        return remote(
            y_out.at[target, :, columns],
            y_in.at[:, columns],
            tail_send,
            tail_recv.at[i],
            lane,
            place,
        )

    def tail_waiting(i):
        first, width = tails[i]
        return pending(y_in.at[:, first : first + width], tail_recv.at[i])

    def simple(ref, sent, received, member):
        return remote(ref, ref, sent, received, member, place)

    swap_x = simple(xall.at[own], both_sent, swap_recv, side)
    swap_total = simple(total.at[core], both_sent, total_recv, side)
    observed = simple(full.at[own], sent, observed_recv, across)
    observed_side = simple(full.at[own], sent, side_recv, side)
    observed_far = simple(full.at[rows_of(across)], sent, side_recv, side)
    piece_rows = pl.ds(pl.multiple_of(place * chunk, SUBLANES), chunk)
    piece = total.at[core, piece_rows]
    cross_total = total.at[core, pl.ds(stripe, SUBLANES)]
    piece_far = simple(piece, sent, piece_recv, across)
    cross_far = simple(cross_total, sent, piece_recv, across)
    sums, mixes = [
        [remote(out, into.at[core], sent, sem, m, place) for m in (across, diagonal)]
        for out, into, sem in ((sum_out, sum_in, sum_recv), (mix_out, mix_in, mix_recv))
    ]
    spread = [
        remote(piece, piece, both_sent, spread_recv, rank, p) for p in peers
    ]
    others = total.at[core, : (spaces - 1) * chunk]

    barrier = pltpu.get_barrier_semaphore()

    def greet(member, space):
        pl.semaphore_signal(
            barrier, inc=1, device_id={"member": member, "space": space}, device_id_type=MESH
        )

    @pl.when(upper)
    def _():
        greet(across, place)
        greet(side, place)
        for p in peers:
            greet(rank, p)

    @pl.when(lower)
    def _():
        greet(across, place)
        greet(diagonal, place)
        for p in peers:
            greet(across, p)

    def loading(t):
        columns = slice(t * part, (t + 1) * part)
        return pltpu.make_async_copy(x_hbm.at[:, columns], xall.at[own, columns], load.at[t])

    part = points // LOADS

    tables = [
        pltpu.make_async_copy(src, dst, small)
        for src, dst in ((idx_hbm, idx_ref), (data_hbm, data_ref), (sigma_hbm, sigma_ref))
    ]
    for copy in tables:
        copy.start()
    for t in range(LOADS):
        loading(t).start()
    full[own, :] = jnp.zeros((rows, slots), jnp.float32)

    @pl.when(lower)
    def _():
        pl.semaphore_wait(barrier, 1)

    loading(0).wait()

    @pl.when(lower)
    def _():
        for i in range(EARLY):
            stream(i).start()

    loaded = sum_in.at[0, :, : 3 * slots]
    pltpu.make_async_copy(loaded, loaded, small).wait()
    gather_rows(xall, rank * rows, idx_ref, full, rows, 0, part)
    for t in range(1, LOADS):
        loading(t).wait()
        gather_rows(xall, rank * rows, idx_ref, full, rows, t * part, (t + 1) * part)

    @pl.when(upper)
    def _():
        pl.semaphore_wait(barrier, 2 * spaces + 1)
        pl.semaphore_signal(
            ready, inc=1, device_id={"member": across, "space": place}, device_id_type=MESH
        )
        observed.start()
        swap_x.start()
        sum_out[...] = jnp.sum(xall[own, :], axis=0, keepdims=True)
        for copy in sums:
            copy.start()
        for i in range(EARLY):
            arriving(i).wait_recv()
            forward(i).start()
        pending(total.at[core, : chunk + SUBLANES], piece_recv).wait_recv()
        for copy in spread:
            copy.start()

    @pl.when(lower)
    def _():
        pl.semaphore_wait(ready, 1)
        observed_side.start()
        observed.wait_recv()
        observed_far.start()
        swap_x.start()
        pending(full.at[:half], side_recv).wait_recv()
        slot = lax.broadcasted_iota(jnp.int32, (1, slots), 1)
        weight = jnp.where(slot < used_ref[0], 1.0 / flat_row(sigma_ref), 0.0)
        ev = full[...]
        mean = jnp.sum(ev, axis=0, keepdims=True) * (1.0 / samples)
        anomalies = (ev - mean) * weight
        innovation = (flat_row(data_ref) - mean) * weight
        first = lax.broadcasted_iota(jnp.int32, (SUBLANES, slots), 0) == 0
        extra = jnp.where(first, jnp.broadcast_to(innovation, (SUBLANES, slots)), 0.0)
        across_rows = ((1,), (1,))

        @pl.when(core == 0)
        def _():
            gram[...] = dot3(anomalies[:stripe], anomalies[:half], across_rows)
            cross[...] = dot3(extra, anomalies[:half], across_rows)

        @pl.when(core == 1)
        def _():
            top = samples - stripe
            gram[:top, :] = dot3(anomalies[stripe:], anomalies[:half], across_rows)
            gram[top:, :] = dot3(anomalies[half:], anomalies[half:], across_rows)
            cross[...] = dot3(extra, anomalies[half:], across_rows)

        scatter = []
        for d, p in enumerate(peers):
            source = gram.at[pl.ds(pl.multiple_of(p * chunk, SUBLANES), chunk)]
            for src, dst in (
                (source, parts.at[d, :chunk]),
                (cross, parts.at[d, pl.ds(chunk, SUBLANES)]),
            ):
                scatter.append(remote(src, dst, sent, reduce_recv, rank, p))
        for copy in scatter:
            copy.start()
        acc = gram[piece_rows, :]
        acc_cross = cross[...]
        pending(parts, reduce_recv).wait_recv()
        for d in range(spaces - 1):
            acc = acc + parts[d, :chunk, :]
            acc_cross = acc_cross + parts[d, chunk:, :]
        total[core, piece_rows, :] = acc
        total[core, stripe : stripe + SUBLANES, :] = acc_cross
        piece_far.start()
        cross_far.start()
        for copy in spread:
            copy.start()
        for i in range(EARLY, len(chunks)):
            stream(i).start()

    pending(others, spread_recv).wait_recv()
    swap_total.start()
    swap_total.wait_recv()

    rest = stripe - half
    blocks = {
        (0, 0): total[0, :half, :],
        (1, 0): jnp.concatenate([total[0, half:stripe, :], total[1, : half - rest, :]], axis=0),
        (1, 1): total[1, half - rest : stripe, :],
    }
    cross_row = jnp.concatenate(
        [total[0, stripe : stripe + 1, :], total[1, stripe : stripe + 1, :]], axis=1
    )
    transform_of(blocks, cross_row, t_ref, inv_ref, w_ref)

    def tiles(first, last, body):
        def step(t, _):
            body(pl.ds(pl.multiple_of(t * TILE, LANES), TILE))
            return 0

        lax.fori_loop(first, last, step, 0)

    @pl.when(lower)
    def _():
        swap_x.wait_recv()
        pending(sum_in, sum_recv).wait_recv()

        def product(target, first, width):
            at = rows_of(target + 2)
            columns = slice(tail_first + first, tail_first + first + width)
            x = xall[:half, columns]
            mean = jnp.sum(x, axis=0, keepdims=True)
            mean = (mean + sum_in[0, :, columns] + sum_in[1, :, columns]) * (1.0 / samples)
            scale = 1.0 - jnp.sum(t_ref[at, half:], axis=1, keepdims=True)
            y = split_dot(left_parts(t_ref[at, :half]), x - mean)
            y_out[target, :, first : first + width] = y + scale * mean

        for i in range(last_tail):
            product(core, *tails[i])
            tail_copy(i, core, across).start()

        @pl.when(core == 1)
        def _():
            for target, lane in ((1, 3), (0, 2)):
                product(target, *tails[last_tail])
                tail_copy(last_tail, target, lane).start()

        mine = left_parts(t_ref[own, :half])
        weight_sum = jnp.sum(w_ref[0:1, half:], axis=1, keepdims=True)

        def body(columns):
            x = xall[:half, columns]
            mean = jnp.sum(x, axis=0, keepdims=True)
            mean = (mean + sum_in[0, :, columns] + sum_in[1, :, columns]) * (1.0 / samples)
            out_ref[:, columns] = split_dot(mine, x - mean) + (1.0 - weight_sum) * mean

        tiles(0, points // TILE, body)
        pending(mix_in, mix_recv).wait_recv()

        def mixed(columns):
            other = mix_in[0, :, columns] + mix_in[1, :, columns]
            out_ref[:, columns] = out_ref[:, columns] + other

        tiles(0, points // TILE, mixed)
        pieces_sent = spaces * (chunk + SUBLANES) * half
        pending(
            total_bytes(rows * tail_first + 2 * rows * slots + pieces_sent), sent
        ).wait_send()
        single = sum(TAIL[:last_tail])

        @pl.when(core == 0)
        def _():
            pending(y_out.at[0, :, :single], tail_send).wait_send()

        @pl.when(core == 1)
        def _():
            pending(y_out.at[:, :, : single // 2 + TAIL[last_tail]], tail_send).wait_send()

    @pl.when(upper)
    def _():
        arriving(1).wait_recv()
        forward(1).start()
        mix = dot3(own_weights(w_ref, core), xall[own, :])
        mix_out[...] = mix[0:1, :]
        for copy in mixes:
            copy.start()
        mine = left_parts(t_ref[own, :])
        swap_x.wait_recv()

        def body(columns):
            x = xall[:, columns]
            mean = jnp.sum(x, axis=0, keepdims=True) * (1.0 / samples)
            out_ref[:, columns] = split_dot(mine, x - mean) + mean

        near = left_parts(t_ref[own, half:])

        def local(columns):
            out_ref[:, columns] = split_dot(near, xall[half:, columns])

        def done(i):
            forward(i).wait_recv()
            first, width = chunks[i]
            tiles(first // TILE, (first + width) // TILE, body)

        done(0)
        arriving(2).wait_recv()
        forward(2).start()
        done(1)
        tiles(tail_first // TILE, points // TILE, local)
        done(2)
        for i in range(len(tails)):
            first, width = tails[i]
            tail_waiting(i).wait_recv()
            columns = slice(tail_first + first, tail_first + first + width)
            out_ref[:, columns] = out_ref[:, columns] + y_in[:, first : first + width]
        pending(total_bytes(rows * tail_first + rows * slots + 4 * points), sent).wait_send()

    both_parts = rows * points + (stripe + SUBLANES) * half + (spaces - 1) * chunk * half
    pending(total_bytes(both_parts), both_sent).wait_send()


def filtered(prior, index, data, sigma, used, spaces):
    rows, points = prior.shape
    slots = index.size
    samples = 4 * rows
    half = samples // 2
    stripe = 3 * half // 2
    f32 = jnp.float32
    dma = pltpu.SemaphoreType.DMA
    vmem = pltpu.VMEM
    chunk = stripe // spaces
    pieces = (len(CHUNKS),)
    return pl.pallas_call(
        functools.partial(filter_kernel, spaces),
        out_shape=jax.ShapeDtypeStruct((rows, points), f32),
        in_specs=[pl.BlockSpec(memory_space=pltpu.HBM)] * 4
        + [pl.BlockSpec(memory_space=pltpu.SMEM)],
        out_specs=VMEM_SPEC,
        scratch_shapes=[
            vmem(index.shape, jnp.int32),
            vmem(data.shape, f32),
            vmem(sigma.shape, f32),
            vmem((samples, points), f32),
            vmem((samples, slots), f32),
            vmem((stripe, half), f32),
            vmem((SUBLANES, half), f32),
            vmem((spaces - 1, chunk + SUBLANES, half), f32),
            vmem((2, stripe + SUBLANES, half), f32),
            vmem((samples, samples), f32),
            vmem((samples, samples), f32),
            vmem((SUBLANES, samples), f32),
            vmem((1, points), f32),
            vmem((2, 1, points), f32),
            vmem((1, points), f32),
            vmem((2, 1, points), f32),
            vmem((2, rows, sum(TAIL)), f32),
            vmem((rows, sum(TAIL)), f32),
            pltpu.SemaphoreType.REGULAR,
            dma((LOADS,)),
            dma(()),
            dma(()),
            dma(()),
            dma(pieces),
            dma(pieces),
            dma(()),
            dma((len(TAIL),)),
            dma(()),
            dma(()),
            dma(()),
            dma(()),
            dma(()),
            dma(()),
            dma(()),
            dma(()),
            dma(()),
        ],
        compiler_params=pltpu.CompilerParams(
            collective_id=0, has_side_effects=True, vmem_limit_bytes=32 * MIB
        ),
    )(prior, index, data, sigma, used)


def body(*arrays):
    prior_sample, location = arrays[:2]
    rows, points = prior_sample.shape
    members, spaces = lax.axis_size("member"), lax.axis_size("space")
    if (
        members != 4
        or rows * members != 2 * LANES
        or 3 * LANES // 2 % (SUBLANES * spaces)
        or points != sum(CHUNKS) + sum(TAIL)
        or location.shape[1] != LANES
    ):
        return general_body(*arrays)
    held = [pltpu.with_memory_space_constraint(a, pltpu.HBM) for a in arrays[:4]]
    return filtered(*held, arrays[4], spaces)


def solution(mesh):
    placed = (
        P("member", "space"),
        P("space", None),
        P("space", None),
        P("space", None),
        P("space"),
    )
    return jax.shard_map(
        body, mesh=mesh, in_specs=placed, out_specs=P("member", "space"), check_vma=False
    )
```
